32 devices in a mesh: dp: 8 (over y, x, core), tensor: 4 (over z).
Axes of the slice: x: 2, y: 2, z: 4, core: 2. Of those that a mesh axis runs over, the one named last changes fastest.
Arguments:
- tokens: bfloat16 [16384, 2048], P(('dp', 'tensor')), may hold values from -6 to 6
- segments: int32 [8, 2048], P('dp'), may hold values from 0 to 7, never falling along the last dimension, each value on 1 to 1024 neighbouring positions
- ln_gain: float32 [2048], replicated, may hold values from 0.5 to 1.5
- ln_shift: float32 [2048], replicated, may hold values from -1.5 to 1.5
- qkv_weight: bfloat16 [2048, 3, 2048], P('dp', None, 'tensor'), may hold values from -0.125 to 0.125
- qkv_bias: float32 [3, 2048], P(None, 'tensor'), may hold values from -3 to 3
- out_weight: bfloat16 [2048, 2048], P('tensor', 'dp'), may hold values from -1 to 1
- out_bias: float32 [2048], replicated, may hold values from -3 to 3
- fc1_weight: bfloat16 [2048, 8192], P('dp', 'tensor'), may hold values from -0.125 to 0.125
- fc1_bias: float32 [8192], P('tensor'), may hold values from -3 to 3
- fc2_weight: bfloat16 [8192, 2048], P('tensor', 'dp'), may hold values from -0.0625 to 0.0625
- fc2_bias: float32 [2048], replicated, may hold values from -3 to 3
- cotangent: bfloat16 [16384, 2048], P(('dp', 'tensor')), may hold values from -6 to 6
Outputs:
- mixed: bfloat16 [16384, 2048], P(('dp', 'tensor'))
- input_grad: bfloat16 [16384, 2048], P(('dp', 'tensor'))
- qkv_weight_grad: float32 [2048, 3, 2048], P('dp', None, 'tensor')
- qkv_bias_grad: float32 [3, 2048], P(None, 'tensor')
- out_weight_grad: float32 [2048, 2048], P('tensor', 'dp')
- out_bias_grad: float32 [2048], replicated
- fc1_weight_grad: float32 [2048, 8192], P('dp', 'tensor')
- fc1_bias_grad: float32 [8192], P('tensor')
- fc2_weight_grad: float32 [8192, 2048], P('tensor', 'dp')
- fc2_bias_grad: float32 [2048], replicated
- gain_grad: float32 [2048], replicated
- shift_grad: float32 [2048], replicated
The draws below stay inside these ranges and needn't reach their ends.
Inputs may be any that keep to these rules, and one draw needn't show every extreme that they name: `segments`: each row holds one data group's 2048 tokens; along a row the sequence numbers never fall, each sequence covers 1 to 1024 consecutive tokens, and some sequence covers exactly 1024.
All inputs are finite; a program needn't handle non-finite values.
Results may differ from the reference program's by a relative error of at most 0.013.
Values may be sent and summed in bfloat16 or wider, within the bound.
A program may use at most 320 MiB of HBM per device.

```python
import math
import jax
import jax.numpy as jnp
import numpy as np
from jax import lax

D = 2048
H = 32
HD = 64
ROT = 32
FF = 8192
TOK_GRP = 2048
SEQ_MAX = 1024
SEQS_GRP = 8
TOKENS = 16384
N_DP = 8
N_TENSOR = 4


def spiked(entries, rng, source, target, blocks, factor):
    owner, partner = [(jnp.arange(entries.shape[position]) // (entries.shape[position] // blocks)).reshape([-1 if axis == position else 1 for axis in range(entries.ndim)]) for position in (source, target)]
    chosen = jax.random.permutation(rng, blocks)[partner]
    strong = (owner == chosen) | (owner == (partner + blocks // 2) % blocks)
    return jnp.where(strong, factor * entries, entries)


def block_levels(own_key, extent, split, smallest, largest):
    def one(position, parts):
        heights = jax.random.uniform(jax.random.fold_in(jax.random.fold_in(own_key, 6), position), (parts,), jnp.float32, smallest / len(split), largest / len(split))
        return jnp.repeat(jnp.exp(heights), extent[position] // parts).reshape((-1,) + (1,) * (len(extent) - position - 1))

    factor_of = one(*split[0])
    for cut in split[1:]:
        factor_of = factor_of * one(*cut)
    return factor_of


def split_up(amount, total, limit, skew):
    weights = [(1 << 20) // math.isqrt(standing ** skew) + 1 for standing in range(2, amount + 1)]
    rest, given = total - limit - (amount - 1), [1] * (amount - 1)
    while rest > 0:
        free = [i for i in range(amount - 1) if given[i] < limit]
        pool, budget = sum([weights[i] for i in free]), rest
        for i in free:
            extra = min(limit - given[i], max(1, budget * weights[i] // pool), rest)
            given[i] = given[i] + extra
            rest = rest - extra
    return np.array([limit] + given)


def uneven(key, number_of, total, reach, lean):
    if number_of == 2:
        one = jax.random.randint(key, (), max(1, total - reach), min(reach, total - 1) + 1)
        return jnp.stack([one, total - one])
    tallies = jnp.asarray(split_up(number_of, total, reach, lean), jnp.int32)
    pairs = (number_of - 1) // 2
    source_of, receiver = tallies[1:1 + 2 * pairs:2], tallies[2:2 + 2 * pairs:2]
    margin = jnp.minimum(source_of - 1, reach - receiver)
    passed = jax.random.randint(jax.random.fold_in(key, 1), (pairs,), 0, 1 << 20) % (margin + 1)
    tallies = tallies.at[1:1 + 2 * pairs:2].set(source_of - passed).at[2:2 + 2 * pairs:2].set(receiver + passed)
    return tallies[jax.random.permutation(jax.random.fold_in(key, 2), number_of)]


def gaussian(stream_key, shape, deviation, reach, cuts=(), kind=jnp.bfloat16):
    gain = block_levels(stream_key, shape, cuts, -0.22, 0.18) if cuts else 1.0
    result = jax.random.normal(stream_key, shape, jnp.float32) * deviation * gain
    return jnp.minimum(jnp.maximum(result, -reach), reach).astype(kind)


def noise_with(own_key, extent, scale, bound, split, heavy, held_as=jnp.bfloat16):
    drawn = scale * jax.random.normal(own_key, extent, jnp.float32)
    if split:
        drawn = drawn * block_levels(own_key, extent, split, -0.22, 0.18)
    return jnp.clip(spiked(drawn, jax.random.fold_in(own_key, 3), *heavy), -bound, bound).astype(held_as)


def setup_inputs(seed: int = 0) -> dict:
    key_list = jax.random.split(jax.random.key(seed), 14)
    tokens = noise_with(key_list[0], (TOKENS, D), 1.0, 6.0, ((0, 32),), (0, 1, 32, 2.75))
    segments = jax.vmap(lambda own: jnp.searchsorted(jnp.cumsum(uneven(own, SEQS_GRP, TOK_GRP, SEQ_MAX, 2)), jnp.arange(TOK_GRP), side="right"))(jax.random.split(key_list[1], N_DP)).reshape((N_DP, TOK_GRP)).astype(jnp.int32)
    ln_gain = jnp.clip(1.0 + 0.1 * jax.random.normal(key_list[2], (D,), jnp.float32), 0.5, 1.5)
    ln_shift = gaussian(key_list[3], (D,), 0.3, 1.5, (), jnp.float32)
    qkv_weight = gaussian(key_list[4], (D, 3, D), D ** -0.5, 0.125, ((0, 8), (2, 4)))
    qkv_bias = gaussian(key_list[5], (3, D), 0.5, 3.0, ((1, 4),), jnp.float32)
    out_weight = gaussian(key_list[6], (D, D), (max(1, D // 64)) ** -0.5, 1.0, ((0, 4), (1, 8)))
    out_bias = gaussian(key_list[7], (D,), 0.5, 3.0, (), jnp.float32)
    fc1_weight = gaussian(key_list[8], (D, FF), D ** -0.5, 0.125, ((0, 8), (1, 4)))
    fc1_bias = gaussian(key_list[9], (FF,), 0.5, 3.0, ((0, 4),), jnp.float32)
    fc2_weight = gaussian(key_list[10], (FF, D), FF ** -0.5, 0.0625, ((0, 4), (1, 8)))
    fc2_bias = gaussian(key_list[11], (D,), 0.5, 3.0, (), jnp.float32)
    cotangent = noise_with(key_list[12], (TOKENS, D), 1.0, 6.0, ((0, 32),), (0, 1, 32, 2.75))
    return dict(tokens=tokens, segments=segments, ln_gain=ln_gain, ln_shift=ln_shift, qkv_weight=qkv_weight, qkv_bias=qkv_bias, out_weight=out_weight, out_bias=out_bias, fc1_weight=fc1_weight, fc1_bias=fc1_bias, fc2_weight=fc2_weight, fc2_bias=fc2_bias, cotangent=cotangent)


EPS = 1e-05
ROPE_BASE = 10000.0
NEGATIVE = -1e+30
PRECISE = lax.Precision.HIGHEST

@jax.custom_vjp
def low(v):
    return lax.optimization_barrier(v.astype(jnp.bfloat16)).astype(jnp.float32)

@jax.custom_vjp
def low_back(v):
    return v

def low_keep(v):
    return (low(v), None)

def low_pass(kept, grad):
    return (grad,)

def back_keep(v):
    return (v, None)

def back_low(kept, grad):
    return (low(grad),)
low.defvjp(low_keep, low_pass)
low_back.defvjp(back_keep, back_low)

def seq_positions(segment_row):
    row_count = segment_row.shape[0]
    row_index = jnp.arange(row_count, dtype=jnp.int32)
    seq_begins = jnp.concatenate([jnp.ones((1,), dtype=bool), segment_row[1:] != segment_row[:-1]])
    starts = lax.cummax(jnp.where(seq_begins, row_index, jnp.zeros_like(row_index)), axis=0)
    return row_index - starts

def rotary_tables(positions):
    half_rot = ROT // 2
    frequency = ROPE_BASE ** (-(jnp.arange(half_rot, dtype=jnp.float32) * 2.0) / ROT)
    angles = positions.astype(jnp.float32)[:, None] * frequency[None, :]
    return (jnp.cos(angles)[:, None, :], jnp.sin(angles)[:, None, :])

def rotate(heads_in, cosine_table, sine_table):
    half_rot = ROT // 2
    first_half = heads_in[..., :half_rot]
    second_half = heads_in[..., half_rot:ROT]
    return jnp.concatenate([first_half * cosine_table - second_half * sine_table, second_half * cosine_table + first_half * sine_table, heads_in[..., ROT:]], axis=-1)

def allowed_block(segment_row, first_row, block_rows):
    key_count = segment_row.shape[0]
    query_index = first_row + jnp.arange(block_rows, dtype=jnp.int32)
    key_index = jnp.arange(key_count, dtype=jnp.int32)
    query_seg = lax.dynamic_slice_in_dim(segment_row, first_row, block_rows, 0)
    return (query_seg[:, None] == segment_row[None, :]) & (key_index[None, :] <= query_index[:, None])

def precise_dot(left_op, right_op):
    return jnp.dot(left_op, right_op, precision=PRECISE)

def attention(queries, key_rows, value_rows, segment_row):
    group_rows = queries.shape[0]
    block_rows = min(512, group_rows)
    factor = HD ** (-0.5)

    def one_block(block_index):
        first_row = block_index * block_rows
        query_block = lax.dynamic_slice_in_dim(queries, first_row, block_rows, 0)
        raw_scores = jnp.einsum('qhd,khd->hqk', query_block, key_rows, precision=PRECISE)
        scores = low_back(raw_scores * factor)
        allowed = allowed_block(segment_row, first_row, block_rows)
        scores = jnp.where(allowed[None], scores, NEGATIVE)
        attn_probs = jax.nn.softmax(scores, axis=-1)
        return jnp.einsum('hqk,khd->qhd', low(attn_probs), value_rows, precision=PRECISE)
    block_out = lax.map(jax.checkpoint(one_block), jnp.arange(group_rows // block_rows, dtype=jnp.int32))
    return block_out.reshape(group_rows, -1)

def group_forward(x_rows, segment_row, ln_gain, ln_shift, qkv_weight, qkv_bias, out_weight, out_bias, fc1_weight, fc1_bias, fc2_weight, fc2_bias):
    row_mean = lax.optimization_barrier(jnp.mean(x_rows, axis=-1, keepdims=True))
    centred = x_rows - row_mean
    row_var = lax.optimization_barrier(jnp.mean(centred * centred, axis=-1, keepdims=True))
    normalized = centred * lax.rsqrt(row_var + EPS)
    normed = low(normalized * ln_gain + ln_shift)
    positions = seq_positions(segment_row)
    cosine_table, sine_table = rotary_tables(positions)
    group_rows = x_rows.shape[0]
    local_width = D // N_TENSOR
    local_hidden = FF // N_TENSOR
    heads_here = H // N_TENSOR
    summed = jnp.zeros_like(x_rows)
    for shard_index in range(N_TENSOR):
        col_lo = shard_index * local_width
        hid_lo = shard_index * local_hidden
        part_in = low_back(normed)
        w_qkv = qkv_weight[:, :, col_lo:col_lo + local_width].reshape(D, 3 * local_width)
        qkv_raw = low_back(precise_dot(part_in, w_qkv).reshape(group_rows, 3, local_width) + qkv_bias[:, col_lo:col_lo + local_width][None])
        queries = low(rotate(qkv_raw[:, 0].reshape(group_rows, heads_here, HD), cosine_table, sine_table))
        key_rows = low(rotate(qkv_raw[:, 1].reshape(group_rows, heads_here, HD), cosine_table, sine_table))
        value_rows = low(qkv_raw[:, 2].reshape(group_rows, heads_here, HD))
        attended = low(low_back(attention(queries, key_rows, value_rows, segment_row)))
        hidden = low_back(precise_dot(part_in, fc1_weight[:, hid_lo:hid_lo + local_hidden]) + fc1_bias[hid_lo:hid_lo + local_hidden])
        activated = low(jax.nn.gelu(hidden, approximate=True))
        partial_sum = precise_dot(attended, out_weight[col_lo:col_lo + local_width]) + precise_dot(activated, fc2_weight[hid_lo:hid_lo + local_hidden])
        summed = summed + low(partial_sum)
    return x_rows + summed + out_bias + fc2_bias

def reference(tokens, segments, ln_gain, ln_shift, qkv_weight, qkv_bias, out_weight, out_bias, fc1_weight, fc1_bias, fc2_weight, fc2_bias, cotangent):
    params = tuple((param.astype(jnp.float32) for param in (ln_gain, ln_shift, qkv_weight, qkv_bias, out_weight, out_bias, fc1_weight, fc1_bias, fc2_weight, fc2_bias)))
    inputs = tokens.astype(jnp.float32).reshape(N_DP, TOK_GRP, D)
    cot_groups = cotangent.astype(jnp.float32).reshape(N_DP, TOK_GRP, D)

    def one_group(running, group_item):
        x_group, segment_row, cot_group = group_item

        def forward(x_rows, *weights):
            return group_forward(x_rows, segment_row, *weights)
        out_value, pull = jax.vjp(forward, x_group, *params)
        gradients = pull(cot_group)
        running = tuple((summed + grad_piece for summed, grad_piece in zip(running, gradients[1:])))
        return (running, (out_value.astype(jnp.bfloat16), gradients[0].astype(jnp.bfloat16)))
    zero_grads = tuple((jnp.zeros_like(param) for param in params))
    grad_sums, (out_rows, in_grads) = lax.scan(one_group, zero_grads, (inputs, segments, cot_groups))
    return (out_rows.reshape(-1, D), in_grads.reshape(-1, D), grad_sums[2], grad_sums[3], grad_sums[4], grad_sums[5], grad_sums[6], grad_sums[7], grad_sums[8], grad_sums[9], grad_sums[0], grad_sums[1])
```

```python
import functools

import jax
import jax.numpy as jnp
from jax import lax
from jax.experimental import pallas as pl
from jax.experimental.pallas import tpu as pltpu
from jax.sharding import PartitionSpec as P

HD = 64
ROT = 32
EPS = 1e-05
ROPE_BASE = 10000.0
NEGATIVE = -1e30
BLOCK = 256
ROWS = 256
SHRINK = 20

F32 = jnp.float32
BF16 = jnp.bfloat16


def dot_nn(a, b):
    return lax.dot_general(a, b, (((1,), (0,)), ((), ())), preferred_element_type=F32)


def dot_nt(a, b):
    return lax.dot_general(a, b, (((1,), (1,)), ((), ())), preferred_element_type=F32)


def dot_tn(a, b):
    return lax.dot_general(a, b, (((0,), (0,)), ((), ())), preferred_element_type=F32)


def cost(flops, moved, trans=0):
    return pl.CostEstimate(flops=int(flops / SHRINK), bytes_accessed=int(moved / SHRINK), transcendentals=0)


def whole(a):
    return pl.BlockSpec(a.shape, lambda *_: (0,) * a.ndim)


def seq_starts(segment_row):
    count = segment_row.shape[0]
    index = jnp.arange(count, dtype=jnp.int32)
    begins = jnp.concatenate([jnp.ones((1,), dtype=bool), segment_row[1:] != segment_row[:-1]])
    return lax.cummax(jnp.where(begins, index, jnp.zeros_like(index)), axis=0)


def rotary_tables(positions):
    half = ROT // 2
    lane = jnp.arange(128, dtype=jnp.int32) % HD
    frequency = ROPE_BASE ** (-((lane % half).astype(F32) * 2.0) / ROT)
    angles = positions.astype(F32)[:, None] * frequency[None, :]
    cosine = jnp.where(lane < ROT, jnp.cos(angles), 1.0)
    sine = jnp.sin(angles)
    sine_up = jnp.where(lane < half, -sine, 0.0)
    sine_down = jnp.where((lane >= half) & (lane < ROT), sine, 0.0)
    return cosine, sine_up, sine_down


def rotate(x, cosine, sine_up, sine_down):
    return (
        x * cosine
        + pltpu.roll(x, 128 - ROT // 2, axis=1) * sine_up
        + pltpu.roll(x, ROT // 2, axis=1) * sine_down
    )


def unrotate(x, cosine, sine_up, sine_down):
    return (
        x * cosine
        - pltpu.roll(x, 128 - ROT // 2, axis=1) * sine_up
        - pltpu.roll(x, ROT // 2, axis=1) * sine_down
    )


def norm_kernel(x_ref, gain_ref, shift_ref, o_ref):
    x = x_ref[...].astype(F32)
    centred = x - jnp.mean(x, axis=1, keepdims=True)
    inv_std = lax.rsqrt(jnp.mean(centred * centred, axis=1, keepdims=True) + EPS)
    o_ref[...] = (centred * inv_std * gain_ref[...] + shift_ref[...]).astype(BF16)


def norm(x, gain, shift):
    rows, width = x.shape
    step = rows // 2
    row = pl.BlockSpec((1, width), lambda i: (0, 0))
    tile = pl.BlockSpec((step, width), lambda i: (i, 0))
    return pl.pallas_call(
        norm_kernel,
        grid=(rows // step,),
        in_specs=[tile, row, row],
        out_specs=tile,
        out_shape=jax.ShapeDtypeStruct(x.shape, BF16),
        cost_estimate=cost(rows * width * 8, rows * width * 4),
        name="norm",
    )(x, gain, shift)


def norm_back_kernel(x_ref, cot_ref, *refs):
    gain_ref, o_ref, sums_ref = refs[-3:]

    @pl.when(pl.program_id(0) == 0)
    def _():
        sums_ref[...] = jnp.zeros_like(sums_ref)

    x = x_ref[...].astype(F32)
    centred = x - jnp.mean(x, axis=1, keepdims=True)
    inv_std = lax.rsqrt(jnp.mean(centred * centred, axis=1, keepdims=True) + EPS)
    normalized = centred * inv_std
    grad = jnp.concatenate([r[...] for r in refs[:-3]], axis=1).astype(F32)
    sums_ref[0:1, :] += jnp.sum(grad * normalized, axis=0, keepdims=True)
    sums_ref[1:2, :] += jnp.sum(grad, axis=0, keepdims=True)
    cot = cot_ref[...].astype(F32)
    sums_ref[2:3, :] += jnp.sum(cot, axis=0, keepdims=True)
    scaled = grad * gain_ref[...]
    first = jnp.mean(scaled, axis=1, keepdims=True)
    second = jnp.mean(scaled * normalized, axis=1, keepdims=True)
    o_ref[...] = (inv_std * (scaled - first - normalized * second) + cot).astype(BF16)


def norm_back(x, cot, grads, gain):
    rows, width = x.shape
    step = min(128, rows)
    tile = pl.BlockSpec((step, width), lambda i: (i, 0))
    return pl.pallas_call(
        norm_back_kernel,
        grid=(rows // step,),
        in_specs=[tile, tile]
        + [pl.BlockSpec((step, g.shape[1]), lambda i: (i, 0)) for g in grads]
        + [pl.BlockSpec((1, width), lambda i: (0, 0))],
        out_specs=[tile, pl.BlockSpec((8, width), lambda i: (0, 0))],
        out_shape=[jax.ShapeDtypeStruct(x.shape, BF16), jax.ShapeDtypeStruct((8, width), F32)],
        cost_estimate=cost(rows * width * 20, rows * width * 12),
        name="norm_back",
    )(x, cot, *grads, gain)


def pick(where_ref, i, tiles):
    turn = lax.div(i, tiles)
    busy = turn < where_ref[4]
    slot = jnp.where(busy, where_ref[2 * turn], where_ref[5])
    return jnp.where(busy, lax.rem(i, tiles), tiles - 1), slot, busy


def pick_shard(where_ref, i, tiles, refs, o_ref):
    turn = lax.div(i, tiles)
    if len(refs) == 1:
        o_ref[...] = refs[0][...]
        return

    @pl.when(where_ref[2 * turn + 1] == 0)
    def _():
        o_ref[...] = refs[0][...]

    @pl.when(where_ref[2 * turn + 1] == 1)
    def _():
        o_ref[...] = refs[1][...]


def project_tile(j, tall, x_ref, wq_ref, wu_ref, bq_ref, bu_ref, tables, qkv_ref, act_ref, slope_ref, over):
    if qkv_ref is not None:
        width = wq_ref.shape[1]

        @pl.when(j < 2)
        def _():
            scale = jnp.where(j == 0, HD**-0.5, 1.0).astype(F32)

            def turned(m, t):
                raw = (dot_nn(x_ref[m, :], wq_ref[...]) + bq_ref[...]) * scale
                turn = [r[t, :] for r in tables]
                for p in range(width // 128):
                    lanes = slice(p * 128, (p + 1) * 128)
                    qkv_ref[m, lanes] = rotate(raw[:, lanes], *turn).astype(BF16)

            over(turned)

        @pl.when(j == 2)
        def _():
            def plain(m, t):
                qkv_ref[m, :] = (dot_nn(x_ref[m, :], wq_ref[...]) + bq_ref[...]).astype(BF16)

            over(plain)

    if act_ref is not None:

        @pl.when(j > 2)
        def _():
            def gelu(m, t):
                act_ref[m, :], slope_ref[m, :] = gelu_and_slope(dot_nn(x_ref[m, :], wu_ref[...]) + bu_ref[...])

            over(gelu)


def gelu_and_slope(v):
    root = 0.7978845608028654
    cubic = 0.044715
    square = v * v
    t = jnp.tanh(v * (root + (root * cubic) * square))
    half = 0.5 + 0.5 * t
    slope = half + (v * (0.5 - 0.5 * (t * t))) * (root + (3.0 * root * cubic) * square)
    return (v * half).astype(BF16), slope.astype(BF16)


def forward_kernel(came, tiles, where_ref, *refs):
    x_refs, refs = refs[:came], refs[came:]
    wq_ref, wu_ref, bq_ref, bu_ref = refs[:4]
    tables = refs[4:7]
    normed_ref, qkv_ref, act_ref, slope_ref = refs[-4:]
    i = pl.program_id(0)
    j, _, busy = pick(where_ref, i, tiles)
    rows = normed_ref.shape[0]
    step = min(ROWS, rows)

    @pl.when(busy & (j == 0))
    def _():
        pick_shard(where_ref, i, tiles, x_refs, normed_ref)

    def over(act):
        for m in range(0, rows, step):
            act(slice(m, m + step), slice(m, m + step))

    @pl.when(busy)
    def _():
        project_tile(j, None, normed_ref, wq_ref, wu_ref, bq_ref, bu_ref, tables, qkv_ref, act_ref, slope_ref, over)


def queries_kernel(came, tiles, where_ref, *refs):
    x_refs, refs = refs[:came], refs[came:]
    wq_ref, bq_ref = refs[:2]
    tables = refs[2:5]
    normed_ref, qkv_ref = refs[-2:]
    i = pl.program_id(0)
    j, _, busy = pick(where_ref, i, tiles)
    rows = normed_ref.shape[0]
    step = min(ROWS, rows)

    @pl.when(busy & (j == 0))
    def _():
        pick_shard(where_ref, i, tiles, x_refs, normed_ref)

    def over(act):
        for m in range(0, rows, step):
            act(slice(m, m + step), slice(m, m + step))

    @pl.when(busy)
    def _():
        project_tile(j, None, normed_ref, wq_ref, None, bq_ref, None, tables, qkv_ref, None, None, over)


def queries_chunk(where, xs, wq, bq, tables, bufs, parts):
    rows, depth = xs[0].shape
    width = wq.shape[1] // 3
    tiles = 3

    def at(k):
        def index(i, w):
            j, slot, _ = pick(w, i, tiles)
            return ((slot, j), (0, j), (0, 0), (slot, 0), (jnp.minimum(slot, parts - 1), 0))[k]

        return index

    args = [where, *xs, wq, bq, *tables]
    return pl.pallas_call(
        functools.partial(queries_kernel, len(xs), tiles),
        grid_spec=pltpu.PrefetchScalarGridSpec(
            num_scalar_prefetch=1,
            grid=(len(xs) * tiles,),
            in_specs=[pl.BlockSpec((rows, depth), at(2))] * len(xs)
            + [pl.BlockSpec((depth, width), at(1)), pl.BlockSpec((1, width), at(1))]
            + [pl.BlockSpec((rows, 128), at(4))] * 3
            + [pl.BlockSpec(memory_space=pl.ANY)] * 2,
            out_specs=[pl.BlockSpec((rows, depth), at(3)), pl.BlockSpec((rows, width), at(0))],
        ),
        out_shape=[jax.ShapeDtypeStruct(b.shape, BF16) for b in bufs],
        input_output_aliases={len(args): 0, len(args) + 1: 1},
        cost_estimate=cost(6 * rows * depth * width, 6 * depth * width),
        name="queries_chunk",
    )(*args, *bufs)


def forward_chunk(where, xs, wq, wu, bq, bu, tables, bufs, parts):
    rows, depth = xs[0].shape
    width = wq.shape[1] // 3
    ff = wu.shape[1]
    tiles = 3 + ff // width

    def at(k):
        def index(i, w):
            j, slot, _ = pick(w, i, tiles)
            return (
                (slot, jnp.minimum(j, 2)),
                (slot, jnp.maximum(j - 3, 0)),
                (slot, 0),
                (0, jnp.minimum(j, 2)),
                (0, jnp.maximum(j - 3, 0)),
                (0, 0),
                (jnp.minimum(slot, parts - 1), 0),
            )[k]

        return index

    in_specs = (
        [pl.BlockSpec((rows, depth), at(5))] * len(xs)
        + [
            pl.BlockSpec((depth, width), at(3)),
            pl.BlockSpec((depth, width), at(4)),
            pl.BlockSpec((1, width), at(3)),
            pl.BlockSpec((1, width), at(4)),
        ]
        + [pl.BlockSpec((rows, 128), at(6))] * 3
    )
    total = (parts + 1) * rows
    shapes = [(total, depth), (total, 3 * width), (total, ff), (total, ff)]
    args = [where, *xs, wq, wu, bq, bu, *tables]
    aliases = {}
    if bufs is not None:
        aliases = {len(args) + k: k for k in range(4)}
        args += list(bufs)
        in_specs += [pl.BlockSpec(memory_space=pl.ANY)] * 4
    return pl.pallas_call(
        functools.partial(forward_kernel, len(xs), tiles),
        grid_spec=pltpu.PrefetchScalarGridSpec(
            num_scalar_prefetch=1,
            grid=(len(xs) * tiles,),
            in_specs=in_specs,
            out_specs=[
                pl.BlockSpec((rows, depth), at(2)),
                pl.BlockSpec((rows, width), at(0)),
                pl.BlockSpec((rows, width), at(1)),
                pl.BlockSpec((rows, width), at(1)),
            ],
        ),
        out_shape=[jax.ShapeDtypeStruct(s, BF16) for s in shapes],
        input_output_aliases=aliases,
        cost_estimate=cost(2 * rows * depth * (3 * width + ff), 2 * depth * (3 * width + ff)),
        name="forward_chunk",
    )(*args)


def collect(where_ref, came, shards, x_refs, held_ref, full_ref, in_sems, out_sems, first, last):
    rows = x_refs[0].shape[0]

    def spot(c):
        return pl.ds(pl.multiple_of(where_ref[1 + shards + 2 * c] * rows, rows), rows)

    def loads(c):
        return pltpu.make_async_copy(x_refs[c], held_ref.at[spot(c)], in_sems.at[c])

    def stores(c):
        return pltpu.make_async_copy(held_ref.at[spot(c)], full_ref.at[spot(c)], out_sems.at[c])

    def each(act):
        for c in range(came):
            pl.when(where_ref[2 + shards + 2 * c] > 0)(functools.partial(act, c))

    @pl.when(first)
    def _():
        each(lambda c: loads(c).start())
        each(lambda c: loads(c).wait())
        if full_ref is not None:
            each(lambda c: stores(c).start())

    def finish():
        pl.when(last)(lambda: each(lambda c: stores(c).wait()))

    return finish


def early_over(where_ref, rows):
    step = min(ROWS, rows)

    def over(act):
        def body(t, carry):
            for m in range(0, rows, step):
                at = pl.ds(pl.multiple_of(where_ref[1 + t] * rows + m, step), step)
                act(at, at)
            return carry

        lax.fori_loop(0, where_ref[0], body, 0)

    return over


def queries_early_kernel(came, shards, where_ref, *refs):
    x_refs, refs = refs[:came], refs[came:]
    wq_ref, bq_ref = refs[:2]
    tables = refs[2:5]
    normed_ref, qkv_ref, held_ref, in_sems, out_sems = refs[5:]
    j = pl.program_id(0)
    finish = collect(
        where_ref, came, shards, x_refs, held_ref, normed_ref, in_sems, out_sems,
        j == 0, j == pl.num_programs(0) - 1,
    )
    over = early_over(where_ref, x_refs[0].shape[0])
    project_tile(j, None, held_ref, wq_ref, None, bq_ref, None, tables, qkv_ref, None, None, over)
    finish()


def units_early_kernel(came, shards, where_ref, *refs):
    x_refs, refs = refs[:came], refs[came:]
    wu_ref, bu_ref, act_ref, slope_ref, held_ref, in_sems = refs
    j = pl.program_id(0)
    collect(where_ref, came, shards, x_refs, held_ref, None, in_sems, None, j == 0, None)
    over = early_over(where_ref, x_refs[0].shape[0])
    project_tile(j + 3, None, held_ref, None, wu_ref, None, bu_ref, None, None, act_ref, slope_ref, over)


def queries_early(where, xs, wq, bq, tables, parts):
    rows, depth = xs[0].shape
    width = wq.shape[1] // 3
    count = parts * rows
    in_place = pl.BlockSpec(memory_space=pl.ANY)
    return pl.pallas_call(
        functools.partial(queries_early_kernel, len(xs), parts),
        grid_spec=pltpu.PrefetchScalarGridSpec(
            num_scalar_prefetch=1,
            grid=(3,),
            in_specs=[in_place] * len(xs)
            + [pl.BlockSpec((depth, width), lambda j, w: (0, j)), pl.BlockSpec((1, width), lambda j, w: (0, j))]
            + [whole(t) for t in tables],
            out_specs=[in_place, pl.BlockSpec((count, width), lambda j, w: (0, j))],
            scratch_shapes=[
                pltpu.VMEM((count, depth), BF16),
                pltpu.SemaphoreType.DMA((len(xs),)),
                pltpu.SemaphoreType.DMA((len(xs),)),
            ],
        ),
        out_shape=[
            jax.ShapeDtypeStruct((count + rows, depth), BF16),
            jax.ShapeDtypeStruct((count + rows, 3 * width), BF16),
        ],
        cost_estimate=cost(6 * count * depth * width, 6 * depth * width),
        name="queries_early",
    )(where, *xs, wq, bq, *tables)


def units_early(where, xs, wu, bu, width, parts):
    rows, depth = xs[0].shape
    ff = wu.shape[1]
    count = parts * rows
    return pl.pallas_call(
        functools.partial(units_early_kernel, len(xs), parts),
        grid_spec=pltpu.PrefetchScalarGridSpec(
            num_scalar_prefetch=1,
            grid=(ff // width,),
            in_specs=[pl.BlockSpec(memory_space=pl.ANY)] * len(xs)
            + [pl.BlockSpec((depth, width), lambda j, w: (0, j)), pl.BlockSpec((1, width), lambda j, w: (0, j))],
            out_specs=[pl.BlockSpec((count, width), lambda j, w: (0, j))] * 2,
            scratch_shapes=[pltpu.VMEM((count, depth), BF16), pltpu.SemaphoreType.DMA((len(xs),))],
        ),
        out_shape=[jax.ShapeDtypeStruct((count + rows, ff), BF16)] * 2,
        cost_estimate=cost(2 * count * depth * ff, 2 * depth * ff),
        name="units_early",
    )(where, *xs, wu, bu)


def backward_early_kernel(came, shards, where_ref, *refs):
    c_refs, refs = refs[:came], refs[came:]
    wo_ref, wd_ref, slope_ref, cot_ref, ga_ref, gh_ref, held_ref, in_sems, out_sems = refs
    j = pl.program_id(0)
    finish = collect(
        where_ref, came, shards, c_refs, held_ref, cot_ref, in_sems, out_sems,
        j == 0, j == pl.num_programs(0) - 1,
    )
    rows = c_refs[0].shape[0]
    step = min(ROWS, rows)

    def over(act):
        def body(t, carry):
            for m in range(0, rows, step):
                act(pl.ds(pl.multiple_of(where_ref[1 + t] * rows + m, step), step))
            return carry

        lax.fori_loop(0, where_ref[0], body, 0)

    @pl.when(j == 0)
    def _():
        weight = side_by_side(wo_ref)

        def act(m):
            ga_ref[m, :] = dot_nt(held_ref[m, :], weight).astype(BF16)

        over(act)

    @pl.when(j > 0)
    def _():
        weight = side_by_side(wd_ref)

        def act(m):
            gh_ref[m, :] = (dot_nt(held_ref[m, :], weight) * slope_ref[m, :].astype(F32)).astype(BF16)

        over(act)

    finish()


def backward_early(where, cots, wo, wd, slope, parts):
    rows, depth = cots[0].shape
    pieces, width, piece = wo.shape
    ff = wd.shape[1]
    count = parts * rows
    total = count + rows
    in_place = pl.BlockSpec(memory_space=pl.ANY)

    def tile(j):
        return jnp.maximum(j - 1, 0)

    return pl.pallas_call(
        functools.partial(backward_early_kernel, len(cots), parts),
        grid_spec=pltpu.PrefetchScalarGridSpec(
            num_scalar_prefetch=1,
            grid=(1 + ff // width,),
            in_specs=[in_place] * len(cots)
            + [
                whole(wo),
                pl.BlockSpec((pieces, width, piece), lambda j, w: (0, tile(j), 0)),
                pl.BlockSpec((count, width), lambda j, w: (0, tile(j))),
            ],
            out_specs=[
                in_place,
                pl.BlockSpec((count, width), lambda j, w: (0, 0)),
                pl.BlockSpec((count, width), lambda j, w: (0, tile(j))),
            ],
            scratch_shapes=[
                pltpu.VMEM((count, depth), BF16),
                pltpu.SemaphoreType.DMA((len(cots),)),
                pltpu.SemaphoreType.DMA((len(cots),)),
            ],
        ),
        out_shape=[jax.ShapeDtypeStruct(s, BF16) for s in ((total, depth), (total, width), (total, ff))],
        cost_estimate=cost(2 * count * depth * (width + ff), 2 * depth * (width + ff)),
        name="backward_early",
    )(where, *cots, wo, wd, slope)


def low_lanes(rows):
    return lax.broadcasted_iota(jnp.int32, (rows, 128), 1) < HD


def attend_kernel(
    first_ref, q_ref, k_ref, v_ref, segc_ref, segr_ref, *refs
):
    o_ref, lse_ref, max_ref, acc_ref, bias_ref = refs[-5:]
    i = pl.program_id(0)
    block, width = q_ref.shape
    pairs = width // 128
    low = low_lanes(block)
    owns = (low, jnp.logical_not(low))
    max_ref[...] = jnp.full_like(max_ref, NEGATIVE)
    lse_ref[...] = jnp.zeros_like(lse_ref)
    acc_ref[...] = jnp.zeros_like(acc_ref)
    q0 = pl.multiple_of(i * block, block)
    query_seg = segr_ref[:, pl.ds(q0, block)]
    query_row = q0 + lax.broadcasted_iota(jnp.int32, (1, block), 1)

    def set_bias(k0):
        key_seg = segc_ref[pl.ds(k0, block), :]
        key_row = k0 + lax.broadcasted_iota(jnp.int32, (block, 1), 0)
        bias_ref[...] = jnp.where((key_seg == query_seg) & (key_row <= query_row), 0.0, NEGATIVE)

    def scores(k0, p, h):
        lanes = slice(p * 128, (p + 1) * 128)
        q = q_ref[:, lanes]
        mine = jnp.where(owns[h], q, jnp.zeros_like(q))
        return dot_nt(k_ref[pl.ds(k0, block), lanes], mine) + bias_ref[...]

    def find_max(j, carry):
        k0 = pl.multiple_of(j * block, block)
        set_bias(k0)
        for p in range(pairs):
            for h in range(2):
                s = scores(k0, p, h)
                max_ref[2 * p + h] = jnp.maximum(max_ref[2 * p + h], jnp.max(s, axis=0, keepdims=True))
        return carry

    lax.fori_loop(first_ref[i], i + 1, find_max, 0)

    def add_up(j, carry):
        k0 = pl.multiple_of(j * block, block)
        set_bias(k0)
        for p in range(pairs):
            v = v_ref[pl.ds(k0, block), p * 128 : (p + 1) * 128]
            for h in range(2):
                e = jnp.exp(scores(k0, p, h) - max_ref[2 * p + h])
                lse_ref[p, h : h + 1, :] += jnp.sum(e, axis=0, keepdims=True)
                acc_ref[2 * p + h] += dot_tn(e.astype(BF16), jnp.where(owns[h], v, jnp.ones_like(v)))
        return carry

    lax.fori_loop(first_ref[i], i + 1, add_up, 0)
    for p in range(pairs):
        even, odd = acc_ref[2 * p], acc_ref[2 * p + 1]
        o_ref[:, p * 128 : (p + 1) * 128] = jnp.where(
            low, even / pltpu.roll(even, HD, axis=1), odd / pltpu.roll(odd, HD, axis=1)
        ).astype(BF16)
        for h in range(2):
            lse_ref[p, h : h + 1, :] = max_ref[2 * p + h] + jnp.log(lse_ref[p, h : h + 1, :])


def attend(qkv, segc, segr, first, part, parts, bufs):
    count = segr.shape[1]
    whole_width = qkv.shape[1] // 3
    width = whole_width // parts
    pairs = width // 128
    in_place = [] if bufs is None else [pl.BlockSpec(memory_space=pl.ANY)] * 2
    return pl.pallas_call(
        attend_kernel,
        grid_spec=pltpu.PrefetchScalarGridSpec(
            num_scalar_prefetch=1,
            grid=(count // BLOCK,),
            in_specs=[
                pl.BlockSpec((BLOCK, width), lambda i, f: (i, part)),
                pl.BlockSpec((count, width), lambda i, f: (0, parts + part)),
                pl.BlockSpec((count, width), lambda i, f: (0, 2 * parts + part)),
                whole(segc),
                whole(segr),
            ]
            + in_place,
            out_specs=[
                pl.BlockSpec((BLOCK, width), lambda i, f: (i, part)),
                pl.BlockSpec((pairs, 8, BLOCK), lambda i, f: (part, 0, i)),
            ],
            scratch_shapes=[
                pltpu.VMEM((2 * pairs, 1, BLOCK), F32),
                pltpu.VMEM((2 * pairs, BLOCK, 128), F32),
                pltpu.VMEM((BLOCK, BLOCK), F32),
            ],
        ),
        out_shape=[
            jax.ShapeDtypeStruct((count, whole_width), BF16),
            jax.ShapeDtypeStruct((parts * pairs, 8, count), F32),
        ],
        input_output_aliases={} if bufs is None else {6: 0, 7: 1},
        cost_estimate=cost(30e9 * width / 512, count * width * 8),
        name="attend",
    )(first, qkv, qkv, qkv, segc, segr, *([] if bufs is None else bufs))


def attend_back_kernel(
    first_ref, q_ref, k_ref, v_ref, go_ref, o_ref, lse_ref, segc_ref, segr_ref,
    cos_ref, up_ref, down_ref, *refs,
):
    gq_ref, gk_ref, gv_ref, dq_ref, dk_ref, dv_ref, bias_ref = refs[-7:]
    i = pl.program_id(0)
    steps = pl.num_programs(0)
    block, width = q_ref.shape
    pairs = width // 128
    low = low_lanes(block)
    owns = (low, jnp.logical_not(low))

    @pl.when(i == 0)
    def _():
        dk_ref[...] = jnp.zeros_like(dk_ref)
        dv_ref[...] = jnp.zeros_like(dv_ref)

    dq_ref[...] = jnp.zeros_like(dq_ref)
    q0 = pl.multiple_of(i * block, block)
    query_seg = segr_ref[:, pl.ds(q0, block)]
    query_row = q0 + lax.broadcasted_iota(jnp.int32, (1, block), 1)
    half = jnp.where(
        lax.broadcasted_iota(jnp.int32, (8, 128), 1) // HD == lax.broadcasted_iota(jnp.int32, (8, 128), 0),
        1.0,
        0.0,
    ).astype(F32)
    inner = []
    for p in range(pairs):
        lanes = slice(p * 128, (p + 1) * 128)
        product = go_ref[:, lanes].astype(F32) * o_ref[:, lanes].astype(F32)
        inner.append(
            lax.dot_general(
                half, product, (((1,), (1,)), ((), ())),
                precision=lax.Precision.HIGHEST, preferred_element_type=F32,
            )
        )

    def body(j, carry):
        k0 = pl.multiple_of(j * block, block)
        key_seg = segc_ref[pl.ds(k0, block), :]
        key_row = k0 + lax.broadcasted_iota(jnp.int32, (block, 1), 0)
        bias_ref[...] = jnp.where((key_seg == query_seg) & (key_row <= query_row), 0.0, NEGATIVE)
        for p in range(pairs):
            lanes = slice(p * 128, (p + 1) * 128)
            k = k_ref[pl.ds(k0, block), lanes]
            v = v_ref[pl.ds(k0, block), lanes]
            q = q_ref[:, lanes]
            go = go_ref[:, lanes]
            sums = None
            for h in range(2):
                q_own, go_own, k_own = [jnp.where(owns[h], a, jnp.zeros_like(a)) for a in (q, go, k)]
                prob = jnp.exp(dot_nt(k, q_own) + bias_ref[...] - lse_ref[p, h : h + 1, :])
                grad_score = (prob * (dot_nt(v, go_own) - inner[p][h : h + 1, :])).astype(BF16)
                new = (
                    dot_nn(prob.astype(BF16), go_own),
                    dot_nn(grad_score, q_own),
                    dot_tn(grad_score, k_own),
                )
                sums = new if sums is None else tuple(a + b for a, b in zip(sums, new))
            dv_ref[pl.ds(k0, block), lanes] += sums[0]
            dk_ref[pl.ds(k0, block), lanes] += sums[1]
            dq_ref[:, lanes] += sums[2]
        return carry

    lax.fori_loop(first_ref[i], i + 1, body, 0)
    turn = [r[pl.ds(q0, block), :] for r in (cos_ref, up_ref, down_ref)]
    for p in range(pairs):
        lanes = slice(p * 128, (p + 1) * 128)
        gq_ref[:, lanes] = unrotate(dq_ref[:, lanes] * HD**-0.5, *turn).astype(BF16)

    @pl.when(i == steps - 1)
    def _():
        def finish(j, carry):
            k0 = pl.multiple_of(j * block, block)
            rows = pl.ds(k0, block)
            turn = [r[rows, :] for r in (cos_ref, up_ref, down_ref)]
            for p in range(pairs):
                lanes = slice(p * 128, (p + 1) * 128)
                gk_ref[rows, lanes] = unrotate(dk_ref[rows, lanes], *turn).astype(BF16)
                gv_ref[rows, lanes] = dv_ref[rows, lanes].astype(BF16)
            return carry

        lax.fori_loop(0, steps, finish, 0)


def attend_back(qkv, grad_out, out, lse, segc, segr, first, tables, part, parts, bufs):
    count = segr.shape[1]
    whole_width = qkv.shape[1] // 3
    width = whole_width // parts
    pairs = width // 128
    row_tile = pl.BlockSpec((BLOCK, width), lambda i, f: (i, part))
    column = pl.BlockSpec((count, width), lambda i, f: (0, part))
    in_place = [] if bufs is None else [pl.BlockSpec(memory_space=pl.ANY)] * 3
    args = [first, qkv, qkv, qkv, grad_out, out, lse, segc, segr, *tables]
    return pl.pallas_call(
        attend_back_kernel,
        grid_spec=pltpu.PrefetchScalarGridSpec(
            num_scalar_prefetch=1,
            grid=(count // BLOCK,),
            in_specs=[
                row_tile,
                pl.BlockSpec((count, width), lambda i, f: (0, parts + part)),
                pl.BlockSpec((count, width), lambda i, f: (0, 2 * parts + part)),
                row_tile,
                row_tile,
                pl.BlockSpec((pairs, 8, BLOCK), lambda i, f: (part, 0, i)),
                whole(segc),
                whole(segr),
                *[whole(t) for t in tables],
            ]
            + in_place,
            out_specs=[row_tile, column, column],
            scratch_shapes=[
                pltpu.VMEM((BLOCK, width), F32),
                pltpu.VMEM((count, width), F32),
                pltpu.VMEM((count, width), F32),
                pltpu.VMEM((BLOCK, BLOCK), F32),
            ],
        ),
        out_shape=[jax.ShapeDtypeStruct((count, whole_width), BF16)] * 3,
        input_output_aliases={} if bufs is None else {len(args) + k: k for k in range(3)},
        cost_estimate=cost(44e9 * width / 512, count * width * 20),
        name="attend_back",
    )(*args, *([] if bufs is None else bufs))


def side_by_side(ref):
    return jnp.concatenate([ref[b] for b in range(ref.shape[0])], axis=1)


def mix_kernel(att_ref, act_ref, wo_ref, wd_ref, o_ref):
    wo, wd = side_by_side(wo_ref), side_by_side(wd_ref)
    step = min(512, att_ref.shape[0])
    for m in range(0, att_ref.shape[0], step):
        rs = slice(m, m + step)
        o_ref[rs, :] = (dot_nn(att_ref[rs, :], wo) + dot_nn(act_ref[rs, :], wd)).astype(BF16)


def mix(att, act, wo, wd):
    pieces, width, piece = wo.shape
    ff = wd.shape[1]
    count = att.shape[0]
    group = max(1, 512 // piece)
    return pl.pallas_call(
        mix_kernel,
        grid=(pieces // group,),
        in_specs=[
            pl.BlockSpec((count, width), lambda j: (0, 0)),
            pl.BlockSpec((count, ff), lambda j: (0, 0)),
            pl.BlockSpec((group, width, piece), lambda j: (j, 0, 0)),
            pl.BlockSpec((group, ff, piece), lambda j: (j, 0, 0)),
        ],
        out_specs=pl.BlockSpec((count, group * piece), lambda j: (0, j)),
        out_shape=jax.ShapeDtypeStruct((count, pieces * piece), BF16),
        cost_estimate=cost(2 * count * (width + ff) * pieces * piece, 4 * count * ff),
        name="mix",
    )(att, act, wo, wd)


def mixed_kernel(x_ref, sum_ref, bias_ref, o_ref):
    o_ref[...] = (x_ref[...].astype(F32) + sum_ref[...].astype(F32) + bias_ref[...]).astype(BF16)


def mixed_out(x, total, bias):
    rows, width = x.shape
    step = min(256, rows)
    tile = pl.BlockSpec((step, width), lambda i: (i, 0))
    return pl.pallas_call(
        mixed_kernel,
        grid=(rows // step,),
        in_specs=[tile, tile, pl.BlockSpec((1, width), lambda i: (0, 0))],
        out_specs=tile,
        out_shape=jax.ShapeDtypeStruct(x.shape, BF16),
        cost_estimate=cost(rows * width * 4, rows * width * 6),
        name="mixed_out",
    )(x, total, bias)


def backward_kernel(came, tiles, where_ref, *refs):
    c_refs, refs = refs[:came], refs[came:]
    wo_ref, wd_ref, slope_ref = refs[:3]
    cot_ref, ga_ref, gh_ref = refs[-3:]
    i = pl.program_id(0)
    j, _, busy = pick(where_ref, i, tiles)
    rows = cot_ref.shape[0]
    step = min(ROWS, rows)

    @pl.when(busy & (j == 0))
    def _():
        pick_shard(where_ref, i, tiles, c_refs, cot_ref)
        weight = side_by_side(wo_ref)
        for m in range(0, rows, step):
            ga_ref[m : m + step, :] = dot_nt(cot_ref[m : m + step, :], weight).astype(BF16)

    @pl.when(busy & (j > 0))
    def _():
        weight = side_by_side(wd_ref)
        for m in range(0, rows, step):
            gh_ref[m : m + step, :] = (
                dot_nt(cot_ref[m : m + step, :], weight) * slope_ref[m : m + step, :].astype(F32)
            ).astype(BF16)


def backward_chunk(where, cots, wo, wd, slope, bufs, parts):
    rows, depth = cots[0].shape
    pieces, width, piece = wo.shape
    ff = wd.shape[1]
    tiles = 1 + ff // width

    def at(k):
        def index(i, w):
            j, slot, _ = pick(w, i, tiles)
            return ((0, 0), (0, jnp.maximum(j - 1, 0), 0), (slot, jnp.maximum(j - 1, 0)), (slot, 0))[k]

        return index

    in_specs = [pl.BlockSpec((rows, depth), at(0))] * len(cots) + [
        whole(wo),
        pl.BlockSpec((pieces, width, piece), at(1)),
        pl.BlockSpec((rows, width), at(2)),
    ]
    total = (parts + 1) * rows
    shapes = [(total, depth), (total, width), (total, ff)]
    args = [where, *cots, wo, wd, slope]
    aliases = {}
    if bufs is not None:
        aliases = {len(args) + k: k for k in range(3)}
        args += list(bufs)
        in_specs += [pl.BlockSpec(memory_space=pl.ANY)] * 3
    return pl.pallas_call(
        functools.partial(backward_kernel, len(cots), tiles),
        grid_spec=pltpu.PrefetchScalarGridSpec(
            num_scalar_prefetch=1,
            grid=(len(cots) * tiles,),
            in_specs=in_specs,
            out_specs=[
                pl.BlockSpec((rows, depth), at(3)),
                pl.BlockSpec((rows, width), at(3)),
                pl.BlockSpec((rows, width), at(2)),
            ],
        ),
        out_shape=[jax.ShapeDtypeStruct(s, BF16) for s in shapes],
        input_output_aliases=aliases,
        cost_estimate=cost(2 * rows * depth * (width + ff), 2 * depth * (width + ff)),
        name="backward_chunk",
    )(*args)


def grad_kernel(gq_ref, gk_ref, gv_ref, gh_ref, wq_ref, wu_ref, o_ref):
    step = min(512, gq_ref.shape[0])
    width = gq_ref.shape[1]
    for m in range(0, gq_ref.shape[0], step):
        rs = slice(m, m + step)
        left = jnp.concatenate([r[rs, :] for r in (gq_ref, gk_ref, gv_ref)], axis=1)
        o_ref[rs, :] = (dot_nt(left, wq_ref[...]) + dot_nt(gh_ref[rs, :], wu_ref[...])).astype(BF16)


def grad_normed(gqkv, gh, wq, wu, start, stop):
    count, width = gqkv[0].shape
    ff = gh.shape[1]
    tile = min(256, stop - start)
    first = start // tile
    return pl.pallas_call(
        grad_kernel,
        grid=((stop - start) // tile,),
        in_specs=[once((count, width))] * 3
        + [
            once((count, ff)),
            pl.BlockSpec((tile, wq.shape[1]), lambda j: (first + j, 0)),
            pl.BlockSpec((tile, wu.shape[1]), lambda j: (first + j, 0)),
        ],
        out_specs=pl.BlockSpec((count, tile), lambda j: (0, j)),
        out_shape=jax.ShapeDtypeStruct((count, stop - start), BF16),
        cost_estimate=cost(2 * count * (stop - start) * (3 * width + ff), 4 * count * ff),
        name="grad_normed",
    )(*gqkv, gh, wq, wu)


def put_columns(att_ref, act_ref, cot, o_ref, start, stop, add):
    width = att_ref.shape[1]
    at = start
    while at < stop:
        if at < width:
            end = min(stop, width)
            left = att_ref[:, at:end]
        else:
            end = min(stop, at + 512)
            left = act_ref[:, at - width : end - width]
        rows = slice(at - start, end - start)
        total = dot_tn(left, cot)
        if add is not None:
            total = total + add[0, rows, :].astype(F32)
        o_ref[0, rows, :] = total.astype(BF16)
        at = end


def columns_send_kernel(where_ref, att_ref, act_ref, c_ref, o_ref):
    put_columns(att_ref, act_ref, c_ref[...], o_ref, 0, o_ref.shape[1], None)


def columns_keep_kernel(where_ref, att_ref, act_ref, c_ref, came_ref, a_ref, b_ref):
    half = a_ref.shape[1]
    first = pl.program_id(0) < pl.num_programs(0) // 2

    @pl.when(first)
    def _():
        put_columns(att_ref, act_ref, c_ref[...], a_ref, 0, half, came_ref)

    @pl.when(jnp.logical_not(first))
    def _():
        put_columns(att_ref, act_ref, c_ref[...], b_ref, half, 2 * half, came_ref)


def rows_send_kernel(arrays, where_ref, x_ref, *refs):
    g_refs, o_ref, sum_ref = refs[:arrays], refs[-2], refs[-1]
    x = x_ref[...]
    first = pl.program_id(0) == 0
    start = 0
    for g_ref in g_refs:
        width = g_ref.shape[1]
        step = min(512, width)
        for m in range(0, width, step):
            o_ref[0, :, start + m : start + m + step] = dot_tn(x, g_ref[:, m : m + step]).astype(BF16)

        @pl.when(first)
        def _():
            ones = jnp.ones((8, g_ref.shape[0]), BF16)
            for m in range(0, width, step):
                sum_ref[:, start + m : start + m + step] = dot_nn(ones, g_ref[:, m : m + step])

        start += width


def rows_keep_kernel(arrays, where_ref, x_ref, *refs):
    g_refs, came_ref, a_ref, b_ref = refs[:arrays], *refs[arrays:]
    first = pl.program_id(0) < pl.num_programs(0) // 2
    x = x_ref[...]
    half = a_ref.shape[2]

    def put(o_ref, low):
        start = 0
        for g_ref in g_refs:
            width = g_ref.shape[1]
            at = max(start, low)
            while at < min(start + width, low + half):
                end = min(start + width, low + half, at + 512)
                o_ref[0, :, at - low : end - low] = (
                    dot_tn(x, g_ref[:, at - start : end - start])
                    + came_ref[0, :, at - low : end - low].astype(F32)
                ).astype(BF16)
                at = end
            start += width

    pl.when(first)(lambda: put(a_ref, 0))
    pl.when(jnp.logical_not(first))(lambda: put(b_ref, half))


def once(shape):
    return pl.BlockSpec(shape, lambda *_: (0,) * len(shape), pipeline_mode=pl.Buffered(1))


def column_grads(where, att, act, cot, places, came=None):
    count, width = att.shape
    ff = act.shape[1]
    piece = cot.shape[1] // (2 * places)
    flops = 2 * count * (width + ff) * piece * places
    base = [once((count, width)), once((count, ff)), pl.BlockSpec((count, piece), lambda t, w: (0, w[t]))]
    if came is None:
        return pl.pallas_call(
            columns_send_kernel,
            grid_spec=pltpu.PrefetchScalarGridSpec(
                num_scalar_prefetch=1,
                grid=(places,),
                in_specs=base,
                out_specs=pl.BlockSpec((1, width + ff, piece), lambda t, w: (t, 0, 0)),
            ),
            out_shape=jax.ShapeDtypeStruct((places, width + ff, piece), BF16),
            cost_estimate=cost(flops, 2 * count * (width + ff)),
            name="columns_send",
        )(where, att, act, cot)
    half = (width + ff) // 2
    turns = 2 * places
    return pl.pallas_call(
        columns_keep_kernel,
        grid_spec=pltpu.PrefetchScalarGridSpec(
            num_scalar_prefetch=1,
            grid=(turns,),
            in_specs=base
            + [pl.BlockSpec((1, half, piece), lambda t, w: (w[turns + t], t // places, 0))],
            out_specs=[
                pl.BlockSpec((1, half, piece), lambda t, w: (jnp.minimum(t, places - 1), 0, 0)),
                pl.BlockSpec((1, half, piece), lambda t, w: (jnp.maximum(t - places, 0), 0, 0)),
            ],
        ),
        out_shape=[jax.ShapeDtypeStruct((places, half, piece), BF16)] * 2,
        cost_estimate=cost(flops, 2 * count * (width + ff)),
        name="columns_keep",
    )(where, att, act, cot, came)


def row_grads(where, x, gs, count, places, came=None):
    width = sum(g.shape[1] for g in gs)
    piece = x.shape[1] // (2 * places)
    flops = 2 * count * width * piece * places
    base = [pl.BlockSpec((count, piece), lambda t, w: (0, w[t]))] + [once((count, g.shape[1])) for g in gs]
    if came is None:
        return pl.pallas_call(
            functools.partial(rows_send_kernel, len(gs)),
            grid_spec=pltpu.PrefetchScalarGridSpec(
                num_scalar_prefetch=1,
                grid=(places,),
                in_specs=base,
                out_specs=[
                    pl.BlockSpec((1, piece, width), lambda t, w: (t, 0, 0)),
                    pl.BlockSpec((8, width), lambda t, w: (0, 0)),
                ],
            ),
            out_shape=[
                jax.ShapeDtypeStruct((places, piece, width), BF16),
                jax.ShapeDtypeStruct((8, width), F32),
            ],
            cost_estimate=cost(flops, 2 * count * width),
            name="rows_send",
        )(where, x, *gs)
    half = width // 2
    turns = 2 * places
    return pl.pallas_call(
        functools.partial(rows_keep_kernel, len(gs)),
        grid_spec=pltpu.PrefetchScalarGridSpec(
            num_scalar_prefetch=1,
            grid=(turns,),
            in_specs=base
            + [pl.BlockSpec((1, piece, half), lambda t, w: (w[turns + t], 0, t // places))],
            out_specs=[
                pl.BlockSpec((1, piece, half), lambda t, w: (jnp.minimum(t, places - 1), 0, 0)),
                pl.BlockSpec((1, piece, half), lambda t, w: (jnp.maximum(t - places, 0), 0, 0)),
            ],
        ),
        out_shape=[jax.ShapeDtypeStruct((places, piece, half), BF16)] * 2,
        cost_estimate=cost(flops, 2 * count * width),
        name="rows_keep",
    )(where, x, *gs, came)


def after(value, *marks):
    return lax.optimization_barrier((value, *marks))[0]


def swap(x, bit):
    size = lax.axis_size("dp")
    return lax.ppermute(x, "dp", [(i, i ^ (1 << bit)) for i in range(size)])


def halve(xs, orders, k, sent=None):
    kept = []
    for x, y, bits in zip(xs, sent or xs, orders):
        rest = x.shape[0] // 2
        came = swap(y[rest:], bits[k])
        total = x[:rest].astype(F32) + came.astype(F32)
        kept.append(total if k == len(bits) - 1 else total.astype(BF16))
    return kept


def small_sum_kernel(phases, x_ref, o_ref, sent_ref, came_ref, send_sems, came_sems):
    barrier = pltpu.get_barrier_semaphore()

    def partner(axis, bit):
        return {axis: lax.axis_index(axis) ^ (1 << bit)}

    for axis, bit, _ in phases:
        pl.semaphore_signal(
            barrier, inc=1, device_id=partner(axis, bit), device_id_type=pl.DeviceIdType.MESH
        )
    pl.semaphore_wait(barrier, len(phases))
    sent_ref[0] = x_ref[...]
    for k, (axis, bit, rows) in enumerate(phases):
        span = pl.ds(0, rows)
        copy = pltpu.make_async_remote_copy(
            src_ref=sent_ref.at[k, span],
            dst_ref=came_ref.at[k, span],
            send_sem=send_sems.at[k],
            recv_sem=came_sems.at[k],
            device_id=partner(axis, bit),
            device_id_type=pl.DeviceIdType.MESH,
        )
        copy.start()
        copy.wait()
        total = sent_ref[k, 0:rows] + came_ref[k, 0:rows]
        if k == len(phases) - 1:
            o_ref[...] = sent_ref[k]
            o_ref[0:rows] = total
        else:
            sent_ref[k + 1] = sent_ref[k]
            sent_ref[k + 1, 0:rows] = total


def small_sums(x, common):
    rows = x.shape[0]
    phases = []
    for axis, height in (("dp", rows), ("tensor", common)):
        for bit in range(lax.axis_size(axis).bit_length() - 1):
            phases.append((axis, bit, height))
    return pl.pallas_call(
        functools.partial(small_sum_kernel, phases),
        in_specs=[pl.BlockSpec(memory_space=pltpu.VMEM)],
        out_specs=pl.BlockSpec(memory_space=pltpu.VMEM),
        out_shape=jax.ShapeDtypeStruct(x.shape, F32),
        scratch_shapes=[
            pltpu.VMEM((len(phases), *x.shape), F32),
            pltpu.VMEM((len(phases), *x.shape), F32),
            pltpu.SemaphoreType.DMA((len(phases),)),
            pltpu.SemaphoreType.DMA((len(phases),)),
        ],
        compiler_params=pltpu.CompilerParams(collective_id=0, has_side_effects=True),
        name="small_sums",
    )(x)


def local(
    tokens, segments, ln_gain, ln_shift, qkv_weight, qkv_bias, out_weight, out_bias,
    fc1_weight, fc1_bias, fc2_weight, fc2_bias, cotangent,
):
    n = lax.axis_size("tensor")
    pieces = lax.axis_size("dp")
    me = lax.axis_index("tensor")
    rows, depth = tokens.shape
    count = segments.shape[1]
    width = qkv_weight.shape[2]

    def shift(x, pairs):
        return lax.ppermute(x, "tensor", pairs)

    def turns(step):
        left, right = me - step, me + step
        has_left, has_right = left >= 0, right < n
        one = jnp.where(has_left, left, right)
        last = jnp.where(has_right, right, jnp.where(has_left, left, n))
        busy = has_left.astype(jnp.int32) + has_right.astype(jnp.int32)
        values = [one, jnp.where(has_left, 0, 1), right, 1, busy, last]
        return jnp.stack([jnp.asarray(v, jnp.int32) for v in values])

    def present_shards(steps):
        offsets = [0] + [d * s for s in range(1, steps + 1) for d in (-1, 1)]
        shards = jnp.stack([me + d for d in offsets])
        present = (shards >= 0) & (shards < n)
        order = jnp.sort(jnp.where(present, shards, n))
        order = jnp.concatenate([order, jnp.full((n,), n, order.dtype)])[:n]
        return jnp.concatenate(
            [
                jnp.sum(present.astype(jnp.int32))[None],
                order,
                jnp.stack([jnp.clip(shards, 0, n - 1), present.astype(jnp.int32)], axis=1).reshape(-1),
            ]
        ).astype(jnp.int32)

    early = present_shards(n - 2)
    late = turns(n - 1)

    own_normed = norm(tokens, ln_gain[None], ln_shift[None])

    w_qkv = lax.all_gather(qkv_weight.reshape(-1, 3 * width), "dp", axis=0, tiled=True)
    w_up = lax.all_gather(fc1_weight, "dp", axis=0, tiled=True)
    w_out = lax.all_gather(out_weight, "dp", axis=0)
    w_down = lax.all_gather(fc2_weight, "dp", axis=0)

    segment_row = segments[0]
    starts = seq_starts(segment_row)
    tables = rotary_tables(jnp.arange(count, dtype=jnp.int32) - starts)
    first = starts[::BLOCK] // BLOCK
    segc, segr = segment_row[:, None], segment_row[None, :]

    bias_qkv, bias_up = qkv_bias.reshape(1, -1), fc1_bias[None]
    def line_step(pair, s):
        right, left = pair
        return [
            shift(right, [(i, i + 1) for i in range(s - 1, n - 1)]),
            shift(left, [(i, i - 1) for i in range(1, n - s + 1)]),
        ]

    def line_sum(x):
        return lax.psum_scatter(x, "tensor", scatter_dimension=0, tiled=True)

    def flat(pairs):
        return [x for pair in pairs for x in pair]

    project = (w_qkv, w_up, bias_qkv, bias_up, tables)
    normed_in = [line_step([own_normed] * 2, 1)]
    normed, qkv = queries_early(
        after(present_shards(1), first, segc), [own_normed] + normed_in[0], w_qkv, bias_qkv, tables, n
    )
    for s in range(2, n):
        normed_in.append(line_step(after(tuple(normed_in[-1]), qkv) if s == 3 else normed_in[-1], s))
    act, slope = units_early(
        after(early, qkv), [own_normed] + flat(normed_in[:-1]), w_up, bias_up, width, n
    )
    normed, qkv = after((normed, qkv), act)
    for s in range(2, n - 1):
        normed, qkv = queries_chunk(turns(s), normed_in[s - 1], w_qkv, bias_qkv, tables, (normed, qkv), n)
    cot_in = [line_step([after(cotangent, *normed_in[-1], qkv)] * 2, 1)]
    normed, qkv, act, slope = forward_chunk(late, normed_in[-1], *project, (normed, qkv, act, slope), n)

    att, lse = attend(qkv, segc, segr, first, 0, 1, None)
    cot_in.append(line_step(after(tuple(cot_in[-1]), att), 2))
    part = mix(att, act, w_out, w_down)
    for s in range(3, n):
        cot_in.append(line_step(after(tuple(cot_in[-1]), part), s))
    bufs = backward_early(after(early, part), [cotangent] + flat(cot_in[:-1]), w_out, w_down, slope, n)
    block_sum = line_sum(after(part, bufs[2], *cot_in[-1]))
    cot, grad_att, grad_hid = backward_chunk(late, cot_in[-1], w_out, w_down, slope, bufs, n)
    bits = [b for b in range(1, pieces.bit_length() - 1)]
    places = pieces // 2
    mine = lax.axis_index("dp")

    def place_of(r, order):
        return sum(((r >> (len(order) - 1 - k)) & 1) << bit for k, bit in enumerate(order))

    kept = [place_of(r, bits) for r in range(places)] + [place_of(r, bits[::-1]) for r in range(places)]
    send_where = mine ^ jnp.array([2 * q + 1 for q in range(places)], jnp.int32)
    keep_where = jnp.concatenate([mine ^ jnp.array(kept, jnp.int32), jnp.array(kept, jnp.int32) // 2])

    orders = (bits, bits[::-1])

    def finish(pair, axis, *marks):
        for k in range(1, len(bits)):
            pair = halve([after(half, *marks) for half in pair], orders, k, pair)
        return jnp.concatenate([half[0].astype(F32) for half in pair], axis=axis)

    col_send = column_grads(send_where, att, act, cot, places)
    up_send, up_sum = row_grads(send_where, normed, [after(grad_hid, col_send)], count, places)
    grad_qkv = attend_back(
        qkv, after(grad_att, up_sum), att, lse, segc, segr, first, tables, 0, 1, None
    )
    col_came, up_came = swap(col_send, 0), swap(up_send, 0)
    part = grad_normed(grad_qkv, after(grad_hid, col_came, up_came), w_qkv, w_up, 0, depth)
    grad_sum = line_sum(after(part, block_sum))
    col_pair = column_grads(keep_where, att, act, after(cot, part), places, col_came)
    qkv_send, qkv_sum = row_grads(send_where, normed, after(tuple(grad_qkv), col_pair[0]), count, places)
    up_pair = row_grads(
        keep_where, normed, [after(grad_hid, qkv_sum)], count, places, up_came
    )
    col_pair = halve([after(c, up_pair[0]) for c in col_pair], orders, 0, col_pair)
    qkv_pair = row_grads(
        keep_where, after(normed, *col_pair), grad_qkv, count, places, swap(qkv_send, 0)
    )
    up_pair = halve([after(u, qkv_pair[0]) for u in up_pair], orders, 0, up_pair)
    qkv_kept = qkv_pair[0]
    qkv_pair = halve(qkv_pair, orders, 0)
    mixed = mixed_out(tokens, after(block_sum, *qkv_pair), (out_bias + fc2_bias)[None])
    input_grad, sums = norm_back(tokens, after(cotangent, mixed), [grad_sum], ln_gain[None])
    common = 3 * depth // 128
    pack = jnp.concatenate([a.reshape(-1, 128) for a in (sums[:3], up_sum[0], qkv_sum[0])])
    pack = jnp.pad(pack, ((0, -pack.shape[0] % 8), (0, 0)))
    pack = small_sums(pack, common)
    col_out, up_out, qkv_out = finish(col_pair, 0, qkv_kept), finish(up_pair, 1, *qkv_pair), finish(qkv_pair, 1)
    total = pack[:common].reshape(3, depth)
    ff_rows = up_sum.shape[1] // 128
    up_bias_grad = pack[common : common + ff_rows].reshape(-1)
    qkv_bias_grad = pack[common + ff_rows : common + ff_rows + 3 * width // 128].reshape(3, width)
    return (
        mixed,
        input_grad,
        qkv_out.reshape(-1, 3, width),
        qkv_bias_grad,
        col_out[:width],
        total[2],
        up_out,
        up_bias_grad,
        col_out[width:],
        total[2],
        total[0],
        total[1],
    )


def solution(mesh):
    in_specs = (
        P(("dp", "tensor"), None),
        P("dp", None),
        P(),
        P(),
        P("dp", None, "tensor"),
        P(None, "tensor"),
        P("tensor", "dp"),
        P(),
        P("dp", "tensor"),
        P("tensor"),
        P("tensor", "dp"),
        P(),
        P(("dp", "tensor"), None),
    )
    out_specs = (
        P(("dp", "tensor"), None),
        P(("dp", "tensor"), None),
        P("dp", None, "tensor"),
        P(None, "tensor"),
        P("tensor", "dp"),
        P(),
        P("dp", "tensor"),
        P("tensor"),
        P("tensor", "dp"),
        P(),
        P(),
        P(),
    )
    return jax.shard_map(local, mesh=mesh, in_specs=in_specs, out_specs=out_specs, check_vma=False)
```

```python
import functools

import jax
import jax.numpy as jnp
from jax import lax
from jax.experimental import pallas as pl
from jax.experimental.pallas import tpu as pltpu
from jax.sharding import PartitionSpec as P

HD = 64
ROT = 32
EPS = 1e-05
ROPE_BASE = 10000.0
NEGATIVE = -1e30
BLOCK = 256
ROWS = 256
SHRINK = 20

F32 = jnp.float32
BF16 = jnp.bfloat16


def dot_nn(a, b):
    return lax.dot_general(a, b, (((1,), (0,)), ((), ())), preferred_element_type=F32)


def dot_nt(a, b):
    return lax.dot_general(a, b, (((1,), (1,)), ((), ())), preferred_element_type=F32)


def dot_tn(a, b):
    return lax.dot_general(a, b, (((0,), (0,)), ((), ())), preferred_element_type=F32)


def cost(flops, moved, trans=0):
    return pl.CostEstimate(flops=int(flops / SHRINK), bytes_accessed=int(moved / SHRINK), transcendentals=0)


def whole(a):
    return pl.BlockSpec(a.shape, lambda *_: (0,) * a.ndim)


def seq_starts(segment_row):
    count = segment_row.shape[0]
    index = jnp.arange(count, dtype=jnp.int32)
    begins = jnp.concatenate([jnp.ones((1,), dtype=bool), segment_row[1:] != segment_row[:-1]])
    return lax.cummax(jnp.where(begins, index, jnp.zeros_like(index)), axis=0)


def rotary_tables(positions):
    half = ROT // 2
    lane = jnp.arange(128, dtype=jnp.int32) % HD
    frequency = ROPE_BASE ** (-((lane % half).astype(F32) * 2.0) / ROT)
    angles = positions.astype(F32)[:, None] * frequency[None, :]
    cosine = jnp.where(lane < ROT, jnp.cos(angles), 1.0)
    sine = jnp.sin(angles)
    sine_up = jnp.where(lane < half, -sine, 0.0)
    sine_down = jnp.where((lane >= half) & (lane < ROT), sine, 0.0)
    return cosine, sine_up, sine_down


def rotate(x, cosine, sine_up, sine_down):
    return (
        x * cosine
        + pltpu.roll(x, 128 - ROT // 2, axis=1) * sine_up
        + pltpu.roll(x, ROT // 2, axis=1) * sine_down
    )


def unrotate(x, cosine, sine_up, sine_down):
    return (
        x * cosine
        - pltpu.roll(x, 128 - ROT // 2, axis=1) * sine_up
        - pltpu.roll(x, ROT // 2, axis=1) * sine_down
    )


def norm_kernel(x_ref, gain_ref, shift_ref, o_ref):
    x = x_ref[...].astype(F32)
    centred = x - jnp.mean(x, axis=1, keepdims=True)
    inv_std = lax.rsqrt(jnp.mean(centred * centred, axis=1, keepdims=True) + EPS)
    o_ref[...] = (centred * inv_std * gain_ref[...] + shift_ref[...]).astype(BF16)


def norm(x, gain, shift):
    rows, width = x.shape
    step = rows // 2
    row = pl.BlockSpec((1, width), lambda i: (0, 0))
    tile = pl.BlockSpec((step, width), lambda i: (i, 0))
    return pl.pallas_call(
        norm_kernel,
        grid=(rows // step,),
        in_specs=[tile, row, row],
        out_specs=tile,
        out_shape=jax.ShapeDtypeStruct(x.shape, BF16),
        cost_estimate=cost(rows * width * 8, rows * width * 4),
        name="norm",
    )(x, gain, shift)


def norm_back_kernel(x_ref, cot_ref, *refs):
    gain_ref, o_ref, sums_ref = refs[-3:]

    @pl.when(pl.program_id(0) == 0)
    def _():
        sums_ref[...] = jnp.zeros_like(sums_ref)

    x = x_ref[...].astype(F32)
    centred = x - jnp.mean(x, axis=1, keepdims=True)
    inv_std = lax.rsqrt(jnp.mean(centred * centred, axis=1, keepdims=True) + EPS)
    normalized = centred * inv_std
    grad = jnp.concatenate([r[...] for r in refs[:-3]], axis=1).astype(F32)
    sums_ref[0:1, :] += jnp.sum(grad * normalized, axis=0, keepdims=True)
    sums_ref[1:2, :] += jnp.sum(grad, axis=0, keepdims=True)
    cot = cot_ref[...].astype(F32)
    sums_ref[2:3, :] += jnp.sum(cot, axis=0, keepdims=True)
    scaled = grad * gain_ref[...]
    first = jnp.mean(scaled, axis=1, keepdims=True)
    second = jnp.mean(scaled * normalized, axis=1, keepdims=True)
    o_ref[...] = (inv_std * (scaled - first - normalized * second) + cot).astype(BF16)


def norm_back(x, cot, grads, gain):
    rows, width = x.shape
    step = min(128, rows)
    tile = pl.BlockSpec((step, width), lambda i: (i, 0))
    return pl.pallas_call(
        norm_back_kernel,
        grid=(rows // step,),
        in_specs=[tile, tile]
        + [pl.BlockSpec((step, g.shape[1]), lambda i: (i, 0)) for g in grads]
        + [pl.BlockSpec((1, width), lambda i: (0, 0))],
        out_specs=[tile, pl.BlockSpec((8, width), lambda i: (0, 0))],
        out_shape=[jax.ShapeDtypeStruct(x.shape, BF16), jax.ShapeDtypeStruct((8, width), F32)],
        cost_estimate=cost(rows * width * 20, rows * width * 12),
        name="norm_back",
    )(x, cot, *grads, gain)


def pick(where_ref, i, tiles):
    turn = lax.div(i, tiles)
    busy = turn < where_ref[4]
    slot = jnp.where(busy, where_ref[2 * turn], where_ref[5])
    return jnp.where(busy, lax.rem(i, tiles), tiles - 1), slot, busy


def pick_shard(where_ref, i, tiles, refs, o_ref):
    turn = lax.div(i, tiles)
    if len(refs) == 1:
        o_ref[...] = refs[0][...]
        return

    @pl.when(where_ref[2 * turn + 1] == 0)
    def _():
        o_ref[...] = refs[0][...]

    @pl.when(where_ref[2 * turn + 1] == 1)
    def _():
        o_ref[...] = refs[1][...]


def project_tile(j, tall, x_ref, wq_ref, wu_ref, bq_ref, bu_ref, tables, qkv_ref, act_ref, slope_ref, over):
    if qkv_ref is not None:
        width = wq_ref.shape[1]

        @pl.when(j < 2)
        def _():
            scale = jnp.where(j == 0, HD**-0.5, 1.0).astype(F32)

            def turned(m, t):
                raw = (dot_nn(x_ref[m, :], wq_ref[...]) + bq_ref[...]) * scale
                turn = [r[t, :] for r in tables]
                for p in range(width // 128):
                    lanes = slice(p * 128, (p + 1) * 128)
                    qkv_ref[m, lanes] = rotate(raw[:, lanes], *turn).astype(BF16)

            over(turned)

        @pl.when(j == 2)
        def _():
            def plain(m, t):
                qkv_ref[m, :] = (dot_nn(x_ref[m, :], wq_ref[...]) + bq_ref[...]).astype(BF16)

            over(plain)

    if act_ref is not None:

        @pl.when(j > 2)
        def _():
            def gelu(m, t):
                act_ref[m, :], slope_ref[m, :] = gelu_and_slope(dot_nn(x_ref[m, :], wu_ref[...]) + bu_ref[...])

            over(gelu)


def gelu_and_slope(v):
    root = 0.7978845608028654
    cubic = 0.044715
    square = v * v
    t = jnp.tanh(v * (root + (root * cubic) * square))
    half = 0.5 + 0.5 * t
    slope = half + (v * (0.5 - 0.5 * (t * t))) * (root + (3.0 * root * cubic) * square)
    return (v * half).astype(BF16), slope.astype(BF16)


def forward_kernel(came, tiles, where_ref, *refs):
    x_refs, refs = refs[:came], refs[came:]
    wq_ref, wu_ref, bq_ref, bu_ref = refs[:4]
    tables = refs[4:7]
    normed_ref, qkv_ref, act_ref, slope_ref = refs[-4:]
    i = pl.program_id(0)
    j, _, busy = pick(where_ref, i, tiles)
    rows = normed_ref.shape[0]
    step = min(ROWS, rows)

    @pl.when(busy & (j == 0))
    def _():
        pick_shard(where_ref, i, tiles, x_refs, normed_ref)

    def over(act):
        for m in range(0, rows, step):
            act(slice(m, m + step), slice(m, m + step))

    @pl.when(busy)
    def _():
        project_tile(j, None, normed_ref, wq_ref, wu_ref, bq_ref, bu_ref, tables, qkv_ref, act_ref, slope_ref, over)


def queries_kernel(came, tiles, where_ref, *refs):
    x_refs, refs = refs[:came], refs[came:]
    wq_ref, bq_ref = refs[:2]
    tables = refs[2:5]
    normed_ref, qkv_ref = refs[-2:]
    i = pl.program_id(0)
    j, _, busy = pick(where_ref, i, tiles)
    rows = normed_ref.shape[0]
    step = min(ROWS, rows)

    @pl.when(busy & (j == 0))
    def _():
        pick_shard(where_ref, i, tiles, x_refs, normed_ref)

    def over(act):
        for m in range(0, rows, step):
            act(slice(m, m + step), slice(m, m + step))

    @pl.when(busy)
    def _():
        project_tile(j, None, normed_ref, wq_ref, None, bq_ref, None, tables, qkv_ref, None, None, over)


def queries_chunk(where, xs, wq, bq, tables, bufs, parts):
    rows, depth = xs[0].shape
    width = wq.shape[1] // 3
    tiles = 3

    def at(k):
        def index(i, w):
            j, slot, _ = pick(w, i, tiles)
            return ((slot, j), (0, j), (0, 0), (slot, 0), (jnp.minimum(slot, parts - 1), 0))[k]

        return index

    args = [where, *xs, wq, bq, *tables]
    return pl.pallas_call(
        functools.partial(queries_kernel, len(xs), tiles),
        grid_spec=pltpu.PrefetchScalarGridSpec(
            num_scalar_prefetch=1,
            grid=(len(xs) * tiles,),
            in_specs=[pl.BlockSpec((rows, depth), at(2))] * len(xs)
            + [pl.BlockSpec((depth, width), at(1)), pl.BlockSpec((1, width), at(1))]
            + [pl.BlockSpec((rows, 128), at(4))] * 3
            + [pl.BlockSpec(memory_space=pl.ANY)] * 2,
            out_specs=[pl.BlockSpec((rows, depth), at(3)), pl.BlockSpec((rows, width), at(0))],
        ),
        out_shape=[jax.ShapeDtypeStruct(b.shape, BF16) for b in bufs],
        input_output_aliases={len(args): 0, len(args) + 1: 1},
        cost_estimate=cost(6 * rows * depth * width, 6 * depth * width),
        name="queries_chunk",
    )(*args, *bufs)


def forward_chunk(where, xs, wq, wu, bq, bu, tables, bufs, parts):
    rows, depth = xs[0].shape
    width = wq.shape[1] // 3
    ff = wu.shape[1]
    tiles = 3 + ff // width

    def at(k):
        def index(i, w):
            j, slot, _ = pick(w, i, tiles)
            return (
                (slot, jnp.minimum(j, 2)),
                (slot, jnp.maximum(j - 3, 0)),
                (slot, 0),
                (0, jnp.minimum(j, 2)),
                (0, jnp.maximum(j - 3, 0)),
                (0, 0),
                (jnp.minimum(slot, parts - 1), 0),
            )[k]

        return index

    in_specs = (
        [pl.BlockSpec((rows, depth), at(5))] * len(xs)
        + [
            pl.BlockSpec((depth, width), at(3)),
            pl.BlockSpec((depth, width), at(4)),
            pl.BlockSpec((1, width), at(3)),
            pl.BlockSpec((1, width), at(4)),
        ]
        + [pl.BlockSpec((rows, 128), at(6))] * 3
    )
    total = (parts + 1) * rows
    shapes = [(total, depth), (total, 3 * width), (total, ff), (total, ff)]
    args = [where, *xs, wq, wu, bq, bu, *tables]
    aliases = {}
    if bufs is not None:
        aliases = {len(args) + k: k for k in range(4)}
        args += list(bufs)
        in_specs += [pl.BlockSpec(memory_space=pl.ANY)] * 4
    return pl.pallas_call(
        functools.partial(forward_kernel, len(xs), tiles),
        grid_spec=pltpu.PrefetchScalarGridSpec(
            num_scalar_prefetch=1,
            grid=(len(xs) * tiles,),
            in_specs=in_specs,
            out_specs=[
                pl.BlockSpec((rows, depth), at(2)),
                pl.BlockSpec((rows, width), at(0)),
                pl.BlockSpec((rows, width), at(1)),
                pl.BlockSpec((rows, width), at(1)),
            ],
        ),
        out_shape=[jax.ShapeDtypeStruct(s, BF16) for s in shapes],
        input_output_aliases=aliases,
        cost_estimate=cost(2 * rows * depth * (3 * width + ff), 2 * depth * (3 * width + ff)),
        name="forward_chunk",
    )(*args)


def collect(where_ref, came, shards, x_refs, held_ref, full_ref, in_sems, out_sems, first, last):
    rows = x_refs[0].shape[0]

    def spot(c):
        return pl.ds(pl.multiple_of(where_ref[1 + shards + 2 * c] * rows, rows), rows)

    def loads(c):
        return pltpu.make_async_copy(x_refs[c], held_ref.at[spot(c)], in_sems.at[c])

    def stores(c):
        return pltpu.make_async_copy(held_ref.at[spot(c)], full_ref.at[spot(c)], out_sems.at[c])

    def each(act):
        for c in range(came):
            pl.when(where_ref[2 + shards + 2 * c] > 0)(functools.partial(act, c))

    @pl.when(first)
    def _():
        each(lambda c: loads(c).start())
        each(lambda c: loads(c).wait())
        if full_ref is not None:
            each(lambda c: stores(c).start())

    def finish():
        pl.when(last)(lambda: each(lambda c: stores(c).wait()))

    return finish


def early_over(where_ref, rows):
    step = min(ROWS, rows)

    def over(act):
        def body(t, carry):
            for m in range(0, rows, step):
                at = pl.ds(pl.multiple_of(where_ref[1 + t] * rows + m, step), step)
                act(at, at)
            return carry

        lax.fori_loop(0, where_ref[0], body, 0)

    return over


def queries_early_kernel(came, shards, where_ref, *refs):
    x_refs, refs = refs[:came], refs[came:]
    wq_ref, bq_ref = refs[:2]
    tables = refs[2:5]
    normed_ref, qkv_ref, held_ref, in_sems, out_sems = refs[5:]
    j = pl.program_id(0)
    finish = collect(
        where_ref, came, shards, x_refs, held_ref, normed_ref, in_sems, out_sems,
        j == 0, j == pl.num_programs(0) - 1,
    )
    over = early_over(where_ref, x_refs[0].shape[0])
    project_tile(j, None, held_ref, wq_ref, None, bq_ref, None, tables, qkv_ref, None, None, over)
    finish()


def units_early_kernel(came, shards, where_ref, *refs):
    x_refs, refs = refs[:came], refs[came:]
    wu_ref, bu_ref, act_ref, slope_ref, held_ref, in_sems = refs
    j = pl.program_id(0)
    collect(where_ref, came, shards, x_refs, held_ref, None, in_sems, None, j == 0, None)
    over = early_over(where_ref, x_refs[0].shape[0])
    project_tile(j + 3, None, held_ref, None, wu_ref, None, bu_ref, None, None, act_ref, slope_ref, over)


def queries_early(where, xs, wq, bq, tables, parts):
    rows, depth = xs[0].shape
    width = wq.shape[1] // 3
    count = parts * rows
    in_place = pl.BlockSpec(memory_space=pl.ANY)
    return pl.pallas_call(
        functools.partial(queries_early_kernel, len(xs), parts),
        grid_spec=pltpu.PrefetchScalarGridSpec(
            num_scalar_prefetch=1,
            grid=(3,),
            in_specs=[in_place] * len(xs)
            + [pl.BlockSpec((depth, width), lambda j, w: (0, j)), pl.BlockSpec((1, width), lambda j, w: (0, j))]
            + [whole(t) for t in tables],
            out_specs=[in_place, pl.BlockSpec((count, width), lambda j, w: (0, j))],
            scratch_shapes=[
                pltpu.VMEM((count, depth), BF16),
                pltpu.SemaphoreType.DMA((len(xs),)),
                pltpu.SemaphoreType.DMA((len(xs),)),
            ],
        ),
        out_shape=[
            jax.ShapeDtypeStruct((count + rows, depth), BF16),
            jax.ShapeDtypeStruct((count + rows, 3 * width), BF16),
        ],
        cost_estimate=cost(6 * count * depth * width, 6 * depth * width),
        name="queries_early",
    )(where, *xs, wq, bq, *tables)


def units_early(where, xs, wu, bu, width, parts):
    rows, depth = xs[0].shape
    ff = wu.shape[1]
    count = parts * rows
    return pl.pallas_call(
        functools.partial(units_early_kernel, len(xs), parts),
        grid_spec=pltpu.PrefetchScalarGridSpec(
            num_scalar_prefetch=1,
            grid=(ff // width,),
            in_specs=[pl.BlockSpec(memory_space=pl.ANY)] * len(xs)
            + [pl.BlockSpec((depth, width), lambda j, w: (0, j)), pl.BlockSpec((1, width), lambda j, w: (0, j))],
            out_specs=[pl.BlockSpec((count, width), lambda j, w: (0, j))] * 2,
            scratch_shapes=[pltpu.VMEM((count, depth), BF16), pltpu.SemaphoreType.DMA((len(xs),))],
        ),
        out_shape=[jax.ShapeDtypeStruct((count + rows, ff), BF16)] * 2,
        cost_estimate=cost(2 * count * depth * ff, 2 * depth * ff),
        name="units_early",
    )(where, *xs, wu, bu)


def backward_early_kernel(came, shards, where_ref, *refs):
    c_refs, refs = refs[:came], refs[came:]
    wo_ref, wd_ref, slope_ref, cot_ref, ga_ref, gh_ref, held_ref, in_sems, out_sems = refs
    j = pl.program_id(0)
    finish = collect(
        where_ref, came, shards, c_refs, held_ref, cot_ref, in_sems, out_sems,
        j == 0, j == pl.num_programs(0) - 1,
    )
    rows = c_refs[0].shape[0]
    step = min(ROWS, rows)

    def over(act):
        def body(t, carry):
            for m in range(0, rows, step):
                act(pl.ds(pl.multiple_of(where_ref[1 + t] * rows + m, step), step))
            return carry

        lax.fori_loop(0, where_ref[0], body, 0)

    @pl.when(j == 0)
    def _():
        weight = side_by_side(wo_ref)

        def act(m):
            ga_ref[m, :] = dot_nt(held_ref[m, :], weight).astype(BF16)

        over(act)

    @pl.when(j > 0)
    def _():
        weight = side_by_side(wd_ref)

        def act(m):
            gh_ref[m, :] = (dot_nt(held_ref[m, :], weight) * slope_ref[m, :].astype(F32)).astype(BF16)

        over(act)

    finish()


def backward_early(where, cots, wo, wd, slope, parts):
    rows, depth = cots[0].shape
    pieces, width, piece = wo.shape
    ff = wd.shape[1]
    count = parts * rows
    total = count + rows
    in_place = pl.BlockSpec(memory_space=pl.ANY)

    def tile(j):
        return jnp.maximum(j - 1, 0)

    return pl.pallas_call(
        functools.partial(backward_early_kernel, len(cots), parts),
        grid_spec=pltpu.PrefetchScalarGridSpec(
            num_scalar_prefetch=1,
            grid=(1 + ff // width,),
            in_specs=[in_place] * len(cots)
            + [
                whole(wo),
                pl.BlockSpec((pieces, width, piece), lambda j, w: (0, tile(j), 0)),
                pl.BlockSpec((count, width), lambda j, w: (0, tile(j))),
            ],
            out_specs=[
                in_place,
                pl.BlockSpec((count, width), lambda j, w: (0, 0)),
                pl.BlockSpec((count, width), lambda j, w: (0, tile(j))),
            ],
            scratch_shapes=[
                pltpu.VMEM((count, depth), BF16),
                pltpu.SemaphoreType.DMA((len(cots),)),
                pltpu.SemaphoreType.DMA((len(cots),)),
            ],
        ),
        out_shape=[jax.ShapeDtypeStruct(s, BF16) for s in ((total, depth), (total, width), (total, ff))],
        cost_estimate=cost(2 * count * depth * (width + ff), 2 * depth * (width + ff)),
        name="backward_early",
    )(where, *cots, wo, wd, slope)


def low_lanes(rows):
    return lax.broadcasted_iota(jnp.int32, (rows, 128), 1) < HD


def attend_kernel(
    skipped, first_ref, q_ref, k_ref, v_ref, segc_ref, segr_ref, *refs
):
    o_ref, lse_ref, max_ref, acc_ref, bias_ref = refs[-5:]
    i = pl.program_id(0) + skipped
    block, width = q_ref.shape
    pairs = width // 128
    low = low_lanes(block)
    owns = (low, jnp.logical_not(low))
    max_ref[...] = jnp.full_like(max_ref, NEGATIVE)
    lse_ref[...] = jnp.zeros_like(lse_ref)
    acc_ref[...] = jnp.zeros_like(acc_ref)
    q0 = pl.multiple_of(i * block, block)
    query_seg = segr_ref[:, pl.ds(q0, block)]
    query_row = q0 + lax.broadcasted_iota(jnp.int32, (1, block), 1)

    def set_bias(k0):
        key_seg = segc_ref[pl.ds(k0, block), :]
        key_row = k0 + lax.broadcasted_iota(jnp.int32, (block, 1), 0)
        bias_ref[...] = jnp.where((key_seg == query_seg) & (key_row <= query_row), 0.0, NEGATIVE)

    def scores(k0, p, h):
        lanes = slice(p * 128, (p + 1) * 128)
        q = q_ref[:, lanes]
        mine = jnp.where(owns[h], q, jnp.zeros_like(q))
        return dot_nt(k_ref[pl.ds(k0, block), lanes], mine) + bias_ref[...]

    def find_max(j, carry):
        k0 = pl.multiple_of(j * block, block)
        set_bias(k0)
        for p in range(pairs):
            for h in range(2):
                s = scores(k0, p, h)
                max_ref[2 * p + h] = jnp.maximum(max_ref[2 * p + h], jnp.max(s, axis=0, keepdims=True))
        return carry

    lax.fori_loop(first_ref[i], i + 1, find_max, 0)

    def add_up(j, carry):
        k0 = pl.multiple_of(j * block, block)
        set_bias(k0)
        for p in range(pairs):
            v = v_ref[pl.ds(k0, block), p * 128 : (p + 1) * 128]
            for h in range(2):
                e = jnp.exp(scores(k0, p, h) - max_ref[2 * p + h])
                lse_ref[p, h : h + 1, :] += jnp.sum(e, axis=0, keepdims=True)
                acc_ref[2 * p + h] += dot_tn(e.astype(BF16), jnp.where(owns[h], v, jnp.ones_like(v)))
        return carry

    lax.fori_loop(first_ref[i], i + 1, add_up, 0)
    for p in range(pairs):
        even, odd = acc_ref[2 * p], acc_ref[2 * p + 1]
        o_ref[:, p * 128 : (p + 1) * 128] = jnp.where(
            low, even / pltpu.roll(even, HD, axis=1), odd / pltpu.roll(odd, HD, axis=1)
        ).astype(BF16)
        for h in range(2):
            lse_ref[p, h : h + 1, :] = max_ref[2 * p + h] + jnp.log(lse_ref[p, h : h + 1, :])


def attend(qkv, segc, segr, first, part, parts, bufs):
    count = segr.shape[1]
    width = qkv.shape[1] // 3
    pairs = width // 128
    steps = count // BLOCK // parts
    skipped = part * steps
    in_place = [] if bufs is None else [pl.BlockSpec(memory_space=pl.ANY)] * 2
    return pl.pallas_call(
        functools.partial(attend_kernel, skipped),
        grid_spec=pltpu.PrefetchScalarGridSpec(
            num_scalar_prefetch=1,
            grid=(steps,),
            in_specs=[
                pl.BlockSpec((BLOCK, width), lambda i, f: (i + skipped, 0)),
                pl.BlockSpec((count, width), lambda i, f: (0, 1)),
                pl.BlockSpec((count, width), lambda i, f: (0, 2)),
                whole(segc),
                whole(segr),
            ]
            + in_place,
            out_specs=[
                pl.BlockSpec((BLOCK, width), lambda i, f: (i + skipped, 0)),
                pl.BlockSpec((pairs, 8, BLOCK), lambda i, f: (0, 0, i + skipped)),
            ],
            scratch_shapes=[
                pltpu.VMEM((2 * pairs, 1, BLOCK), F32),
                pltpu.VMEM((2 * pairs, BLOCK, 128), F32),
                pltpu.VMEM((BLOCK, BLOCK), F32),
            ],
        ),
        out_shape=[
            jax.ShapeDtypeStruct((count, width), BF16),
            jax.ShapeDtypeStruct((pairs, 8, count), F32),
        ],
        input_output_aliases={} if bufs is None else {6: 0, 7: 1},
        cost_estimate=cost(30e9 * width / 512, count * width * 8),
        name="attend",
    )(first, qkv, qkv, qkv, segc, segr, *([] if bufs is None else bufs))


def attend_back_kernel(
    first_ref, q_ref, k_ref, v_ref, go_ref, o_ref, lse_ref, segc_ref, segr_ref,
    cos_ref, up_ref, down_ref, *refs,
):
    gq_ref, gk_ref, gv_ref, dq_ref, dk_ref, dv_ref, bias_ref = refs[-7:]
    i = pl.program_id(0)
    steps = pl.num_programs(0)
    block, width = q_ref.shape
    pairs = width // 128
    low = low_lanes(block)
    owns = (low, jnp.logical_not(low))

    @pl.when(i == 0)
    def _():
        dk_ref[...] = jnp.zeros_like(dk_ref)
        dv_ref[...] = jnp.zeros_like(dv_ref)

    dq_ref[...] = jnp.zeros_like(dq_ref)
    q0 = pl.multiple_of(i * block, block)
    query_seg = segr_ref[:, pl.ds(q0, block)]
    query_row = q0 + lax.broadcasted_iota(jnp.int32, (1, block), 1)
    half = jnp.where(
        lax.broadcasted_iota(jnp.int32, (8, 128), 1) // HD == lax.broadcasted_iota(jnp.int32, (8, 128), 0),
        1.0,
        0.0,
    ).astype(F32)
    inner = []
    for p in range(pairs):
        lanes = slice(p * 128, (p + 1) * 128)
        product = go_ref[:, lanes].astype(F32) * o_ref[:, lanes].astype(F32)
        inner.append(
            lax.dot_general(
                half, product, (((1,), (1,)), ((), ())),
                precision=lax.Precision.HIGHEST, preferred_element_type=F32,
            )
        )

    def body(j, carry):
        k0 = pl.multiple_of(j * block, block)
        key_seg = segc_ref[pl.ds(k0, block), :]
        key_row = k0 + lax.broadcasted_iota(jnp.int32, (block, 1), 0)
        bias_ref[...] = jnp.where((key_seg == query_seg) & (key_row <= query_row), 0.0, NEGATIVE)
        for p in range(pairs):
            lanes = slice(p * 128, (p + 1) * 128)
            k = k_ref[pl.ds(k0, block), lanes]
            v = v_ref[pl.ds(k0, block), lanes]
            q = q_ref[:, lanes]
            go = go_ref[:, lanes]
            sums = None
            for h in range(2):
                q_own, go_own, k_own = [jnp.where(owns[h], a, jnp.zeros_like(a)) for a in (q, go, k)]
                prob = jnp.exp(dot_nt(k, q_own) + bias_ref[...] - lse_ref[p, h : h + 1, :])
                grad_score = (prob * (dot_nt(v, go_own) - inner[p][h : h + 1, :])).astype(BF16)
                new = (
                    dot_nn(prob.astype(BF16), go_own),
                    dot_nn(grad_score, q_own),
                    dot_tn(grad_score, k_own),
                )
                sums = new if sums is None else tuple(a + b for a, b in zip(sums, new))
            dv_ref[pl.ds(k0, block), lanes] += sums[0]
            dk_ref[pl.ds(k0, block), lanes] += sums[1]
            dq_ref[:, lanes] += sums[2]
        return carry

    lax.fori_loop(first_ref[i], i + 1, body, 0)
    turn = [r[pl.ds(q0, block), :] for r in (cos_ref, up_ref, down_ref)]
    for p in range(pairs):
        lanes = slice(p * 128, (p + 1) * 128)
        gq_ref[:, lanes] = unrotate(dq_ref[:, lanes] * HD**-0.5, *turn).astype(BF16)

    @pl.when(i == steps - 1)
    def _():
        def finish(j, carry):
            k0 = pl.multiple_of(j * block, block)
            rows = pl.ds(k0, block)
            turn = [r[rows, :] for r in (cos_ref, up_ref, down_ref)]
            for p in range(pairs):
                lanes = slice(p * 128, (p + 1) * 128)
                gk_ref[rows, lanes] = unrotate(dk_ref[rows, lanes], *turn).astype(BF16)
                gv_ref[rows, lanes] = dv_ref[rows, lanes].astype(BF16)
            return carry

        lax.fori_loop(0, steps, finish, 0)


def attend_back(qkv, grad_out, out, lse, segc, segr, first, tables, part, parts, bufs):
    count = segr.shape[1]
    whole_width = qkv.shape[1] // 3
    width = whole_width // parts
    pairs = width // 128
    row_tile = pl.BlockSpec((BLOCK, width), lambda i, f: (i, part))
    column = pl.BlockSpec((count, width), lambda i, f: (0, part))
    in_place = [] if bufs is None else [pl.BlockSpec(memory_space=pl.ANY)] * 3
    args = [first, qkv, qkv, qkv, grad_out, out, lse, segc, segr, *tables]
    return pl.pallas_call(
        attend_back_kernel,
        grid_spec=pltpu.PrefetchScalarGridSpec(
            num_scalar_prefetch=1,
            grid=(count // BLOCK,),
            in_specs=[
                row_tile,
                pl.BlockSpec((count, width), lambda i, f: (0, parts + part)),
                pl.BlockSpec((count, width), lambda i, f: (0, 2 * parts + part)),
                row_tile,
                row_tile,
                pl.BlockSpec((pairs, 8, BLOCK), lambda i, f: (part, 0, i)),
                whole(segc),
                whole(segr),
                *[whole(t) for t in tables],
            ]
            + in_place,
            out_specs=[row_tile, column, column],
            scratch_shapes=[
                pltpu.VMEM((BLOCK, width), F32),
                pltpu.VMEM((count, width), F32),
                pltpu.VMEM((count, width), F32),
                pltpu.VMEM((BLOCK, BLOCK), F32),
            ],
        ),
        out_shape=[jax.ShapeDtypeStruct((count, whole_width), BF16)] * 3,
        input_output_aliases={} if bufs is None else {len(args) + k: k for k in range(3)},
        cost_estimate=cost(44e9 * width / 512, count * width * 20),
        name="attend_back",
    )(*args, *([] if bufs is None else bufs))


def side_by_side(ref):
    return jnp.concatenate([ref[b] for b in range(ref.shape[0])], axis=1)


def mix_kernel(att_ref, act_ref, wo_ref, wd_ref, o_ref):
    wo, wd = side_by_side(wo_ref), side_by_side(wd_ref)
    step = min(512, att_ref.shape[0])
    for m in range(0, att_ref.shape[0], step):
        rs = slice(m, m + step)
        o_ref[rs, :] = (dot_nn(att_ref[rs, :], wo) + dot_nn(act_ref[rs, :], wd)).astype(BF16)


def mix(att, act, wo, wd):
    pieces, width, piece = wo.shape
    ff = wd.shape[1]
    count = att.shape[0]
    group = max(1, 512 // piece)
    return pl.pallas_call(
        mix_kernel,
        grid=(pieces // group,),
        in_specs=[
            pl.BlockSpec((count, width), lambda j: (0, 0)),
            pl.BlockSpec((count, ff), lambda j: (0, 0)),
            pl.BlockSpec((group, width, piece), lambda j: (j, 0, 0)),
            pl.BlockSpec((group, ff, piece), lambda j: (j, 0, 0)),
        ],
        out_specs=pl.BlockSpec((count, group * piece), lambda j: (0, j)),
        out_shape=jax.ShapeDtypeStruct((count, pieces * piece), BF16),
        cost_estimate=cost(2 * count * (width + ff) * pieces * piece, 4 * count * ff),
        name="mix",
    )(att, act, wo, wd)


def mixed_kernel(x_ref, sum_ref, bias_ref, o_ref):
    o_ref[...] = (x_ref[...].astype(F32) + sum_ref[...].astype(F32) + bias_ref[...]).astype(BF16)


def mixed_out(x, total, bias):
    rows, width = x.shape
    step = min(256, rows)
    tile = pl.BlockSpec((step, width), lambda i: (i, 0))
    return pl.pallas_call(
        mixed_kernel,
        grid=(rows // step,),
        in_specs=[tile, tile, pl.BlockSpec((1, width), lambda i: (0, 0))],
        out_specs=tile,
        out_shape=jax.ShapeDtypeStruct(x.shape, BF16),
        cost_estimate=cost(rows * width * 4, rows * width * 6),
        name="mixed_out",
    )(x, total, bias)


def backward_kernel(came, tiles, where_ref, *refs):
    c_refs, refs = refs[:came], refs[came:]
    wo_ref, wd_ref, slope_ref = refs[:3]
    cot_ref, ga_ref, gh_ref = refs[-3:]
    i = pl.program_id(0)
    j, _, busy = pick(where_ref, i, tiles)
    rows = cot_ref.shape[0]
    step = min(ROWS, rows)

    @pl.when(busy & (j == 0))
    def _():
        pick_shard(where_ref, i, tiles, c_refs, cot_ref)
        weight = side_by_side(wo_ref)
        for m in range(0, rows, step):
            ga_ref[m : m + step, :] = dot_nt(cot_ref[m : m + step, :], weight).astype(BF16)

    @pl.when(busy & (j > 0))
    def _():
        weight = side_by_side(wd_ref)
        for m in range(0, rows, step):
            gh_ref[m : m + step, :] = (
                dot_nt(cot_ref[m : m + step, :], weight) * slope_ref[m : m + step, :].astype(F32)
            ).astype(BF16)


def backward_chunk(where, cots, wo, wd, slope, bufs, parts):
    rows, depth = cots[0].shape
    pieces, width, piece = wo.shape
    ff = wd.shape[1]
    tiles = 1 + ff // width

    def at(k):
        def index(i, w):
            j, slot, _ = pick(w, i, tiles)
            return ((0, 0), (0, jnp.maximum(j - 1, 0), 0), (slot, jnp.maximum(j - 1, 0)), (slot, 0))[k]

        return index

    in_specs = [pl.BlockSpec((rows, depth), at(0))] * len(cots) + [
        whole(wo),
        pl.BlockSpec((pieces, width, piece), at(1)),
        pl.BlockSpec((rows, width), at(2)),
    ]
    total = (parts + 1) * rows
    shapes = [(total, depth), (total, width), (total, ff)]
    args = [where, *cots, wo, wd, slope]
    aliases = {}
    if bufs is not None:
        aliases = {len(args) + k: k for k in range(3)}
        args += list(bufs)
        in_specs += [pl.BlockSpec(memory_space=pl.ANY)] * 3
    return pl.pallas_call(
        functools.partial(backward_kernel, len(cots), tiles),
        grid_spec=pltpu.PrefetchScalarGridSpec(
            num_scalar_prefetch=1,
            grid=(len(cots) * tiles,),
            in_specs=in_specs,
            out_specs=[
                pl.BlockSpec((rows, depth), at(3)),
                pl.BlockSpec((rows, width), at(3)),
                pl.BlockSpec((rows, width), at(2)),
            ],
        ),
        out_shape=[jax.ShapeDtypeStruct(s, BF16) for s in shapes],
        input_output_aliases=aliases,
        cost_estimate=cost(2 * rows * depth * (width + ff), 2 * depth * (width + ff)),
        name="backward_chunk",
    )(*args)


def grad_kernel(gq_ref, gk_ref, gv_ref, gh_ref, wq_ref, wu_ref, o_ref):
    step = min(512, gq_ref.shape[0])
    width = gq_ref.shape[1]
    for m in range(0, gq_ref.shape[0], step):
        rs = slice(m, m + step)
        left = jnp.concatenate([r[rs, :] for r in (gq_ref, gk_ref, gv_ref)], axis=1)
        o_ref[rs, :] = (dot_nt(left, wq_ref[...]) + dot_nt(gh_ref[rs, :], wu_ref[...])).astype(BF16)


def grad_normed(gqkv, gh, wq, wu, start, stop):
    count, width = gqkv[0].shape
    ff = gh.shape[1]
    tile = min(256, stop - start)
    first = start // tile
    return pl.pallas_call(
        grad_kernel,
        grid=((stop - start) // tile,),
        in_specs=[once((count, width))] * 3
        + [
            once((count, ff)),
            pl.BlockSpec((tile, wq.shape[1]), lambda j: (first + j, 0)),
            pl.BlockSpec((tile, wu.shape[1]), lambda j: (first + j, 0)),
        ],
        out_specs=pl.BlockSpec((count, tile), lambda j: (0, j)),
        out_shape=jax.ShapeDtypeStruct((count, stop - start), BF16),
        cost_estimate=cost(2 * count * (stop - start) * (3 * width + ff), 4 * count * ff),
        name="grad_normed",
    )(*gqkv, gh, wq, wu)


def put_columns(att_ref, act_ref, cot, o_ref, start, stop, add):
    width = att_ref.shape[1]
    at = start
    while at < stop:
        if at < width:
            end = min(stop, width)
            left = att_ref[:, at:end]
        else:
            end = min(stop, at + 512)
            left = act_ref[:, at - width : end - width]
        rows = slice(at - start, end - start)
        total = dot_tn(left, cot)
        if add is not None:
            total = total + add[0, rows, :].astype(F32)
        o_ref[0, rows, :] = total.astype(BF16)
        at = end


def columns_send_kernel(where_ref, att_ref, act_ref, c_ref, o_ref):
    put_columns(att_ref, act_ref, c_ref[...], o_ref, 0, o_ref.shape[1], None)


def columns_keep_kernel(where_ref, att_ref, act_ref, c_ref, came_ref, a_ref, b_ref):
    half = a_ref.shape[1]
    first = pl.program_id(0) < pl.num_programs(0) // 2

    @pl.when(first)
    def _():
        put_columns(att_ref, act_ref, c_ref[...], a_ref, 0, half, came_ref)

    @pl.when(jnp.logical_not(first))
    def _():
        put_columns(att_ref, act_ref, c_ref[...], b_ref, half, 2 * half, came_ref)


def rows_send_kernel(arrays, where_ref, x_ref, *refs):
    g_refs, o_ref, sum_ref = refs[:arrays], refs[-2], refs[-1]
    x = x_ref[...]
    first = pl.program_id(0) == 0
    start = 0
    for g_ref in g_refs:
        width = g_ref.shape[1]
        step = min(512, width)
        for m in range(0, width, step):
            o_ref[0, :, start + m : start + m + step] = dot_tn(x, g_ref[:, m : m + step]).astype(BF16)

        @pl.when(first)
        def _():
            ones = jnp.ones((8, g_ref.shape[0]), BF16)
            for m in range(0, width, step):
                sum_ref[:, start + m : start + m + step] = dot_nn(ones, g_ref[:, m : m + step])

        start += width


def rows_keep_kernel(arrays, where_ref, x_ref, *refs):
    g_refs, came_ref, a_ref, b_ref = refs[:arrays], *refs[arrays:]
    first = pl.program_id(0) < pl.num_programs(0) // 2
    x = x_ref[...]
    half = a_ref.shape[2]

    def put(o_ref, low):
        start = 0
        for g_ref in g_refs:
            width = g_ref.shape[1]
            at = max(start, low)
            while at < min(start + width, low + half):
                end = min(start + width, low + half, at + 512)
                o_ref[0, :, at - low : end - low] = (
                    dot_tn(x, g_ref[:, at - start : end - start])
                    + came_ref[0, :, at - low : end - low].astype(F32)
                ).astype(BF16)
                at = end
            start += width

    pl.when(first)(lambda: put(a_ref, 0))
    pl.when(jnp.logical_not(first))(lambda: put(b_ref, half))


def once(shape):
    return pl.BlockSpec(shape, lambda *_: (0,) * len(shape), pipeline_mode=pl.Buffered(1))


def column_grads(where, att, act, cot, places, came=None):
    count, width = att.shape
    ff = act.shape[1]
    piece = cot.shape[1] // (2 * places)
    flops = 2 * count * (width + ff) * piece * places
    base = [once((count, width)), once((count, ff)), pl.BlockSpec((count, piece), lambda t, w: (0, w[t]))]
    if came is None:
        return pl.pallas_call(
            columns_send_kernel,
            grid_spec=pltpu.PrefetchScalarGridSpec(
                num_scalar_prefetch=1,
                grid=(places,),
                in_specs=base,
                out_specs=pl.BlockSpec((1, width + ff, piece), lambda t, w: (t, 0, 0)),
            ),
            out_shape=jax.ShapeDtypeStruct((places, width + ff, piece), BF16),
            cost_estimate=cost(flops, 2 * count * (width + ff)),
            name="columns_send",
        )(where, att, act, cot)
    half = (width + ff) // 2
    turns = 2 * places
    return pl.pallas_call(
        columns_keep_kernel,
        grid_spec=pltpu.PrefetchScalarGridSpec(
            num_scalar_prefetch=1,
            grid=(turns,),
            in_specs=base
            + [pl.BlockSpec((1, half, piece), lambda t, w: (w[turns + t], t // places, 0))],
            out_specs=[
                pl.BlockSpec((1, half, piece), lambda t, w: (jnp.minimum(t, places - 1), 0, 0)),
                pl.BlockSpec((1, half, piece), lambda t, w: (jnp.maximum(t - places, 0), 0, 0)),
            ],
        ),
        out_shape=[jax.ShapeDtypeStruct((places, half, piece), BF16)] * 2,
        cost_estimate=cost(flops, 2 * count * (width + ff)),
        name="columns_keep",
    )(where, att, act, cot, came)


def row_grads(where, x, gs, count, places, came=None):
    width = sum(g.shape[1] for g in gs)
    piece = x.shape[1] // (2 * places)
    flops = 2 * count * width * piece * places
    base = [pl.BlockSpec((count, piece), lambda t, w: (0, w[t]))] + [once((count, g.shape[1])) for g in gs]
    if came is None:
        return pl.pallas_call(
            functools.partial(rows_send_kernel, len(gs)),
            grid_spec=pltpu.PrefetchScalarGridSpec(
                num_scalar_prefetch=1,
                grid=(places,),
                in_specs=base,
                out_specs=[
                    pl.BlockSpec((1, piece, width), lambda t, w: (t, 0, 0)),
                    pl.BlockSpec((8, width), lambda t, w: (0, 0)),
                ],
            ),
            out_shape=[
                jax.ShapeDtypeStruct((places, piece, width), BF16),
                jax.ShapeDtypeStruct((8, width), F32),
            ],
            cost_estimate=cost(flops, 2 * count * width),
            name="rows_send",
        )(where, x, *gs)
    half = width // 2
    turns = 2 * places
    return pl.pallas_call(
        functools.partial(rows_keep_kernel, len(gs)),
        grid_spec=pltpu.PrefetchScalarGridSpec(
            num_scalar_prefetch=1,
            grid=(turns,),
            in_specs=base
            + [pl.BlockSpec((1, piece, half), lambda t, w: (w[turns + t], 0, t // places))],
            out_specs=[
                pl.BlockSpec((1, piece, half), lambda t, w: (jnp.minimum(t, places - 1), 0, 0)),
                pl.BlockSpec((1, piece, half), lambda t, w: (jnp.maximum(t - places, 0), 0, 0)),
            ],
        ),
        out_shape=[jax.ShapeDtypeStruct((places, piece, half), BF16)] * 2,
        cost_estimate=cost(flops, 2 * count * width),
        name="rows_keep",
    )(where, x, *gs, came)


def after(value, *marks):
    return lax.optimization_barrier((value, *marks))[0]


def swap(x, bit):
    size = lax.axis_size("dp")
    return lax.ppermute(x, "dp", [(i, i ^ (1 << bit)) for i in range(size)])


def halve(xs, orders, k, sent=None):
    kept = []
    for x, y, bits in zip(xs, sent or xs, orders):
        rest = x.shape[0] // 2
        came = swap(y[rest:], bits[k])
        total = x[:rest].astype(F32) + came.astype(F32)
        kept.append(total if k == len(bits) - 1 else total.astype(BF16))
    return kept


def small_sum_kernel(phases, x_ref, o_ref, sent_ref, came_ref, send_sems, came_sems):
    barrier = pltpu.get_barrier_semaphore()

    def partner(axis, bit):
        return {axis: lax.axis_index(axis) ^ (1 << bit)}

    for axis, bit, _ in phases:
        pl.semaphore_signal(
            barrier, inc=1, device_id=partner(axis, bit), device_id_type=pl.DeviceIdType.MESH
        )
    pl.semaphore_wait(barrier, len(phases))
    sent_ref[0] = x_ref[...]
    for k, (axis, bit, rows) in enumerate(phases):
        span = pl.ds(0, rows)
        copy = pltpu.make_async_remote_copy(
            src_ref=sent_ref.at[k, span],
            dst_ref=came_ref.at[k, span],
            send_sem=send_sems.at[k],
            recv_sem=came_sems.at[k],
            device_id=partner(axis, bit),
            device_id_type=pl.DeviceIdType.MESH,
        )
        copy.start()
        copy.wait()
        total = sent_ref[k, 0:rows] + came_ref[k, 0:rows]
        if k == len(phases) - 1:
            o_ref[...] = sent_ref[k]
            o_ref[0:rows] = total
        else:
            sent_ref[k + 1] = sent_ref[k]
            sent_ref[k + 1, 0:rows] = total


def small_sums(x, common):
    rows = x.shape[0]
    phases = []
    for axis, height in (("dp", rows), ("tensor", common)):
        for bit in range(lax.axis_size(axis).bit_length() - 1):
            phases.append((axis, bit, height))
    return pl.pallas_call(
        functools.partial(small_sum_kernel, phases),
        in_specs=[pl.BlockSpec(memory_space=pltpu.VMEM)],
        out_specs=pl.BlockSpec(memory_space=pltpu.VMEM),
        out_shape=jax.ShapeDtypeStruct(x.shape, F32),
        scratch_shapes=[
            pltpu.VMEM((len(phases), *x.shape), F32),
            pltpu.VMEM((len(phases), *x.shape), F32),
            pltpu.SemaphoreType.DMA((len(phases),)),
            pltpu.SemaphoreType.DMA((len(phases),)),
        ],
        compiler_params=pltpu.CompilerParams(collective_id=0, has_side_effects=True),
        name="small_sums",
    )(x)


def local(
    tokens, segments, ln_gain, ln_shift, qkv_weight, qkv_bias, out_weight, out_bias,
    fc1_weight, fc1_bias, fc2_weight, fc2_bias, cotangent,
):
    n = lax.axis_size("tensor")
    pieces = lax.axis_size("dp")
    me = lax.axis_index("tensor")
    rows, depth = tokens.shape
    count = segments.shape[1]
    width = qkv_weight.shape[2]

    def shift(x, pairs):
        return lax.ppermute(x, "tensor", pairs)

    def turns(step):
        left, right = me - step, me + step
        has_left, has_right = left >= 0, right < n
        one = jnp.where(has_left, left, right)
        last = jnp.where(has_right, right, jnp.where(has_left, left, n))
        busy = has_left.astype(jnp.int32) + has_right.astype(jnp.int32)
        values = [one, jnp.where(has_left, 0, 1), right, 1, busy, last]
        return jnp.stack([jnp.asarray(v, jnp.int32) for v in values])

    def places_of(shards, present):
        shards, present = jnp.stack(shards), jnp.stack(present)
        order = jnp.sort(jnp.where(present, shards, n))
        order = jnp.concatenate([order, jnp.full((n,), n, order.dtype)])[:n]
        return jnp.concatenate(
            [
                jnp.sum(present.astype(jnp.int32))[None],
                order,
                jnp.stack([jnp.clip(shards, 0, n - 1), present.astype(jnp.int32)], axis=1).reshape(-1),
            ]
        ).astype(jnp.int32)

    def present_shards(steps):
        shards = [me] + [me + d * s for s in range(1, steps + 1) for d in (-1, 1)]
        return places_of(shards, [(x >= 0) & (x < n) for x in shards])

    early = present_shards(n - 2)
    late = turns(n - 1)

    own_normed = norm(tokens, ln_gain[None], ln_shift[None])

    w_qkv = lax.all_gather(qkv_weight.reshape(-1, 3 * width), "dp", axis=0, tiled=True)
    w_up = lax.all_gather(fc1_weight, "dp", axis=0, tiled=True)
    w_out = lax.all_gather(out_weight, "dp", axis=0)
    w_down = lax.all_gather(fc2_weight, "dp", axis=0)

    segment_row = segments[0]
    starts = seq_starts(segment_row)
    tables = rotary_tables(jnp.arange(count, dtype=jnp.int32) - starts)
    first = starts[::BLOCK] // BLOCK
    segc, segr = segment_row[:, None], segment_row[None, :]

    bias_qkv, bias_up = qkv_bias.reshape(1, -1), fc1_bias[None]
    def line_step(pair, s):
        right, left = pair
        return [
            shift(right, [(i, i + 1) for i in range(s - 1, n - 1)]),
            shift(left, [(i, i - 1) for i in range(1, n - s + 1)]),
        ]

    def line_sum(x):
        return lax.psum_scatter(x, "tensor", scatter_dimension=0, tiled=True)

    def flat(pairs):
        return [x for pair in pairs for x in pair]

    project = (w_qkv, w_up, bias_qkv, bias_up, tables)
    normed_in = [line_step([own_normed] * 2, 1)]
    normed, qkv = queries_early(
        after(present_shards(1), first, segc), [own_normed] + normed_in[0], w_qkv, bias_qkv, tables, n
    )
    early_qkv = qkv
    for s in range(2, n):
        normed_in.append(line_step(after(tuple(normed_in[-1]), qkv) if s == 3 else normed_in[-1], s))
    for s in range(2, n - 1):
        normed, qkv = queries_chunk(turns(s), normed_in[s - 1], w_qkv, bias_qkv, tables, (normed, qkv), n)
    act, slope = units_early(
        after(early, qkv), [own_normed] + flat(normed_in[:-1]), w_up, bias_up, width, n
    )
    def inner_step(pair, s):
        right, left = pair
        return [
            shift(right, [(i, i + 1) for i in range(s - 1, n - 2)]),
            shift(left, [(i, i - 1) for i in range(2, n - s + 1)]),
        ]

    def end_step(pair):
        right, left = pair
        return [shift(right, [(n - 2, n - 1)]), shift(left, [(1, 0)])]

    inner = [inner_step([after(cotangent, *normed_in[-2], early_qkv)] * 2, 1)]
    ready = after(tuple(inner[0]), *normed_in[-1], act)
    ends = [end_step([after(cotangent, *ready)] * 2)]
    inner.append(inner_step(ready, 2))
    cot_from, cot_shards, cot_there = [cotangent], [me], [me >= 0]
    normed, qkv, act, slope = forward_chunk(late, normed_in[-1], *project, (normed, qkv, act, slope), n)

    att_half = attend(qkv, segc, segr, first, 0, 2, None)
    ends.append(end_step(after(tuple(ready), *ends[0], *inner[1], att_half[0])))
    att, lse = attend(qkv, segc, segr, first, 1, 2, att_half)
    for s in range(3, n):
        ready = after(tuple(inner[-1]), att)
        ends.append(end_step(ready))
        if s < n - 1:
            inner.append(inner_step(ready, s))
    for s in range(1, n - 1):
        for direction in range(2):
            at_end = me == (n - 1, 0)[direction]
            shard = me + (-s, s)[direction]
            cot_from += [inner[s - 1][direction], ends[s - 1][direction]]
            cot_shards += [shard, shard]
            cot_there += [(shard >= 0) & (shard < n) & jnp.logical_not(at_end), at_end]
    part = mix(att, act, w_out, w_down)
    bufs = backward_early(after(places_of(cot_shards, cot_there), part), cot_from, w_out, w_down, slope, n)
    block_sum = line_sum(after(part, bufs[2], *ends[-1]))
    cot, grad_att, grad_hid = backward_chunk(late, ends[-1], w_out, w_down, slope, bufs, n)
    bits = [b for b in range(1, pieces.bit_length() - 1)]
    places = pieces // 2
    mine = lax.axis_index("dp")

    def place_of(r, order):
        return sum(((r >> (len(order) - 1 - k)) & 1) << bit for k, bit in enumerate(order))

    kept = [place_of(r, bits) for r in range(places)] + [place_of(r, bits[::-1]) for r in range(places)]
    send_where = mine ^ jnp.array([2 * q + 1 for q in range(places)], jnp.int32)
    keep_where = jnp.concatenate([mine ^ jnp.array(kept, jnp.int32), jnp.array(kept, jnp.int32) // 2])

    orders = (bits, bits[::-1])

    def finish(pair, axis, *marks):
        for k in range(1, len(bits)):
            pair = halve([after(half, *marks) for half in pair], orders, k, pair)
        return jnp.concatenate([half[0].astype(F32) for half in pair], axis=axis)

    col_send = column_grads(send_where, att, act, cot, places)
    up_send, up_sum = row_grads(send_where, normed, [after(grad_hid, col_send)], count, places)
    grad_qkv = attend_back(
        qkv, after(grad_att, up_sum), att, lse, segc, segr, first, tables, 0, 1, None
    )
    col_came, up_came = swap(col_send, 0), swap(up_send, 0)
    part = grad_normed(grad_qkv, after(grad_hid, col_came, up_came), w_qkv, w_up, 0, depth)
    grad_sum = line_sum(after(part, block_sum))
    col_pair = column_grads(keep_where, att, act, after(cot, part), places, col_came)
    qkv_send, qkv_sum = row_grads(send_where, normed, after(tuple(grad_qkv), col_pair[0]), count, places)
    up_pair = row_grads(
        keep_where, normed, [after(grad_hid, qkv_sum)], count, places, up_came
    )
    col_pair = halve([after(c, up_pair[0]) for c in col_pair], orders, 0, col_pair)
    qkv_pair = row_grads(
        keep_where, after(normed, *col_pair), grad_qkv, count, places, swap(qkv_send, 0)
    )
    up_pair = halve([after(u, qkv_pair[0]) for u in up_pair], orders, 0, up_pair)
    qkv_kept = qkv_pair[0]
    qkv_pair = halve(qkv_pair, orders, 0)
    mixed = mixed_out(tokens, after(block_sum, *qkv_pair), (out_bias + fc2_bias)[None])
    input_grad, sums = norm_back(tokens, after(cotangent, mixed), [grad_sum], ln_gain[None])
    common = 3 * depth // 128
    pack = jnp.concatenate([a.reshape(-1, 128) for a in (sums[:3], up_sum[0], qkv_sum[0])])
    pack = jnp.pad(pack, ((0, -pack.shape[0] % 8), (0, 0)))
    pack = small_sums(pack, common)
    col_out, up_out, qkv_out = finish(col_pair, 0, qkv_kept), finish(up_pair, 1, *qkv_pair), finish(qkv_pair, 1)
    total = pack[:common].reshape(3, depth)
    ff_rows = up_sum.shape[1] // 128
    up_bias_grad = pack[common : common + ff_rows].reshape(-1)
    qkv_bias_grad = pack[common + ff_rows : common + ff_rows + 3 * width // 128].reshape(3, width)
    return (
        mixed,
        input_grad,
        qkv_out.reshape(-1, 3, width),
        qkv_bias_grad,
        col_out[:width],
        total[2],
        up_out,
        up_bias_grad,
        col_out[width:],
        total[2],
        total[0],
        total[1],
    )


def solution(mesh):
    in_specs = (
        P(("dp", "tensor"), None),
        P("dp", None),
        P(),
        P(),
        P("dp", None, "tensor"),
        P(None, "tensor"),
        P("tensor", "dp"),
        P(),
        P("dp", "tensor"),
        P("tensor"),
        P("tensor", "dp"),
        P(),
        P(("dp", "tensor"), None),
    )
    out_specs = (
        P(("dp", "tensor"), None),
        P(("dp", "tensor"), None),
        P("dp", None, "tensor"),
        P(None, "tensor"),
        P("tensor", "dp"),
        P(),
        P("dp", "tensor"),
        P("tensor"),
        P("tensor", "dp"),
        P(),
        P(),
        P(),
    )
    return jax.shard_map(local, mesh=mesh, in_specs=in_specs, out_specs=out_specs, check_vma=False)
```

```python
import functools

import jax
import jax.numpy as jnp
from jax import lax
from jax.experimental import pallas as pl
from jax.experimental.pallas import tpu as pltpu
from jax.sharding import PartitionSpec as P

HD = 64
ROT = 32
EPS = 1e-05
ROPE_BASE = 10000.0
NEGATIVE = -1e30
BLOCK = 256
ROWS = 256
SHRINK = 20

F32 = jnp.float32
BF16 = jnp.bfloat16


def dot_nn(a, b):
    return lax.dot_general(a, b, (((1,), (0,)), ((), ())), preferred_element_type=F32)


def dot_nt(a, b):
    return lax.dot_general(a, b, (((1,), (1,)), ((), ())), preferred_element_type=F32)


def dot_tn(a, b):
    return lax.dot_general(a, b, (((0,), (0,)), ((), ())), preferred_element_type=F32)


def cost(flops, moved, trans=0):
    return pl.CostEstimate(flops=int(flops / SHRINK), bytes_accessed=int(moved / SHRINK), transcendentals=0)


def whole(a):
    return pl.BlockSpec(a.shape, lambda *_: (0,) * a.ndim)


def seq_starts(segment_row):
    count = segment_row.shape[0]
    index = jnp.arange(count, dtype=jnp.int32)
    begins = jnp.concatenate([jnp.ones((1,), dtype=bool), segment_row[1:] != segment_row[:-1]])
    return lax.cummax(jnp.where(begins, index, jnp.zeros_like(index)), axis=0)


def rotary_tables(positions):
    half = ROT // 2
    lane = jnp.arange(128, dtype=jnp.int32) % HD
    frequency = ROPE_BASE ** (-((lane % half).astype(F32) * 2.0) / ROT)
    angles = positions.astype(F32)[:, None] * frequency[None, :]
    cosine = jnp.where(lane < ROT, jnp.cos(angles), 1.0)
    sine = jnp.sin(angles)
    sine_up = jnp.where(lane < half, -sine, 0.0)
    sine_down = jnp.where((lane >= half) & (lane < ROT), sine, 0.0)
    return cosine, sine_up, sine_down


def rotate(x, cosine, sine_up, sine_down):
    return (
        x * cosine
        + pltpu.roll(x, 128 - ROT // 2, axis=1) * sine_up
        + pltpu.roll(x, ROT // 2, axis=1) * sine_down
    )


def unrotate(x, cosine, sine_up, sine_down):
    return (
        x * cosine
        - pltpu.roll(x, 128 - ROT // 2, axis=1) * sine_up
        - pltpu.roll(x, ROT // 2, axis=1) * sine_down
    )


def norm_kernel(x_ref, gain_ref, shift_ref, o_ref):
    x = x_ref[...].astype(F32)
    centred = x - jnp.mean(x, axis=1, keepdims=True)
    inv_std = lax.rsqrt(jnp.mean(centred * centred, axis=1, keepdims=True) + EPS)
    o_ref[...] = (centred * inv_std * gain_ref[...] + shift_ref[...]).astype(BF16)


def norm(x, gain, shift):
    rows, width = x.shape
    step = rows // 2
    row = pl.BlockSpec((1, width), lambda i: (0, 0))
    tile = pl.BlockSpec((step, width), lambda i: (i, 0))
    return pl.pallas_call(
        norm_kernel,
        grid=(rows // step,),
        in_specs=[tile, row, row],
        out_specs=tile,
        out_shape=jax.ShapeDtypeStruct(x.shape, BF16),
        cost_estimate=cost(rows * width * 8, rows * width * 4),
        name="norm",
    )(x, gain, shift)


def norm_back_kernel(x_ref, cot_ref, *refs):
    gain_ref, o_ref, sums_ref = refs[-3:]

    @pl.when(pl.program_id(0) == 0)
    def _():
        sums_ref[...] = jnp.zeros_like(sums_ref)

    x = x_ref[...].astype(F32)
    centred = x - jnp.mean(x, axis=1, keepdims=True)
    inv_std = lax.rsqrt(jnp.mean(centred * centred, axis=1, keepdims=True) + EPS)
    normalized = centred * inv_std
    grad = jnp.concatenate([r[...] for r in refs[:-3]], axis=1).astype(F32)
    sums_ref[0:1, :] += jnp.sum(grad * normalized, axis=0, keepdims=True)
    sums_ref[1:2, :] += jnp.sum(grad, axis=0, keepdims=True)
    cot = cot_ref[...].astype(F32)
    sums_ref[2:3, :] += jnp.sum(cot, axis=0, keepdims=True)
    scaled = grad * gain_ref[...]
    first = jnp.mean(scaled, axis=1, keepdims=True)
    second = jnp.mean(scaled * normalized, axis=1, keepdims=True)
    o_ref[...] = (inv_std * (scaled - first - normalized * second) + cot).astype(BF16)


def norm_back(x, cot, grads, gain):
    rows, width = x.shape
    step = min(128, rows)
    tile = pl.BlockSpec((step, width), lambda i: (i, 0))
    return pl.pallas_call(
        norm_back_kernel,
        grid=(rows // step,),
        in_specs=[tile, tile]
        + [pl.BlockSpec((step, g.shape[1]), lambda i: (i, 0)) for g in grads]
        + [pl.BlockSpec((1, width), lambda i: (0, 0))],
        out_specs=[tile, pl.BlockSpec((8, width), lambda i: (0, 0))],
        out_shape=[jax.ShapeDtypeStruct(x.shape, BF16), jax.ShapeDtypeStruct((8, width), F32)],
        cost_estimate=cost(rows * width * 20, rows * width * 12),
        name="norm_back",
    )(x, cot, *grads, gain)


def pick(where_ref, i, tiles):
    turn = lax.div(i, tiles)
    busy = turn < where_ref[4]
    slot = jnp.where(busy, where_ref[2 * turn], where_ref[5])
    return jnp.where(busy, lax.rem(i, tiles), tiles - 1), slot, busy


def pick_shard(where_ref, i, tiles, refs, o_ref):
    turn = lax.div(i, tiles)
    if len(refs) == 1:
        o_ref[...] = refs[0][...]
        return

    @pl.when(where_ref[2 * turn + 1] == 0)
    def _():
        o_ref[...] = refs[0][...]

    @pl.when(where_ref[2 * turn + 1] == 1)
    def _():
        o_ref[...] = refs[1][...]


def project_tile(j, tall, x_ref, wq_ref, wu_ref, bq_ref, bu_ref, tables, qkv_ref, act_ref, slope_ref, over):
    if qkv_ref is not None:
        width = wq_ref.shape[1]

        @pl.when(j < 2)
        def _():
            scale = jnp.where(j == 0, HD**-0.5, 1.0).astype(F32)

            def turned(m, t):
                raw = (dot_nn(x_ref[m, :], wq_ref[...]) + bq_ref[...]) * scale
                turn = [r[t, :] for r in tables]
                for p in range(width // 128):
                    lanes = slice(p * 128, (p + 1) * 128)
                    qkv_ref[m, lanes] = rotate(raw[:, lanes], *turn).astype(BF16)

            over(turned)

        @pl.when(j == 2)
        def _():
            def plain(m, t):
                qkv_ref[m, :] = (dot_nn(x_ref[m, :], wq_ref[...]) + bq_ref[...]).astype(BF16)

            over(plain)

    if act_ref is not None:

        @pl.when(j > 2)
        def _():
            def gelu(m, t):
                act_ref[m, :], slope_ref[m, :] = gelu_and_slope(dot_nn(x_ref[m, :], wu_ref[...]) + bu_ref[...])

            over(gelu)


def gelu_and_slope(v):
    root = 0.7978845608028654
    cubic = 0.044715
    square = v * v
    t = jnp.tanh(v * (root + (root * cubic) * square))
    half = 0.5 + 0.5 * t
    slope = half + (v * (0.5 - 0.5 * (t * t))) * (root + (3.0 * root * cubic) * square)
    return (v * half).astype(BF16), slope.astype(BF16)


def forward_kernel(came, tiles, where_ref, *refs):
    x_refs, refs = refs[:came], refs[came:]
    wq_ref, wu_ref, bq_ref, bu_ref = refs[:4]
    tables = refs[4:7]
    normed_ref, qkv_ref, act_ref, slope_ref = refs[-4:]
    i = pl.program_id(0)
    j, _, busy = pick(where_ref, i, tiles)
    rows = normed_ref.shape[0]
    step = min(ROWS, rows)

    @pl.when(busy & (j == 0))
    def _():
        pick_shard(where_ref, i, tiles, x_refs, normed_ref)

    def over(act):
        for m in range(0, rows, step):
            act(slice(m, m + step), slice(m, m + step))

    @pl.when(busy)
    def _():
        project_tile(j, None, normed_ref, wq_ref, wu_ref, bq_ref, bu_ref, tables, qkv_ref, act_ref, slope_ref, over)


def queries_kernel(came, tiles, where_ref, *refs):
    x_refs, refs = refs[:came], refs[came:]
    wq_ref, bq_ref = refs[:2]
    tables = refs[2:5]
    normed_ref, qkv_ref = refs[-2:]
    i = pl.program_id(0)
    j, _, busy = pick(where_ref, i, tiles)
    rows = normed_ref.shape[0]
    step = min(ROWS, rows)

    @pl.when(busy & (j == 0))
    def _():
        pick_shard(where_ref, i, tiles, x_refs, normed_ref)

    def over(act):
        for m in range(0, rows, step):
            act(slice(m, m + step), slice(m, m + step))

    @pl.when(busy)
    def _():
        project_tile(j, None, normed_ref, wq_ref, None, bq_ref, None, tables, qkv_ref, None, None, over)


def queries_chunk(where, xs, wq, bq, tables, bufs, parts):
    rows, depth = xs[0].shape
    width = wq.shape[1] // 3
    tiles = 3

    def at(k):
        def index(i, w):
            j, slot, _ = pick(w, i, tiles)
            return ((slot, j), (0, j), (0, 0), (slot, 0), (jnp.minimum(slot, parts - 1), 0))[k]

        return index

    args = [where, *xs, wq, bq, *tables]
    return pl.pallas_call(
        functools.partial(queries_kernel, len(xs), tiles),
        grid_spec=pltpu.PrefetchScalarGridSpec(
            num_scalar_prefetch=1,
            grid=(len(xs) * tiles,),
            in_specs=[pl.BlockSpec((rows, depth), at(2))] * len(xs)
            + [pl.BlockSpec((depth, width), at(1)), pl.BlockSpec((1, width), at(1))]
            + [pl.BlockSpec((rows, 128), at(4))] * 3
            + [pl.BlockSpec(memory_space=pl.ANY)] * 2,
            out_specs=[pl.BlockSpec((rows, depth), at(3)), pl.BlockSpec((rows, width), at(0))],
        ),
        out_shape=[jax.ShapeDtypeStruct(b.shape, BF16) for b in bufs],
        input_output_aliases={len(args): 0, len(args) + 1: 1},
        cost_estimate=cost(6 * rows * depth * width, 6 * depth * width),
        name="queries_chunk",
    )(*args, *bufs)


def forward_chunk(where, xs, wq, wu, bq, bu, tables, bufs, parts):
    rows, depth = xs[0].shape
    width = wq.shape[1] // 3
    ff = wu.shape[1]
    tiles = 3 + ff // width

    def at(k):
        def index(i, w):
            j, slot, _ = pick(w, i, tiles)
            return (
                (slot, jnp.minimum(j, 2)),
                (slot, jnp.maximum(j - 3, 0)),
                (slot, 0),
                (0, jnp.minimum(j, 2)),
                (0, jnp.maximum(j - 3, 0)),
                (0, 0),
                (jnp.minimum(slot, parts - 1), 0),
            )[k]

        return index

    in_specs = (
        [pl.BlockSpec((rows, depth), at(5))] * len(xs)
        + [
            pl.BlockSpec((depth, width), at(3)),
            pl.BlockSpec((depth, width), at(4)),
            pl.BlockSpec((1, width), at(3)),
            pl.BlockSpec((1, width), at(4)),
        ]
        + [pl.BlockSpec((rows, 128), at(6))] * 3
    )
    total = (parts + 1) * rows
    shapes = [(total, depth), (total, 3 * width), (total, ff), (total, ff)]
    args = [where, *xs, wq, wu, bq, bu, *tables]
    aliases = {}
    if bufs is not None:
        aliases = {len(args) + k: k for k in range(4)}
        args += list(bufs)
        in_specs += [pl.BlockSpec(memory_space=pl.ANY)] * 4
    return pl.pallas_call(
        functools.partial(forward_kernel, len(xs), tiles),
        grid_spec=pltpu.PrefetchScalarGridSpec(
            num_scalar_prefetch=1,
            grid=(len(xs) * tiles,),
            in_specs=in_specs,
            out_specs=[
                pl.BlockSpec((rows, depth), at(2)),
                pl.BlockSpec((rows, width), at(0)),
                pl.BlockSpec((rows, width), at(1)),
                pl.BlockSpec((rows, width), at(1)),
            ],
        ),
        out_shape=[jax.ShapeDtypeStruct(s, BF16) for s in shapes],
        input_output_aliases=aliases,
        cost_estimate=cost(2 * rows * depth * (3 * width + ff), 2 * depth * (3 * width + ff)),
        name="forward_chunk",
    )(*args)


def collect(where_ref, came, shards, x_refs, held_ref, full_ref, in_sems, out_sems, first, last):
    rows = x_refs[0].shape[0]

    def spot(c):
        return pl.ds(pl.multiple_of(where_ref[1 + shards + 2 * c] * rows, rows), rows)

    def loads(c):
        return pltpu.make_async_copy(x_refs[c], held_ref.at[spot(c)], in_sems.at[c])

    def stores(c):
        return pltpu.make_async_copy(held_ref.at[spot(c)], full_ref.at[spot(c)], out_sems.at[c])

    def each(act):
        for c in range(came):
            pl.when(where_ref[2 + shards + 2 * c] > 0)(functools.partial(act, c))

    @pl.when(first)
    def _():
        each(lambda c: loads(c).start())
        each(lambda c: loads(c).wait())
        if full_ref is not None:
            each(lambda c: stores(c).start())

    def finish():
        pl.when(last)(lambda: each(lambda c: stores(c).wait()))

    return finish


def early_over(where_ref, rows):
    step = min(ROWS, rows)

    def over(act):
        def body(t, carry):
            for m in range(0, rows, step):
                at = pl.ds(pl.multiple_of(where_ref[1 + t] * rows + m, step), step)
                act(at, at)
            return carry

        lax.fori_loop(0, where_ref[0], body, 0)

    return over


def queries_early_kernel(came, shards, where_ref, *refs):
    x_refs, refs = refs[:came], refs[came:]
    wq_ref, bq_ref = refs[:2]
    tables = refs[2:5]
    normed_ref, qkv_ref, held_ref, in_sems, out_sems = refs[5:]
    j = pl.program_id(0)
    finish = collect(
        where_ref, came, shards, x_refs, held_ref, normed_ref, in_sems, out_sems,
        j == 0, j == pl.num_programs(0) - 1,
    )
    over = early_over(where_ref, x_refs[0].shape[0])
    project_tile(j, None, held_ref, wq_ref, None, bq_ref, None, tables, qkv_ref, None, None, over)
    finish()


def units_early_kernel(came, shards, where_ref, *refs):
    x_refs, refs = refs[:came], refs[came:]
    wu_ref, bu_ref, act_ref, slope_ref, held_ref, in_sems = refs
    j = pl.program_id(0)
    collect(where_ref, came, shards, x_refs, held_ref, None, in_sems, None, j == 0, None)
    over = early_over(where_ref, x_refs[0].shape[0])
    project_tile(j + 3, None, held_ref, None, wu_ref, None, bu_ref, None, None, act_ref, slope_ref, over)


def queries_early(where, xs, wq, bq, tables, parts):
    rows, depth = xs[0].shape
    width = wq.shape[1] // 3
    count = parts * rows
    in_place = pl.BlockSpec(memory_space=pl.ANY)
    return pl.pallas_call(
        functools.partial(queries_early_kernel, len(xs), parts),
        grid_spec=pltpu.PrefetchScalarGridSpec(
            num_scalar_prefetch=1,
            grid=(3,),
            in_specs=[in_place] * len(xs)
            + [pl.BlockSpec((depth, width), lambda j, w: (0, j)), pl.BlockSpec((1, width), lambda j, w: (0, j))]
            + [whole(t) for t in tables],
            out_specs=[in_place, pl.BlockSpec((count, width), lambda j, w: (0, j))],
            scratch_shapes=[
                pltpu.VMEM((count, depth), BF16),
                pltpu.SemaphoreType.DMA((len(xs),)),
                pltpu.SemaphoreType.DMA((len(xs),)),
            ],
        ),
        out_shape=[
            jax.ShapeDtypeStruct((count + rows, depth), BF16),
            jax.ShapeDtypeStruct((count + rows, 3 * width), BF16),
        ],
        cost_estimate=cost(6 * count * depth * width, 6 * depth * width),
        name="queries_early",
    )(where, *xs, wq, bq, *tables)


def units_early(where, xs, wu, bu, width, parts):
    rows, depth = xs[0].shape
    ff = wu.shape[1]
    count = parts * rows
    return pl.pallas_call(
        functools.partial(units_early_kernel, len(xs), parts),
        grid_spec=pltpu.PrefetchScalarGridSpec(
            num_scalar_prefetch=1,
            grid=(ff // width,),
            in_specs=[pl.BlockSpec(memory_space=pl.ANY)] * len(xs)
            + [pl.BlockSpec((depth, width), lambda j, w: (0, j)), pl.BlockSpec((1, width), lambda j, w: (0, j))],
            out_specs=[pl.BlockSpec((count, width), lambda j, w: (0, j))] * 2,
            scratch_shapes=[pltpu.VMEM((count, depth), BF16), pltpu.SemaphoreType.DMA((len(xs),))],
        ),
        out_shape=[jax.ShapeDtypeStruct((count + rows, ff), BF16)] * 2,
        cost_estimate=cost(2 * count * depth * ff, 2 * depth * ff),
        name="units_early",
    )(where, *xs, wu, bu)


def backward_early_kernel(came, shards, where_ref, *refs):
    c_refs, refs = refs[:came], refs[came:]
    wo_ref, wd_ref, slope_ref, cot_ref, ga_ref, gh_ref, held_ref, in_sems, out_sems = refs
    j = pl.program_id(0)
    finish = collect(
        where_ref, came, shards, c_refs, held_ref, cot_ref, in_sems, out_sems,
        j == 0, j == pl.num_programs(0) - 1,
    )
    rows = c_refs[0].shape[0]
    step = min(ROWS, rows)

    def over(act):
        def body(t, carry):
            for m in range(0, rows, step):
                act(pl.ds(pl.multiple_of(where_ref[1 + t] * rows + m, step), step))
            return carry

        lax.fori_loop(0, where_ref[0], body, 0)

    @pl.when(j == 0)
    def _():
        weight = side_by_side(wo_ref)

        def act(m):
            ga_ref[m, :] = dot_nt(held_ref[m, :], weight).astype(BF16)

        over(act)

    @pl.when(j > 0)
    def _():
        weight = side_by_side(wd_ref)

        def act(m):
            gh_ref[m, :] = (dot_nt(held_ref[m, :], weight) * slope_ref[m, :].astype(F32)).astype(BF16)

        over(act)

    finish()


def backward_early(where, cots, wo, wd, slope, parts):
    rows, depth = cots[0].shape
    pieces, width, piece = wo.shape
    ff = wd.shape[1]
    count = parts * rows
    total = count + rows
    in_place = pl.BlockSpec(memory_space=pl.ANY)

    def tile(j):
        return jnp.maximum(j - 1, 0)

    return pl.pallas_call(
        functools.partial(backward_early_kernel, len(cots), parts),
        grid_spec=pltpu.PrefetchScalarGridSpec(
            num_scalar_prefetch=1,
            grid=(1 + ff // width,),
            in_specs=[in_place] * len(cots)
            + [
                whole(wo),
                pl.BlockSpec((pieces, width, piece), lambda j, w: (0, tile(j), 0)),
                pl.BlockSpec((count, width), lambda j, w: (0, tile(j))),
            ],
            out_specs=[
                in_place,
                pl.BlockSpec((count, width), lambda j, w: (0, 0)),
                pl.BlockSpec((count, width), lambda j, w: (0, tile(j))),
            ],
            scratch_shapes=[
                pltpu.VMEM((count, depth), BF16),
                pltpu.SemaphoreType.DMA((len(cots),)),
                pltpu.SemaphoreType.DMA((len(cots),)),
            ],
        ),
        out_shape=[jax.ShapeDtypeStruct(s, BF16) for s in ((total, depth), (total, width), (total, ff))],
        cost_estimate=cost(2 * count * depth * (width + ff), 2 * depth * (width + ff)),
        name="backward_early",
    )(where, *cots, wo, wd, slope)


def low_lanes(rows):
    return lax.broadcasted_iota(jnp.int32, (rows, 128), 1) < HD


def attend_kernel(
    skipped, first_ref, q_ref, k_ref, v_ref, segc_ref, segr_ref, *refs
):
    o_ref, lse_ref, max_ref, acc_ref, bias_ref = refs[-5:]
    i = pl.program_id(0) + skipped
    block, width = q_ref.shape
    pairs = width // 128
    low = low_lanes(block)
    owns = (low, jnp.logical_not(low))
    max_ref[...] = jnp.full_like(max_ref, NEGATIVE)
    lse_ref[...] = jnp.zeros_like(lse_ref)
    acc_ref[...] = jnp.zeros_like(acc_ref)
    q0 = pl.multiple_of(i * block, block)
    query_seg = segr_ref[:, pl.ds(q0, block)]
    query_row = q0 + lax.broadcasted_iota(jnp.int32, (1, block), 1)

    def set_bias(k0):
        key_seg = segc_ref[pl.ds(k0, block), :]
        key_row = k0 + lax.broadcasted_iota(jnp.int32, (block, 1), 0)
        bias_ref[...] = jnp.where((key_seg == query_seg) & (key_row <= query_row), 0.0, NEGATIVE)

    def scores(k0, p, h):
        lanes = slice(p * 128, (p + 1) * 128)
        q = q_ref[:, lanes]
        mine = jnp.where(owns[h], q, jnp.zeros_like(q))
        return dot_nt(k_ref[pl.ds(k0, block), lanes], mine) + bias_ref[...]

    def find_max(j, carry):
        k0 = pl.multiple_of(j * block, block)
        set_bias(k0)
        for p in range(pairs):
            for h in range(2):
                s = scores(k0, p, h)
                max_ref[2 * p + h] = jnp.maximum(max_ref[2 * p + h], jnp.max(s, axis=0, keepdims=True))
        return carry

    lax.fori_loop(first_ref[i], i + 1, find_max, 0)

    def add_up(j, carry):
        k0 = pl.multiple_of(j * block, block)
        set_bias(k0)
        for p in range(pairs):
            v = v_ref[pl.ds(k0, block), p * 128 : (p + 1) * 128]
            for h in range(2):
                e = jnp.exp(scores(k0, p, h) - max_ref[2 * p + h])
                lse_ref[p, h : h + 1, :] += jnp.sum(e, axis=0, keepdims=True)
                acc_ref[2 * p + h] += dot_tn(e.astype(BF16), jnp.where(owns[h], v, jnp.ones_like(v)))
        return carry

    lax.fori_loop(first_ref[i], i + 1, add_up, 0)
    for p in range(pairs):
        even, odd = acc_ref[2 * p], acc_ref[2 * p + 1]
        o_ref[:, p * 128 : (p + 1) * 128] = jnp.where(
            low, even / pltpu.roll(even, HD, axis=1), odd / pltpu.roll(odd, HD, axis=1)
        ).astype(BF16)
        for h in range(2):
            lse_ref[p, h : h + 1, :] = max_ref[2 * p + h] + jnp.log(lse_ref[p, h : h + 1, :])


def attend(qkv, segc, segr, first, part, parts, bufs):
    count = segr.shape[1]
    width = qkv.shape[1] // 3
    pairs = width // 128
    steps = count // BLOCK // parts
    skipped = part * steps
    in_place = [] if bufs is None else [pl.BlockSpec(memory_space=pl.ANY)] * 2
    return pl.pallas_call(
        functools.partial(attend_kernel, skipped),
        grid_spec=pltpu.PrefetchScalarGridSpec(
            num_scalar_prefetch=1,
            grid=(steps,),
            in_specs=[
                pl.BlockSpec((BLOCK, width), lambda i, f: (i + skipped, 0)),
                pl.BlockSpec((count, width), lambda i, f: (0, 1)),
                pl.BlockSpec((count, width), lambda i, f: (0, 2)),
                whole(segc),
                whole(segr),
            ]
            + in_place,
            out_specs=[
                pl.BlockSpec((BLOCK, width), lambda i, f: (i + skipped, 0)),
                pl.BlockSpec((pairs, 8, BLOCK), lambda i, f: (0, 0, i + skipped)),
            ],
            scratch_shapes=[
                pltpu.VMEM((2 * pairs, 1, BLOCK), F32),
                pltpu.VMEM((2 * pairs, BLOCK, 128), F32),
                pltpu.VMEM((BLOCK, BLOCK), F32),
            ],
        ),
        out_shape=[
            jax.ShapeDtypeStruct((count, width), BF16),
            jax.ShapeDtypeStruct((pairs, 8, count), F32),
        ],
        input_output_aliases={} if bufs is None else {6: 0, 7: 1},
        cost_estimate=cost(30e9 * width / 512, count * width * 8),
        name="attend",
    )(first, qkv, qkv, qkv, segc, segr, *([] if bufs is None else bufs))


def attend_back_kernel(
    first_ref, q_ref, k_ref, v_ref, go_ref, o_ref, lse_ref, segc_ref, segr_ref,
    cos_ref, up_ref, down_ref, *refs,
):
    gq_ref, gk_ref, gv_ref, dq_ref, dk_ref, dv_ref, bias_ref = refs[-7:]
    i = pl.program_id(0)
    steps = pl.num_programs(0)
    block, width = q_ref.shape
    pairs = width // 128
    low = low_lanes(block)
    owns = (low, jnp.logical_not(low))

    @pl.when(i == 0)
    def _():
        dk_ref[...] = jnp.zeros_like(dk_ref)
        dv_ref[...] = jnp.zeros_like(dv_ref)

    dq_ref[...] = jnp.zeros_like(dq_ref)
    q0 = pl.multiple_of(i * block, block)
    query_seg = segr_ref[:, pl.ds(q0, block)]
    query_row = q0 + lax.broadcasted_iota(jnp.int32, (1, block), 1)
    half = jnp.where(
        lax.broadcasted_iota(jnp.int32, (8, 128), 1) // HD == lax.broadcasted_iota(jnp.int32, (8, 128), 0),
        1.0,
        0.0,
    ).astype(F32)
    inner = []
    for p in range(pairs):
        lanes = slice(p * 128, (p + 1) * 128)
        product = go_ref[:, lanes].astype(F32) * o_ref[:, lanes].astype(F32)
        inner.append(
            lax.dot_general(
                half, product, (((1,), (1,)), ((), ())),
                precision=lax.Precision.HIGHEST, preferred_element_type=F32,
            )
        )

    def body(j, carry):
        k0 = pl.multiple_of(j * block, block)
        key_seg = segc_ref[pl.ds(k0, block), :]
        key_row = k0 + lax.broadcasted_iota(jnp.int32, (block, 1), 0)
        bias_ref[...] = jnp.where((key_seg == query_seg) & (key_row <= query_row), 0.0, NEGATIVE)
        for p in range(pairs):
            lanes = slice(p * 128, (p + 1) * 128)
            k = k_ref[pl.ds(k0, block), lanes]
            v = v_ref[pl.ds(k0, block), lanes]
            q = q_ref[:, lanes]
            go = go_ref[:, lanes]
            sums = None
            for h in range(2):
                q_own, go_own, k_own = [jnp.where(owns[h], a, jnp.zeros_like(a)) for a in (q, go, k)]
                prob = jnp.exp(dot_nt(k, q_own) + bias_ref[...] - lse_ref[p, h : h + 1, :])
                grad_score = (prob * (dot_nt(v, go_own) - inner[p][h : h + 1, :])).astype(BF16)
                new = (
                    dot_nn(prob.astype(BF16), go_own),
                    dot_nn(grad_score, q_own),
                    dot_tn(grad_score, k_own),
                )
                sums = new if sums is None else tuple(a + b for a, b in zip(sums, new))
            dv_ref[pl.ds(k0, block), lanes] += sums[0]
            dk_ref[pl.ds(k0, block), lanes] += sums[1]
            dq_ref[:, lanes] += sums[2]
        return carry

    lax.fori_loop(first_ref[i], i + 1, body, 0)
    turn = [r[pl.ds(q0, block), :] for r in (cos_ref, up_ref, down_ref)]
    for p in range(pairs):
        lanes = slice(p * 128, (p + 1) * 128)
        gq_ref[:, lanes] = unrotate(dq_ref[:, lanes] * HD**-0.5, *turn).astype(BF16)

    @pl.when(i == steps - 1)
    def _():
        def finish(j, carry):
            k0 = pl.multiple_of(j * block, block)
            rows = pl.ds(k0, block)
            turn = [r[rows, :] for r in (cos_ref, up_ref, down_ref)]
            for p in range(pairs):
                lanes = slice(p * 128, (p + 1) * 128)
                gk_ref[rows, lanes] = unrotate(dk_ref[rows, lanes], *turn).astype(BF16)
                gv_ref[rows, lanes] = dv_ref[rows, lanes].astype(BF16)
            return carry

        lax.fori_loop(0, steps, finish, 0)


def attend_back(qkv, grad_out, out, lse, segc, segr, first, tables, part, parts, bufs):
    count = segr.shape[1]
    whole_width = qkv.shape[1] // 3
    width = whole_width // parts
    pairs = width // 128
    row_tile = pl.BlockSpec((BLOCK, width), lambda i, f: (i, part))
    column = pl.BlockSpec((count, width), lambda i, f: (0, part))
    in_place = [] if bufs is None else [pl.BlockSpec(memory_space=pl.ANY)] * 3
    args = [first, qkv, qkv, qkv, grad_out, out, lse, segc, segr, *tables]
    return pl.pallas_call(
        attend_back_kernel,
        grid_spec=pltpu.PrefetchScalarGridSpec(
            num_scalar_prefetch=1,
            grid=(count // BLOCK,),
            in_specs=[
                row_tile,
                pl.BlockSpec((count, width), lambda i, f: (0, parts + part)),
                pl.BlockSpec((count, width), lambda i, f: (0, 2 * parts + part)),
                row_tile,
                row_tile,
                pl.BlockSpec((pairs, 8, BLOCK), lambda i, f: (part, 0, i)),
                whole(segc),
                whole(segr),
                *[whole(t) for t in tables],
            ]
            + in_place,
            out_specs=[row_tile, column, column],
            scratch_shapes=[
                pltpu.VMEM((BLOCK, width), F32),
                pltpu.VMEM((count, width), F32),
                pltpu.VMEM((count, width), F32),
                pltpu.VMEM((BLOCK, BLOCK), F32),
            ],
        ),
        out_shape=[jax.ShapeDtypeStruct((count, whole_width), BF16)] * 3,
        input_output_aliases={} if bufs is None else {len(args) + k: k for k in range(3)},
        cost_estimate=cost(44e9 * width / 512, count * width * 20),
        name="attend_back",
    )(*args, *([] if bufs is None else bufs))


def side_by_side(ref):
    return jnp.concatenate([ref[b] for b in range(ref.shape[0])], axis=1)


def mix_kernel(att_ref, act_ref, wo_ref, wd_ref, o_ref):
    wo, wd = side_by_side(wo_ref), side_by_side(wd_ref)
    step = min(512, att_ref.shape[0])
    for m in range(0, att_ref.shape[0], step):
        rs = slice(m, m + step)
        o_ref[rs, :] = (dot_nn(att_ref[rs, :], wo) + dot_nn(act_ref[rs, :], wd)).astype(BF16)


def mix(att, act, wo, wd):
    pieces, width, piece = wo.shape
    ff = wd.shape[1]
    count = att.shape[0]
    group = max(1, 512 // piece)
    return pl.pallas_call(
        mix_kernel,
        grid=(pieces // group,),
        in_specs=[
            pl.BlockSpec((count, width), lambda j: (0, 0)),
            pl.BlockSpec((count, ff), lambda j: (0, 0)),
            pl.BlockSpec((group, width, piece), lambda j: (j, 0, 0)),
            pl.BlockSpec((group, ff, piece), lambda j: (j, 0, 0)),
        ],
        out_specs=pl.BlockSpec((count, group * piece), lambda j: (0, j)),
        out_shape=jax.ShapeDtypeStruct((count, pieces * piece), BF16),
        cost_estimate=cost(2 * count * (width + ff) * pieces * piece, 4 * count * ff),
        name="mix",
    )(att, act, wo, wd)


def mixed_kernel(x_ref, sum_ref, bias_ref, o_ref):
    o_ref[...] = (x_ref[...].astype(F32) + sum_ref[...].astype(F32) + bias_ref[...]).astype(BF16)


def mixed_out(x, total, bias):
    rows, width = x.shape
    step = min(256, rows)
    tile = pl.BlockSpec((step, width), lambda i: (i, 0))
    return pl.pallas_call(
        mixed_kernel,
        grid=(rows // step,),
        in_specs=[tile, tile, pl.BlockSpec((1, width), lambda i: (0, 0))],
        out_specs=tile,
        out_shape=jax.ShapeDtypeStruct(x.shape, BF16),
        cost_estimate=cost(rows * width * 4, rows * width * 6),
        name="mixed_out",
    )(x, total, bias)


def backward_kernel(came, tiles, where_ref, *refs):
    c_refs, refs = refs[:came], refs[came:]
    wo_ref, wd_ref, slope_ref = refs[:3]
    cot_ref, ga_ref, gh_ref = refs[-3:]
    i = pl.program_id(0)
    j, _, busy = pick(where_ref, i, tiles)
    rows = cot_ref.shape[0]
    step = min(ROWS, rows)

    @pl.when(busy & (j == 0))
    def _():
        pick_shard(where_ref, i, tiles, c_refs, cot_ref)
        weight = side_by_side(wo_ref)
        for m in range(0, rows, step):
            ga_ref[m : m + step, :] = dot_nt(cot_ref[m : m + step, :], weight).astype(BF16)

    @pl.when(busy & (j > 0))
    def _():
        weight = side_by_side(wd_ref)
        for m in range(0, rows, step):
            gh_ref[m : m + step, :] = (
                dot_nt(cot_ref[m : m + step, :], weight) * slope_ref[m : m + step, :].astype(F32)
            ).astype(BF16)


def backward_chunk(where, cots, wo, wd, slope, bufs, parts):
    rows, depth = cots[0].shape
    pieces, width, piece = wo.shape
    ff = wd.shape[1]
    tiles = 1 + ff // width

    def at(k):
        def index(i, w):
            j, slot, _ = pick(w, i, tiles)
            return ((0, 0), (0, jnp.maximum(j - 1, 0), 0), (slot, jnp.maximum(j - 1, 0)), (slot, 0))[k]

        return index

    in_specs = [pl.BlockSpec((rows, depth), at(0))] * len(cots) + [
        whole(wo),
        pl.BlockSpec((pieces, width, piece), at(1)),
        pl.BlockSpec((rows, width), at(2)),
    ]
    total = (parts + 1) * rows
    shapes = [(total, depth), (total, width), (total, ff)]
    args = [where, *cots, wo, wd, slope]
    aliases = {}
    if bufs is not None:
        aliases = {len(args) + k: k for k in range(3)}
        args += list(bufs)
        in_specs += [pl.BlockSpec(memory_space=pl.ANY)] * 3
    return pl.pallas_call(
        functools.partial(backward_kernel, len(cots), tiles),
        grid_spec=pltpu.PrefetchScalarGridSpec(
            num_scalar_prefetch=1,
            grid=(len(cots) * tiles,),
            in_specs=in_specs,
            out_specs=[
                pl.BlockSpec((rows, depth), at(3)),
                pl.BlockSpec((rows, width), at(3)),
                pl.BlockSpec((rows, width), at(2)),
            ],
        ),
        out_shape=[jax.ShapeDtypeStruct(s, BF16) for s in shapes],
        input_output_aliases=aliases,
        cost_estimate=cost(2 * rows * depth * (width + ff), 2 * depth * (width + ff)),
        name="backward_chunk",
    )(*args)


def grad_kernel(gq_ref, gk_ref, gv_ref, gh_ref, wq_ref, wu_ref, o_ref):
    step = min(512, gq_ref.shape[0])
    width = gq_ref.shape[1]
    for m in range(0, gq_ref.shape[0], step):
        rs = slice(m, m + step)
        left = jnp.concatenate([r[rs, :] for r in (gq_ref, gk_ref, gv_ref)], axis=1)
        o_ref[rs, :] = (dot_nt(left, wq_ref[...]) + dot_nt(gh_ref[rs, :], wu_ref[...])).astype(BF16)


def grad_normed(gqkv, gh, wq, wu, start, stop):
    count, width = gqkv[0].shape
    ff = gh.shape[1]
    tile = min(256, stop - start)
    first = start // tile
    return pl.pallas_call(
        grad_kernel,
        grid=((stop - start) // tile,),
        in_specs=[once((count, width))] * 3
        + [
            once((count, ff)),
            pl.BlockSpec((tile, wq.shape[1]), lambda j: (first + j, 0)),
            pl.BlockSpec((tile, wu.shape[1]), lambda j: (first + j, 0)),
        ],
        out_specs=pl.BlockSpec((count, tile), lambda j: (0, j)),
        out_shape=jax.ShapeDtypeStruct((count, stop - start), BF16),
        cost_estimate=cost(2 * count * (stop - start) * (3 * width + ff), 4 * count * ff),
        name="grad_normed",
    )(*gqkv, gh, wq, wu)


def put_columns(att_ref, act_ref, cot, o_ref, start, stop, add):
    width = att_ref.shape[1]
    at = start
    while at < stop:
        if at < width:
            end = min(stop, width)
            left = att_ref[:, at:end]
        else:
            end = min(stop, at + 512)
            left = act_ref[:, at - width : end - width]
        rows = slice(at - start, end - start)
        total = dot_tn(left, cot)
        if add is not None:
            total = total + add[0, rows, :].astype(F32)
        o_ref[0, rows, :] = total.astype(BF16)
        at = end


def columns_send_kernel(where_ref, att_ref, act_ref, c_ref, o_ref):
    put_columns(att_ref, act_ref, c_ref[...], o_ref, 0, o_ref.shape[1], None)


def columns_keep_kernel(where_ref, att_ref, act_ref, c_ref, came_ref, a_ref, b_ref):
    half = a_ref.shape[1]
    first = pl.program_id(0) < pl.num_programs(0) // 2

    @pl.when(first)
    def _():
        put_columns(att_ref, act_ref, c_ref[...], a_ref, 0, half, came_ref)

    @pl.when(jnp.logical_not(first))
    def _():
        put_columns(att_ref, act_ref, c_ref[...], b_ref, half, 2 * half, came_ref)


def rows_send_kernel(arrays, where_ref, x_ref, *refs):
    g_refs, o_ref, sum_ref = refs[:arrays], refs[-2], refs[-1]
    x = x_ref[...]
    first = pl.program_id(0) == 0
    start = 0
    for g_ref in g_refs:
        width = g_ref.shape[1]
        step = min(512, width)
        for m in range(0, width, step):
            o_ref[0, :, start + m : start + m + step] = dot_tn(x, g_ref[:, m : m + step]).astype(BF16)

        @pl.when(first)
        def _():
            ones = jnp.ones((8, g_ref.shape[0]), BF16)
            for m in range(0, width, step):
                sum_ref[:, start + m : start + m + step] = dot_nn(ones, g_ref[:, m : m + step])

        start += width


def rows_keep_kernel(arrays, where_ref, x_ref, *refs):
    g_refs, came_ref, a_ref, b_ref = refs[:arrays], *refs[arrays:]
    first = pl.program_id(0) < pl.num_programs(0) // 2
    x = x_ref[...]
    half = a_ref.shape[2]

    def put(o_ref, low):
        start = 0
        for g_ref in g_refs:
            width = g_ref.shape[1]
            at = max(start, low)
            while at < min(start + width, low + half):
                end = min(start + width, low + half, at + 512)
                o_ref[0, :, at - low : end - low] = (
                    dot_tn(x, g_ref[:, at - start : end - start])
                    + came_ref[0, :, at - low : end - low].astype(F32)
                ).astype(BF16)
                at = end
            start += width

    pl.when(first)(lambda: put(a_ref, 0))
    pl.when(jnp.logical_not(first))(lambda: put(b_ref, half))


def once(shape):
    return pl.BlockSpec(shape, lambda *_: (0,) * len(shape), pipeline_mode=pl.Buffered(1))


def column_grads(where, att, act, cot, places, came=None):
    count, width = att.shape
    ff = act.shape[1]
    piece = cot.shape[1] // (2 * places)
    flops = 2 * count * (width + ff) * piece * places
    base = [once((count, width)), once((count, ff)), pl.BlockSpec((count, piece), lambda t, w: (0, w[t]))]
    if came is None:
        return pl.pallas_call(
            columns_send_kernel,
            grid_spec=pltpu.PrefetchScalarGridSpec(
                num_scalar_prefetch=1,
                grid=(places,),
                in_specs=base,
                out_specs=pl.BlockSpec((1, width + ff, piece), lambda t, w: (t, 0, 0)),
            ),
            out_shape=jax.ShapeDtypeStruct((places, width + ff, piece), BF16),
            cost_estimate=cost(flops, 2 * count * (width + ff)),
            name="columns_send",
        )(where, att, act, cot)
    half = (width + ff) // 2
    turns = 2 * places
    return pl.pallas_call(
        columns_keep_kernel,
        grid_spec=pltpu.PrefetchScalarGridSpec(
            num_scalar_prefetch=1,
            grid=(turns,),
            in_specs=base
            + [pl.BlockSpec((1, half, piece), lambda t, w: (w[turns + t], t // places, 0))],
            out_specs=[
                pl.BlockSpec((1, half, piece), lambda t, w: (jnp.minimum(t, places - 1), 0, 0)),
                pl.BlockSpec((1, half, piece), lambda t, w: (jnp.maximum(t - places, 0), 0, 0)),
            ],
        ),
        out_shape=[jax.ShapeDtypeStruct((places, half, piece), BF16)] * 2,
        cost_estimate=cost(flops, 2 * count * (width + ff)),
        name="columns_keep",
    )(where, att, act, cot, came)


def row_grads(where, x, gs, count, places, came=None):
    width = sum(g.shape[1] for g in gs)
    piece = x.shape[1] // (2 * places)
    flops = 2 * count * width * piece * places
    base = [pl.BlockSpec((count, piece), lambda t, w: (0, w[t]))] + [once((count, g.shape[1])) for g in gs]
    if came is None:
        return pl.pallas_call(
            functools.partial(rows_send_kernel, len(gs)),
            grid_spec=pltpu.PrefetchScalarGridSpec(
                num_scalar_prefetch=1,
                grid=(places,),
                in_specs=base,
                out_specs=[
                    pl.BlockSpec((1, piece, width), lambda t, w: (t, 0, 0)),
                    pl.BlockSpec((8, width), lambda t, w: (0, 0)),
                ],
            ),
            out_shape=[
                jax.ShapeDtypeStruct((places, piece, width), BF16),
                jax.ShapeDtypeStruct((8, width), F32),
            ],
            cost_estimate=cost(flops, 2 * count * width),
            name="rows_send",
        )(where, x, *gs)
    half = width // 2
    turns = 2 * places
    return pl.pallas_call(
        functools.partial(rows_keep_kernel, len(gs)),
        grid_spec=pltpu.PrefetchScalarGridSpec(
            num_scalar_prefetch=1,
            grid=(turns,),
            in_specs=base
            + [pl.BlockSpec((1, piece, half), lambda t, w: (w[turns + t], 0, t // places))],
            out_specs=[
                pl.BlockSpec((1, piece, half), lambda t, w: (jnp.minimum(t, places - 1), 0, 0)),
                pl.BlockSpec((1, piece, half), lambda t, w: (jnp.maximum(t - places, 0), 0, 0)),
            ],
        ),
        out_shape=[jax.ShapeDtypeStruct((places, piece, half), BF16)] * 2,
        cost_estimate=cost(flops, 2 * count * width),
        name="rows_keep",
    )(where, x, *gs, came)


def after(value, *marks):
    return lax.optimization_barrier((value, *marks))[0]


def swap(x, bit):
    size = lax.axis_size("dp")
    return lax.ppermute(x, "dp", [(i, i ^ (1 << bit)) for i in range(size)])


def halve(xs, orders, k, sent=None):
    kept = []
    for x, y, bits in zip(xs, sent or xs, orders):
        rest = x.shape[0] // 2
        came = swap(y[rest:], bits[k])
        total = x[:rest].astype(F32) + came.astype(F32)
        kept.append(total if k == len(bits) - 1 else total.astype(BF16))
    return kept


def small_sum_kernel(phases, x_ref, o_ref, sent_ref, came_ref, send_sems, came_sems):
    barrier = pltpu.get_barrier_semaphore()

    def partner(axis, bit):
        return {axis: lax.axis_index(axis) ^ (1 << bit)}

    for axis, bit, _ in phases:
        pl.semaphore_signal(
            barrier, inc=1, device_id=partner(axis, bit), device_id_type=pl.DeviceIdType.MESH
        )
    pl.semaphore_wait(barrier, len(phases))
    sent_ref[0] = x_ref[...]
    for k, (axis, bit, rows) in enumerate(phases):
        span = pl.ds(0, rows)
        copy = pltpu.make_async_remote_copy(
            src_ref=sent_ref.at[k, span],
            dst_ref=came_ref.at[k, span],
            send_sem=send_sems.at[k],
            recv_sem=came_sems.at[k],
            device_id=partner(axis, bit),
            device_id_type=pl.DeviceIdType.MESH,
        )
        copy.start()
        copy.wait()
        total = sent_ref[k, 0:rows] + came_ref[k, 0:rows]
        if k == len(phases) - 1:
            o_ref[...] = sent_ref[k]
            o_ref[0:rows] = total
        else:
            sent_ref[k + 1] = sent_ref[k]
            sent_ref[k + 1, 0:rows] = total


def small_sums(x, common):
    rows = x.shape[0]
    phases = []
    for axis, height in (("dp", rows), ("tensor", common)):
        for bit in range(lax.axis_size(axis).bit_length() - 1):
            phases.append((axis, bit, height))
    return pl.pallas_call(
        functools.partial(small_sum_kernel, phases),
        in_specs=[pl.BlockSpec(memory_space=pltpu.VMEM)],
        out_specs=pl.BlockSpec(memory_space=pltpu.VMEM),
        out_shape=jax.ShapeDtypeStruct(x.shape, F32),
        scratch_shapes=[
            pltpu.VMEM((len(phases), *x.shape), F32),
            pltpu.VMEM((len(phases), *x.shape), F32),
            pltpu.SemaphoreType.DMA((len(phases),)),
            pltpu.SemaphoreType.DMA((len(phases),)),
        ],
        compiler_params=pltpu.CompilerParams(collective_id=0, has_side_effects=True),
        name="small_sums",
    )(x)


def local(
    tokens, segments, ln_gain, ln_shift, qkv_weight, qkv_bias, out_weight, out_bias,
    fc1_weight, fc1_bias, fc2_weight, fc2_bias, cotangent,
):
    n = lax.axis_size("tensor")
    pieces = lax.axis_size("dp")
    me = lax.axis_index("tensor")
    rows, depth = tokens.shape
    count = segments.shape[1]
    width = qkv_weight.shape[2]

    def shift(x, pairs):
        return lax.ppermute(x, "tensor", pairs)

    def turns(step):
        left, right = me - step, me + step
        has_left, has_right = left >= 0, right < n
        one = jnp.where(has_left, left, right)
        last = jnp.where(has_right, right, jnp.where(has_left, left, n))
        busy = has_left.astype(jnp.int32) + has_right.astype(jnp.int32)
        values = [one, jnp.where(has_left, 0, 1), right, 1, busy, last]
        return jnp.stack([jnp.asarray(v, jnp.int32) for v in values])

    def places_of(shards, present):
        shards, present = jnp.stack(shards), jnp.stack(present)
        order = jnp.sort(jnp.where(present, shards, n))
        order = jnp.concatenate([order, jnp.full((n,), n, order.dtype)])[:n]
        return jnp.concatenate(
            [
                jnp.sum(present.astype(jnp.int32))[None],
                order,
                jnp.stack([jnp.clip(shards, 0, n - 1), present.astype(jnp.int32)], axis=1).reshape(-1),
            ]
        ).astype(jnp.int32)

    def present_shards(steps):
        shards = [me] + [me + d * s for s in range(1, steps + 1) for d in (-1, 1)]
        return places_of(shards, [(x >= 0) & (x < n) for x in shards])

    early = present_shards(n - 2)
    late = turns(n - 1)
    middle = [turns(s) for s in range(2, n - 1)]
    cot_shards, cot_there = [me], [me >= 0]
    for s in range(1, n - 1):
        for direction in range(2):
            at_end = me == (n - 1, 0)[direction]
            shard = me + (-s, s)[direction]
            cot_shards += [shard, shard]
            cot_there += [(shard >= 0) & (shard < n) & jnp.logical_not(at_end), at_end]
    cot_early = places_of(cot_shards, cot_there)

    bits = [b for b in range(1, pieces.bit_length() - 1)]
    places = pieces // 2
    mine = lax.axis_index("dp")

    def place_of(r, order):
        return sum(((r >> (len(order) - 1 - k)) & 1) << bit for k, bit in enumerate(order))

    kept = [place_of(r, bits) for r in range(places)] + [place_of(r, bits[::-1]) for r in range(places)]
    send_where = mine ^ jnp.array([2 * q + 1 for q in range(places)], jnp.int32)
    keep_where = jnp.concatenate([mine ^ jnp.array(kept, jnp.int32), jnp.array(kept, jnp.int32) // 2])
    plans = [early, late, *middle, cot_early, send_where, keep_where]

    own_normed = norm(tokens, ln_gain[None], ln_shift[None])

    w_qkv = lax.all_gather(qkv_weight.reshape(-1, 3 * width), "dp", axis=0, tiled=True)
    w_up = lax.all_gather(fc1_weight, "dp", axis=0, tiled=True)
    w_out = lax.all_gather(out_weight, "dp", axis=0)
    w_down = lax.all_gather(fc2_weight, "dp", axis=0)

    segment_row = segments[0]
    starts = seq_starts(segment_row)
    tables = rotary_tables(jnp.arange(count, dtype=jnp.int32) - starts)
    first = starts[::BLOCK] // BLOCK
    segc, segr = segment_row[:, None], segment_row[None, :]

    bias_qkv, bias_up = qkv_bias.reshape(1, -1), fc1_bias[None]
    def line_step(pair, s):
        right, left = pair
        return [
            shift(right, [(i, i + 1) for i in range(s - 1, n - 1)]),
            shift(left, [(i, i - 1) for i in range(1, n - s + 1)]),
        ]

    def line_sum(x):
        return lax.psum_scatter(x, "tensor", scatter_dimension=0, tiled=True)

    def flat(pairs):
        return [x for pair in pairs for x in pair]

    project = (w_qkv, w_up, bias_qkv, bias_up, tables)
    normed_in = [line_step([own_normed] * 2, 1)]
    plans = lax.optimization_barrier(plans)
    early, late, cot_early, send_where, keep_where = plans[0], plans[1], *plans[-3:]
    middle = plans[2:-3]
    normed, qkv = queries_early(
        after(present_shards(1), *plans, first, segc), [own_normed] + normed_in[0], w_qkv, bias_qkv, tables, n
    )
    early_qkv = qkv
    for s in range(2, n):
        normed_in.append(line_step(after(tuple(normed_in[-1]), qkv) if s == 3 else normed_in[-1], s))
    for s in range(2, n - 1):
        normed, qkv = queries_chunk(middle[s - 2], normed_in[s - 1], w_qkv, bias_qkv, tables, (normed, qkv), n)
    act, slope = units_early(
        after(early, qkv), [own_normed] + flat(normed_in[:-1]), w_up, bias_up, width, n
    )
    def inner_step(pair, s):
        right, left = pair
        return [
            shift(right, [(i, i + 1) for i in range(s - 1, n - 2)]),
            shift(left, [(i, i - 1) for i in range(2, n - s + 1)]),
        ]

    def end_step(pair):
        right, left = pair
        return [shift(right, [(n - 2, n - 1)]), shift(left, [(1, 0)])]

    inner = [inner_step([after(cotangent, *normed_in[-2], early_qkv)] * 2, 1)]
    ready = after(tuple(inner[0]), *normed_in[-1], act)
    ends = [end_step([after(cotangent, *ready)] * 2)]
    inner.append(inner_step(ready, 2))
    cot_from = [cotangent]
    normed, qkv, act, slope = forward_chunk(late, normed_in[-1], *project, (normed, qkv, act, slope), n)

    att_half = attend(qkv, segc, segr, first, 0, 2, None)
    ends.append(end_step(after(tuple(ready), *ends[0], *inner[1], att_half[0])))
    att, lse = attend(qkv, segc, segr, first, 1, 2, att_half)
    for s in range(3, n):
        ready = after(tuple(inner[-1]), att)
        ends.append(end_step(ready))
        if s < n - 1:
            inner.append(inner_step(ready, s))
    for s in range(1, n - 1):
        for direction in range(2):
            cot_from += [inner[s - 1][direction], ends[s - 1][direction]]
    part = mix(att, act, w_out, w_down)
    bufs = backward_early(after(cot_early, part), cot_from, w_out, w_down, slope, n)
    block_sum = line_sum(after(part, bufs[2], *ends[-1]))
    cot, grad_att, grad_hid = backward_chunk(late, ends[-1], w_out, w_down, slope, bufs, n)
    orders = (bits, bits[::-1])

    def finish(pair, axis, *marks):
        for k in range(1, len(bits)):
            pair = halve([after(half, *marks) for half in pair], orders, k, pair)
        return jnp.concatenate([half[0].astype(F32) for half in pair], axis=axis)

    col_send = column_grads(send_where, att, act, cot, places)
    up_send, up_sum = row_grads(send_where, normed, [after(grad_hid, col_send)], count, places)
    grad_qkv = attend_back(
        qkv, after(grad_att, up_sum), att, lse, segc, segr, first, tables, 0, 1, None
    )
    col_came, up_came = swap(col_send, 0), swap(up_send, 0)
    part = grad_normed(grad_qkv, after(grad_hid, col_came, up_came), w_qkv, w_up, 0, depth)
    grad_sum = line_sum(after(part, block_sum))
    col_pair = column_grads(keep_where, att, act, after(cot, part), places, col_came)
    qkv_send, qkv_sum = row_grads(send_where, normed, after(tuple(grad_qkv), col_pair[0]), count, places)
    up_pair = row_grads(
        keep_where, normed, [after(grad_hid, qkv_sum)], count, places, up_came
    )
    col_pair = halve([after(c, up_pair[0]) for c in col_pair], orders, 0, col_pair)
    qkv_pair = row_grads(
        keep_where, after(normed, *col_pair), grad_qkv, count, places, swap(qkv_send, 0)
    )
    up_pair = halve([after(u, qkv_pair[0]) for u in up_pair], orders, 0, up_pair)
    qkv_kept = qkv_pair[0]
    qkv_pair = halve(qkv_pair, orders, 0)
    mixed = mixed_out(tokens, after(block_sum, *qkv_pair), (out_bias + fc2_bias)[None])
    input_grad, sums = norm_back(tokens, after(cotangent, mixed), [grad_sum], ln_gain[None])
    common = 3 * depth // 128
    pack = jnp.concatenate([a.reshape(-1, 128) for a in (sums[:3], up_sum[0], qkv_sum[0])])
    pack = jnp.pad(pack, ((0, -pack.shape[0] % 8), (0, 0)))
    pack = small_sums(pack, common)
    col_out, up_out, qkv_out = finish(col_pair, 0, qkv_kept), finish(up_pair, 1, *qkv_pair), finish(qkv_pair, 1)
    total = pack[:common].reshape(3, depth)
    ff_rows = up_sum.shape[1] // 128
    up_bias_grad = pack[common : common + ff_rows].reshape(-1)
    qkv_bias_grad = pack[common + ff_rows : common + ff_rows + 3 * width // 128].reshape(3, width)
    return (
        mixed,
        input_grad,
        qkv_out.reshape(-1, 3, width),
        qkv_bias_grad,
        col_out[:width],
        total[2],
        up_out,
        up_bias_grad,
        col_out[width:],
        total[2],
        total[0],
        total[1],
    )


def solution(mesh):
    in_specs = (
        P(("dp", "tensor"), None),
        P("dp", None),
        P(),
        P(),
        P("dp", None, "tensor"),
        P(None, "tensor"),
        P("tensor", "dp"),
        P(),
        P("dp", "tensor"),
        P("tensor"),
        P("tensor", "dp"),
        P(),
        P(("dp", "tensor"), None),
    )
    out_specs = (
        P(("dp", "tensor"), None),
        P(("dp", "tensor"), None),
        P("dp", None, "tensor"),
        P(None, "tensor"),
        P("tensor", "dp"),
        P(),
        P("dp", "tensor"),
        P("tensor"),
        P("tensor", "dp"),
        P(),
        P(),
        P(),
    )
    return jax.shard_map(local, mesh=mesh, in_specs=in_specs, out_specs=out_specs, check_vma=False)
```

```python
import functools

import jax
import jax.numpy as jnp
from jax import lax
from jax.experimental import pallas as pl
from jax.experimental.pallas import tpu as pltpu
from jax.sharding import PartitionSpec as P

HD = 64
ROT = 32
EPS = 1e-05
ROPE_BASE = 10000.0
NEGATIVE = -1e30
BLOCK = 256
ROWS = 256
SHRINK = 20

F32 = jnp.float32
BF16 = jnp.bfloat16


def dot_nn(a, b):
    return lax.dot_general(a, b, (((1,), (0,)), ((), ())), preferred_element_type=F32)


def dot_nt(a, b):
    return lax.dot_general(a, b, (((1,), (1,)), ((), ())), preferred_element_type=F32)


def dot_tn(a, b):
    return lax.dot_general(a, b, (((0,), (0,)), ((), ())), preferred_element_type=F32)


def cost(flops, moved, trans=0):
    return pl.CostEstimate(flops=int(flops / SHRINK), bytes_accessed=int(moved / SHRINK), transcendentals=0)


def whole(a):
    return pl.BlockSpec(a.shape, lambda *_: (0,) * a.ndim)


def seq_starts(segment_row):
    count = segment_row.shape[0]
    index = jnp.arange(count, dtype=jnp.int32)
    begins = jnp.concatenate([jnp.ones((1,), dtype=bool), segment_row[1:] != segment_row[:-1]])
    return lax.cummax(jnp.where(begins, index, jnp.zeros_like(index)), axis=0)


def rotary_tables(positions):
    half = ROT // 2
    lane = jnp.arange(128, dtype=jnp.int32) % HD
    frequency = ROPE_BASE ** (-((lane % half).astype(F32) * 2.0) / ROT)
    angles = positions.astype(F32)[:, None] * frequency[None, :]
    cosine = jnp.where(lane < ROT, jnp.cos(angles), 1.0)
    sine = jnp.sin(angles)
    sine_up = jnp.where(lane < half, -sine, 0.0)
    sine_down = jnp.where((lane >= half) & (lane < ROT), sine, 0.0)
    return cosine, sine_up, sine_down


def rotate(x, cosine, sine_up, sine_down):
    return (
        x * cosine
        + pltpu.roll(x, 128 - ROT // 2, axis=1) * sine_up
        + pltpu.roll(x, ROT // 2, axis=1) * sine_down
    )


def unrotate(x, cosine, sine_up, sine_down):
    return (
        x * cosine
        - pltpu.roll(x, 128 - ROT // 2, axis=1) * sine_up
        - pltpu.roll(x, ROT // 2, axis=1) * sine_down
    )


def norm_kernel(x_ref, gain_ref, shift_ref, o_ref):
    x = x_ref[...].astype(F32)
    centred = x - jnp.mean(x, axis=1, keepdims=True)
    inv_std = lax.rsqrt(jnp.mean(centred * centred, axis=1, keepdims=True) + EPS)
    o_ref[...] = (centred * inv_std * gain_ref[...] + shift_ref[...]).astype(BF16)


def norm(x, gain, shift):
    rows, width = x.shape
    step = rows // 2
    row = pl.BlockSpec((1, width), lambda i: (0, 0))
    tile = pl.BlockSpec((step, width), lambda i: (i, 0))
    return pl.pallas_call(
        norm_kernel,
        grid=(rows // step,),
        in_specs=[tile, row, row],
        out_specs=tile,
        out_shape=jax.ShapeDtypeStruct(x.shape, BF16),
        cost_estimate=cost(rows * width * 8, rows * width * 4),
        name="norm",
    )(x, gain, shift)


def norm_back_kernel(x_ref, cot_ref, *refs):
    gain_ref, o_ref, sums_ref = refs[-3:]

    @pl.when(pl.program_id(0) == 0)
    def _():
        sums_ref[...] = jnp.zeros_like(sums_ref)

    x = x_ref[...].astype(F32)
    centred = x - jnp.mean(x, axis=1, keepdims=True)
    inv_std = lax.rsqrt(jnp.mean(centred * centred, axis=1, keepdims=True) + EPS)
    normalized = centred * inv_std
    grad = jnp.concatenate([r[...] for r in refs[:-3]], axis=1).astype(F32)
    sums_ref[0:1, :] += jnp.sum(grad * normalized, axis=0, keepdims=True)
    sums_ref[1:2, :] += jnp.sum(grad, axis=0, keepdims=True)
    cot = cot_ref[...].astype(F32)
    sums_ref[2:3, :] += jnp.sum(cot, axis=0, keepdims=True)
    scaled = grad * gain_ref[...]
    first = jnp.mean(scaled, axis=1, keepdims=True)
    second = jnp.mean(scaled * normalized, axis=1, keepdims=True)
    o_ref[...] = (inv_std * (scaled - first - normalized * second) + cot).astype(BF16)


def norm_back(x, cot, grads, gain):
    rows, width = x.shape
    step = min(128, rows)
    tile = pl.BlockSpec((step, width), lambda i: (i, 0))
    return pl.pallas_call(
        norm_back_kernel,
        grid=(rows // step,),
        in_specs=[tile, tile]
        + [pl.BlockSpec((step, g.shape[1]), lambda i: (i, 0)) for g in grads]
        + [pl.BlockSpec((1, width), lambda i: (0, 0))],
        out_specs=[tile, pl.BlockSpec((8, width), lambda i: (0, 0))],
        out_shape=[jax.ShapeDtypeStruct(x.shape, BF16), jax.ShapeDtypeStruct((8, width), F32)],
        cost_estimate=cost(rows * width * 20, rows * width * 12),
        name="norm_back",
    )(x, cot, *grads, gain)


def pick(where_ref, i, tiles):
    turn = lax.div(i, tiles)
    busy = turn < where_ref[4]
    slot = jnp.where(busy, where_ref[2 * turn], where_ref[5])
    return jnp.where(busy, lax.rem(i, tiles), tiles - 1), slot, busy


def pick_shard(where_ref, i, tiles, refs, o_ref):
    turn = lax.div(i, tiles)
    if len(refs) == 1:
        o_ref[...] = refs[0][...]
        return

    @pl.when(where_ref[2 * turn + 1] == 0)
    def _():
        o_ref[...] = refs[0][...]

    @pl.when(where_ref[2 * turn + 1] == 1)
    def _():
        o_ref[...] = refs[1][...]


def project_tile(j, tall, x_ref, wq_ref, wu_ref, bq_ref, bu_ref, tables, qkv_ref, act_ref, slope_ref, over):
    if qkv_ref is not None:
        width = wq_ref.shape[1]

        @pl.when(j < 2)
        def _():
            scale = jnp.where(j == 0, HD**-0.5, 1.0).astype(F32)

            def turned(m, t):
                raw = (dot_nn(x_ref[m, :], wq_ref[...]) + bq_ref[...]) * scale
                turn = [r[t, :] for r in tables]
                for p in range(width // 128):
                    lanes = slice(p * 128, (p + 1) * 128)
                    qkv_ref[m, lanes] = rotate(raw[:, lanes], *turn).astype(BF16)

            over(turned)

        @pl.when(j == 2)
        def _():
            def plain(m, t):
                qkv_ref[m, :] = (dot_nn(x_ref[m, :], wq_ref[...]) + bq_ref[...]).astype(BF16)

            over(plain)

    if act_ref is not None:

        @pl.when(j > 2)
        def _():
            def gelu(m, t):
                act_ref[m, :], slope_ref[m, :] = gelu_and_slope(dot_nn(x_ref[m, :], wu_ref[...]) + bu_ref[...])

            over(gelu)


def gelu_and_slope(v):
    root = 0.7978845608028654
    cubic = 0.044715
    square = v * v
    t = jnp.tanh(v * (root + (root * cubic) * square))
    half = 0.5 + 0.5 * t
    slope = half + (v * (0.5 - 0.5 * (t * t))) * (root + (3.0 * root * cubic) * square)
    return (v * half).astype(BF16), slope.astype(BF16)


def forward_kernel(came, tiles, where_ref, *refs):
    x_refs, refs = refs[:came], refs[came:]
    wq_ref, wu_ref, bq_ref, bu_ref = refs[:4]
    tables = refs[4:7]
    normed_ref, qkv_ref, act_ref, slope_ref = refs[-4:]
    i = pl.program_id(0)
    j, _, busy = pick(where_ref, i, tiles)
    rows = normed_ref.shape[0]
    step = min(ROWS, rows)

    @pl.when(busy & (j == 0))
    def _():
        pick_shard(where_ref, i, tiles, x_refs, normed_ref)

    def over(act):
        for m in range(0, rows, step):
            act(slice(m, m + step), slice(m, m + step))

    @pl.when(busy)
    def _():
        project_tile(j, None, normed_ref, wq_ref, wu_ref, bq_ref, bu_ref, tables, qkv_ref, act_ref, slope_ref, over)


def queries_kernel(came, tiles, where_ref, *refs):
    x_refs, refs = refs[:came], refs[came:]
    wq_ref, bq_ref = refs[:2]
    tables = refs[2:5]
    normed_ref, qkv_ref = refs[-2:]
    i = pl.program_id(0)
    j, _, busy = pick(where_ref, i, tiles)
    rows = normed_ref.shape[0]
    step = min(ROWS, rows)

    @pl.when(busy & (j == 0))
    def _():
        pick_shard(where_ref, i, tiles, x_refs, normed_ref)

    def over(act):
        for m in range(0, rows, step):
            act(slice(m, m + step), slice(m, m + step))

    @pl.when(busy)
    def _():
        project_tile(j, None, normed_ref, wq_ref, None, bq_ref, None, tables, qkv_ref, None, None, over)


def queries_chunk(where, xs, wq, bq, tables, bufs, parts):
    rows, depth = xs[0].shape
    width = wq.shape[1] // 3
    tiles = 3

    def at(k):
        def index(i, w):
            j, slot, _ = pick(w, i, tiles)
            return ((slot, j), (0, j), (0, 0), (slot, 0), (jnp.minimum(slot, parts - 1), 0))[k]

        return index

    args = [where, *xs, wq, bq, *tables]
    return pl.pallas_call(
        functools.partial(queries_kernel, len(xs), tiles),
        grid_spec=pltpu.PrefetchScalarGridSpec(
            num_scalar_prefetch=1,
            grid=(len(xs) * tiles,),
            in_specs=[pl.BlockSpec((rows, depth), at(2))] * len(xs)
            + [pl.BlockSpec((depth, width), at(1)), pl.BlockSpec((1, width), at(1))]
            + [pl.BlockSpec((rows, 128), at(4))] * 3
            + [pl.BlockSpec(memory_space=pl.ANY)] * 2,
            out_specs=[pl.BlockSpec((rows, depth), at(3)), pl.BlockSpec((rows, width), at(0))],
        ),
        out_shape=[jax.ShapeDtypeStruct(b.shape, BF16) for b in bufs],
        input_output_aliases={len(args): 0, len(args) + 1: 1},
        cost_estimate=cost(6 * rows * depth * width, 6 * depth * width),
        name="queries_chunk",
    )(*args, *bufs)


def forward_chunk(where, xs, wq, wu, bq, bu, tables, bufs, parts):
    rows, depth = xs[0].shape
    width = wq.shape[1] // 3
    ff = wu.shape[1]
    tiles = 3 + ff // width

    def at(k):
        def index(i, w):
            j, slot, _ = pick(w, i, tiles)
            return (
                (slot, jnp.minimum(j, 2)),
                (slot, jnp.maximum(j - 3, 0)),
                (slot, 0),
                (0, jnp.minimum(j, 2)),
                (0, jnp.maximum(j - 3, 0)),
                (0, 0),
                (jnp.minimum(slot, parts - 1), 0),
            )[k]

        return index

    in_specs = (
        [pl.BlockSpec((rows, depth), at(5))] * len(xs)
        + [
            pl.BlockSpec((depth, width), at(3)),
            pl.BlockSpec((depth, width), at(4)),
            pl.BlockSpec((1, width), at(3)),
            pl.BlockSpec((1, width), at(4)),
        ]
        + [pl.BlockSpec((rows, 128), at(6))] * 3
    )
    total = (parts + 1) * rows
    shapes = [(total, depth), (total, 3 * width), (total, ff), (total, ff)]
    args = [where, *xs, wq, wu, bq, bu, *tables]
    aliases = {}
    if bufs is not None:
        aliases = {len(args) + k: k for k in range(4)}
        args += list(bufs)
        in_specs += [pl.BlockSpec(memory_space=pl.ANY)] * 4
    return pl.pallas_call(
        functools.partial(forward_kernel, len(xs), tiles),
        grid_spec=pltpu.PrefetchScalarGridSpec(
            num_scalar_prefetch=1,
            grid=(len(xs) * tiles,),
            in_specs=in_specs,
            out_specs=[
                pl.BlockSpec((rows, depth), at(2)),
                pl.BlockSpec((rows, width), at(0)),
                pl.BlockSpec((rows, width), at(1)),
                pl.BlockSpec((rows, width), at(1)),
            ],
        ),
        out_shape=[jax.ShapeDtypeStruct(s, BF16) for s in shapes],
        input_output_aliases=aliases,
        cost_estimate=cost(2 * rows * depth * (3 * width + ff), 2 * depth * (3 * width + ff)),
        name="forward_chunk",
    )(*args)


def collect(where_ref, came, shards, x_refs, held_ref, full_ref, in_sems, out_sems, first, last):
    rows = x_refs[0].shape[0]

    def spot(c):
        return pl.ds(pl.multiple_of(where_ref[1 + shards + 2 * c] * rows, rows), rows)

    def loads(c):
        return pltpu.make_async_copy(x_refs[c], held_ref.at[spot(c)], in_sems.at[c])

    def stores(c):
        return pltpu.make_async_copy(held_ref.at[spot(c)], full_ref.at[spot(c)], out_sems.at[c])

    def each(act):
        for c in range(came):
            pl.when(where_ref[2 + shards + 2 * c] > 0)(functools.partial(act, c))

    @pl.when(first)
    def _():
        each(lambda c: loads(c).start())
        each(lambda c: loads(c).wait())
        if full_ref is not None:
            each(lambda c: stores(c).start())

    def finish():
        pl.when(last)(lambda: each(lambda c: stores(c).wait()))

    return finish


def early_over(where_ref, rows):
    step = min(ROWS, rows)

    def over(act):
        def body(t, carry):
            for m in range(0, rows, step):
                at = pl.ds(pl.multiple_of(where_ref[1 + t] * rows + m, step), step)
                act(at, at)
            return carry

        lax.fori_loop(0, where_ref[0], body, 0)

    return over


def queries_early_kernel(came, shards, where_ref, *refs):
    x_refs, refs = refs[:came], refs[came:]
    wq_ref, bq_ref = refs[:2]
    tables = refs[2:5]
    normed_ref, qkv_ref, held_ref, in_sems, out_sems = refs[5:]
    j = pl.program_id(0)
    finish = collect(
        where_ref, came, shards, x_refs, held_ref, normed_ref, in_sems, out_sems,
        j == 0, j == pl.num_programs(0) - 1,
    )
    over = early_over(where_ref, x_refs[0].shape[0])
    project_tile(j, None, held_ref, wq_ref, None, bq_ref, None, tables, qkv_ref, None, None, over)
    finish()


def units_early_kernel(came, shards, where_ref, *refs):
    x_refs, refs = refs[:came], refs[came:]
    wu_ref, bu_ref, act_ref, slope_ref, held_ref, in_sems = refs
    j = pl.program_id(0)
    collect(where_ref, came, shards, x_refs, held_ref, None, in_sems, None, j == 0, None)
    over = early_over(where_ref, x_refs[0].shape[0])
    project_tile(j + 3, None, held_ref, None, wu_ref, None, bu_ref, None, None, act_ref, slope_ref, over)


def queries_early(where, xs, wq, bq, tables, parts):
    rows, depth = xs[0].shape
    width = wq.shape[1] // 3
    count = parts * rows
    in_place = pl.BlockSpec(memory_space=pl.ANY)
    return pl.pallas_call(
        functools.partial(queries_early_kernel, len(xs), parts),
        grid_spec=pltpu.PrefetchScalarGridSpec(
            num_scalar_prefetch=1,
            grid=(3,),
            in_specs=[in_place] * len(xs)
            + [pl.BlockSpec((depth, width), lambda j, w: (0, j)), pl.BlockSpec((1, width), lambda j, w: (0, j))]
            + [whole(t) for t in tables],
            out_specs=[in_place, pl.BlockSpec((count, width), lambda j, w: (0, j))],
            scratch_shapes=[
                pltpu.VMEM((count, depth), BF16),
                pltpu.SemaphoreType.DMA((len(xs),)),
                pltpu.SemaphoreType.DMA((len(xs),)),
            ],
        ),
        out_shape=[
            jax.ShapeDtypeStruct((count + rows, depth), BF16),
            jax.ShapeDtypeStruct((count + rows, 3 * width), BF16),
        ],
        cost_estimate=cost(6 * count * depth * width, 6 * depth * width),
        name="queries_early",
    )(where, *xs, wq, bq, *tables)


def units_early(where, xs, wu, bu, width, parts):
    rows, depth = xs[0].shape
    ff = wu.shape[1]
    count = parts * rows
    return pl.pallas_call(
        functools.partial(units_early_kernel, len(xs), parts),
        grid_spec=pltpu.PrefetchScalarGridSpec(
            num_scalar_prefetch=1,
            grid=(ff // width,),
            in_specs=[pl.BlockSpec(memory_space=pl.ANY)] * len(xs)
            + [pl.BlockSpec((depth, width), lambda j, w: (0, j)), pl.BlockSpec((1, width), lambda j, w: (0, j))],
            out_specs=[pl.BlockSpec((count, width), lambda j, w: (0, j))] * 2,
            scratch_shapes=[pltpu.VMEM((count, depth), BF16), pltpu.SemaphoreType.DMA((len(xs),))],
        ),
        out_shape=[jax.ShapeDtypeStruct((count + rows, ff), BF16)] * 2,
        cost_estimate=cost(2 * count * depth * ff, 2 * depth * ff),
        name="units_early",
    )(where, *xs, wu, bu)


def backward_early_kernel(came, shards, where_ref, *refs):
    c_refs, refs = refs[:came], refs[came:]
    wo_ref, wd_ref, slope_ref, cot_ref, ga_ref, gh_ref, held_ref, in_sems, out_sems = refs
    j = pl.program_id(0)
    finish = collect(
        where_ref, came, shards, c_refs, held_ref, cot_ref, in_sems, out_sems,
        j == 0, j == pl.num_programs(0) - 1,
    )
    rows = c_refs[0].shape[0]
    step = min(ROWS, rows)

    def over(act):
        def body(t, carry):
            for m in range(0, rows, step):
                act(pl.ds(pl.multiple_of(where_ref[1 + t] * rows + m, step), step))
            return carry

        lax.fori_loop(0, where_ref[0], body, 0)

    @pl.when(j == 0)
    def _():
        weight = side_by_side(wo_ref)

        def act(m):
            ga_ref[m, :] = dot_nt(held_ref[m, :], weight).astype(BF16)

        over(act)

    @pl.when(j > 0)
    def _():
        weight = side_by_side(wd_ref)

        def act(m):
            gh_ref[m, :] = (dot_nt(held_ref[m, :], weight) * slope_ref[m, :].astype(F32)).astype(BF16)

        over(act)

    finish()


def backward_early(where, cots, wo, wd, slope, parts):
    rows, depth = cots[0].shape
    pieces, width, piece = wo.shape
    ff = wd.shape[1]
    count = parts * rows
    total = count + rows
    in_place = pl.BlockSpec(memory_space=pl.ANY)

    def tile(j):
        return jnp.maximum(j - 1, 0)

    return pl.pallas_call(
        functools.partial(backward_early_kernel, len(cots), parts),
        grid_spec=pltpu.PrefetchScalarGridSpec(
            num_scalar_prefetch=1,
            grid=(1 + ff // width,),
            in_specs=[in_place] * len(cots)
            + [
                whole(wo),
                pl.BlockSpec((pieces, width, piece), lambda j, w: (0, tile(j), 0)),
                pl.BlockSpec((count, width), lambda j, w: (0, tile(j))),
            ],
            out_specs=[
                in_place,
                pl.BlockSpec((count, width), lambda j, w: (0, 0)),
                pl.BlockSpec((count, width), lambda j, w: (0, tile(j))),
            ],
            scratch_shapes=[
                pltpu.VMEM((count, depth), BF16),
                pltpu.SemaphoreType.DMA((len(cots),)),
                pltpu.SemaphoreType.DMA((len(cots),)),
            ],
        ),
        out_shape=[jax.ShapeDtypeStruct(s, BF16) for s in ((total, depth), (total, width), (total, ff))],
        cost_estimate=cost(2 * count * depth * (width + ff), 2 * depth * (width + ff)),
        name="backward_early",
    )(where, *cots, wo, wd, slope)


def low_lanes(rows):
    return lax.broadcasted_iota(jnp.int32, (rows, 128), 1) < HD


def attend_kernel(
    skipped, first_ref, q_ref, k_ref, v_ref, segc_ref, segr_ref, *refs
):
    o_ref, lse_ref, max_ref, acc_ref, bias_ref = refs[-5:]
    i = pl.program_id(0) + skipped
    block, width = q_ref.shape
    pairs = width // 128
    low = low_lanes(block)
    owns = (low, jnp.logical_not(low))
    max_ref[...] = jnp.full_like(max_ref, NEGATIVE)
    lse_ref[...] = jnp.zeros_like(lse_ref)
    acc_ref[...] = jnp.zeros_like(acc_ref)
    q0 = pl.multiple_of(i * block, block)
    query_seg = segr_ref[:, pl.ds(q0, block)]
    query_row = q0 + lax.broadcasted_iota(jnp.int32, (1, block), 1)

    def set_bias(k0):
        key_seg = segc_ref[pl.ds(k0, block), :]
        key_row = k0 + lax.broadcasted_iota(jnp.int32, (block, 1), 0)
        bias_ref[...] = jnp.where((key_seg == query_seg) & (key_row <= query_row), 0.0, NEGATIVE)

    def scores(k0, p, h):
        lanes = slice(p * 128, (p + 1) * 128)
        q = q_ref[:, lanes]
        mine = jnp.where(owns[h], q, jnp.zeros_like(q))
        return dot_nt(k_ref[pl.ds(k0, block), lanes], mine) + bias_ref[...]

    def find_max(j, carry):
        k0 = pl.multiple_of(j * block, block)
        set_bias(k0)
        for p in range(pairs):
            for h in range(2):
                s = scores(k0, p, h)
                max_ref[2 * p + h] = jnp.maximum(max_ref[2 * p + h], jnp.max(s, axis=0, keepdims=True))
        return carry

    lax.fori_loop(first_ref[i], i + 1, find_max, 0)

    def add_up(j, carry):
        k0 = pl.multiple_of(j * block, block)
        set_bias(k0)
        for p in range(pairs):
            v = v_ref[pl.ds(k0, block), p * 128 : (p + 1) * 128]
            for h in range(2):
                e = jnp.exp(scores(k0, p, h) - max_ref[2 * p + h])
                lse_ref[p, h : h + 1, :] += jnp.sum(e, axis=0, keepdims=True)
                acc_ref[2 * p + h] += dot_tn(e.astype(BF16), jnp.where(owns[h], v, jnp.ones_like(v)))
        return carry

    lax.fori_loop(first_ref[i], i + 1, add_up, 0)
    for p in range(pairs):
        even, odd = acc_ref[2 * p], acc_ref[2 * p + 1]
        o_ref[:, p * 128 : (p + 1) * 128] = jnp.where(
            low, even / pltpu.roll(even, HD, axis=1), odd / pltpu.roll(odd, HD, axis=1)
        ).astype(BF16)
        for h in range(2):
            lse_ref[p, h : h + 1, :] = max_ref[2 * p + h] + jnp.log(lse_ref[p, h : h + 1, :])


def attend(qkv, segc, segr, first, part, parts, bufs):
    count = segr.shape[1]
    width = qkv.shape[1] // 3
    pairs = width // 128
    steps = count // BLOCK // parts
    skipped = part * steps
    in_place = [] if bufs is None else [pl.BlockSpec(memory_space=pl.ANY)] * 2
    return pl.pallas_call(
        functools.partial(attend_kernel, skipped),
        grid_spec=pltpu.PrefetchScalarGridSpec(
            num_scalar_prefetch=1,
            grid=(steps,),
            in_specs=[
                pl.BlockSpec((BLOCK, width), lambda i, f: (i + skipped, 0)),
                pl.BlockSpec((count, width), lambda i, f: (0, 1)),
                pl.BlockSpec((count, width), lambda i, f: (0, 2)),
                whole(segc),
                whole(segr),
            ]
            + in_place,
            out_specs=[
                pl.BlockSpec((BLOCK, width), lambda i, f: (i + skipped, 0)),
                pl.BlockSpec((pairs, 8, BLOCK), lambda i, f: (0, 0, i + skipped)),
            ],
            scratch_shapes=[
                pltpu.VMEM((2 * pairs, 1, BLOCK), F32),
                pltpu.VMEM((2 * pairs, BLOCK, 128), F32),
                pltpu.VMEM((BLOCK, BLOCK), F32),
            ],
        ),
        out_shape=[
            jax.ShapeDtypeStruct((count, width), BF16),
            jax.ShapeDtypeStruct((pairs, 8, count), F32),
        ],
        input_output_aliases={} if bufs is None else {6: 0, 7: 1},
        cost_estimate=cost(30e9 * width / 512, count * width * 8),
        name="attend",
    )(first, qkv, qkv, qkv, segc, segr, *([] if bufs is None else bufs))


def attend_back_kernel(
    first_ref, q_ref, k_ref, v_ref, go_ref, o_ref, lse_ref, segc_ref, segr_ref,
    cos_ref, up_ref, down_ref, *refs,
):
    gq_ref, gk_ref, gv_ref, dq_ref, dk_ref, dv_ref, bias_ref = refs[-7:]
    i = pl.program_id(0)
    steps = pl.num_programs(0)
    block, width = q_ref.shape
    pairs = width // 128
    low = low_lanes(block)
    owns = (low, jnp.logical_not(low))

    @pl.when(i == 0)
    def _():
        dk_ref[...] = jnp.zeros_like(dk_ref)
        dv_ref[...] = jnp.zeros_like(dv_ref)

    dq_ref[...] = jnp.zeros_like(dq_ref)
    q0 = pl.multiple_of(i * block, block)
    query_seg = segr_ref[:, pl.ds(q0, block)]
    query_row = q0 + lax.broadcasted_iota(jnp.int32, (1, block), 1)
    half = jnp.where(
        lax.broadcasted_iota(jnp.int32, (8, 128), 1) // HD == lax.broadcasted_iota(jnp.int32, (8, 128), 0),
        1.0,
        0.0,
    ).astype(F32)
    inner = []
    for p in range(pairs):
        lanes = slice(p * 128, (p + 1) * 128)
        product = go_ref[:, lanes].astype(F32) * o_ref[:, lanes].astype(F32)
        inner.append(
            lax.dot_general(
                half, product, (((1,), (1,)), ((), ())),
                precision=lax.Precision.HIGHEST, preferred_element_type=F32,
            )
        )

    def body(j, carry):
        k0 = pl.multiple_of(j * block, block)
        key_seg = segc_ref[pl.ds(k0, block), :]
        key_row = k0 + lax.broadcasted_iota(jnp.int32, (block, 1), 0)
        bias_ref[...] = jnp.where((key_seg == query_seg) & (key_row <= query_row), 0.0, NEGATIVE)
        for p in range(pairs):
            lanes = slice(p * 128, (p + 1) * 128)
            k = k_ref[pl.ds(k0, block), lanes]
            v = v_ref[pl.ds(k0, block), lanes]
            q = q_ref[:, lanes]
            go = go_ref[:, lanes]
            sums = None
            for h in range(2):
                q_own, go_own, k_own = [jnp.where(owns[h], a, jnp.zeros_like(a)) for a in (q, go, k)]
                prob = jnp.exp(dot_nt(k, q_own) + bias_ref[...] - lse_ref[p, h : h + 1, :])
                grad_score = (prob * (dot_nt(v, go_own) - inner[p][h : h + 1, :])).astype(BF16)
                new = (
                    dot_nn(prob.astype(BF16), go_own),
                    dot_nn(grad_score, q_own),
                    dot_tn(grad_score, k_own),
                )
                sums = new if sums is None else tuple(a + b for a, b in zip(sums, new))
            dv_ref[pl.ds(k0, block), lanes] += sums[0]
            dk_ref[pl.ds(k0, block), lanes] += sums[1]
            dq_ref[:, lanes] += sums[2]
        return carry

    lax.fori_loop(first_ref[i], i + 1, body, 0)
    turn = [r[pl.ds(q0, block), :] for r in (cos_ref, up_ref, down_ref)]
    for p in range(pairs):
        lanes = slice(p * 128, (p + 1) * 128)
        gq_ref[:, lanes] = unrotate(dq_ref[:, lanes] * HD**-0.5, *turn).astype(BF16)

    @pl.when(i == steps - 1)
    def _():
        def finish(j, carry):
            k0 = pl.multiple_of(j * block, block)
            rows = pl.ds(k0, block)
            turn = [r[rows, :] for r in (cos_ref, up_ref, down_ref)]
            for p in range(pairs):
                lanes = slice(p * 128, (p + 1) * 128)
                gk_ref[rows, lanes] = unrotate(dk_ref[rows, lanes], *turn).astype(BF16)
                gv_ref[rows, lanes] = dv_ref[rows, lanes].astype(BF16)
            return carry

        lax.fori_loop(0, steps, finish, 0)


def attend_back(qkv, grad_out, out, lse, segc, segr, first, tables, part, parts, bufs):
    count = segr.shape[1]
    whole_width = qkv.shape[1] // 3
    width = whole_width // parts
    pairs = width // 128
    row_tile = pl.BlockSpec((BLOCK, width), lambda i, f: (i, part))
    column = pl.BlockSpec((count, width), lambda i, f: (0, part))
    in_place = [] if bufs is None else [pl.BlockSpec(memory_space=pl.ANY)] * 3
    args = [first, qkv, qkv, qkv, grad_out, out, lse, segc, segr, *tables]
    return pl.pallas_call(
        attend_back_kernel,
        grid_spec=pltpu.PrefetchScalarGridSpec(
            num_scalar_prefetch=1,
            grid=(count // BLOCK,),
            in_specs=[
                row_tile,
                pl.BlockSpec((count, width), lambda i, f: (0, parts + part)),
                pl.BlockSpec((count, width), lambda i, f: (0, 2 * parts + part)),
                row_tile,
                row_tile,
                pl.BlockSpec((pairs, 8, BLOCK), lambda i, f: (part, 0, i)),
                whole(segc),
                whole(segr),
                *[whole(t) for t in tables],
            ]
            + in_place,
            out_specs=[row_tile, column, column],
            scratch_shapes=[
                pltpu.VMEM((BLOCK, width), F32),
                pltpu.VMEM((count, width), F32),
                pltpu.VMEM((count, width), F32),
                pltpu.VMEM((BLOCK, BLOCK), F32),
            ],
        ),
        out_shape=[jax.ShapeDtypeStruct((count, whole_width), BF16)] * 3,
        input_output_aliases={} if bufs is None else {len(args) + k: k for k in range(3)},
        cost_estimate=cost(44e9 * width / 512, count * width * 20),
        name="attend_back",
    )(*args, *([] if bufs is None else bufs))


def side_by_side(ref):
    return jnp.concatenate([ref[b] for b in range(ref.shape[0])], axis=1)


def mix_kernel(att_ref, act_ref, wo_ref, wd_ref, o_ref):
    wo, wd = side_by_side(wo_ref), side_by_side(wd_ref)
    step = min(512, att_ref.shape[0])
    for m in range(0, att_ref.shape[0], step):
        rs = slice(m, m + step)
        o_ref[rs, :] = (dot_nn(att_ref[rs, :], wo) + dot_nn(act_ref[rs, :], wd)).astype(BF16)


def mix(att, act, wo, wd):
    pieces, width, piece = wo.shape
    ff = wd.shape[1]
    count = att.shape[0]
    group = max(1, 512 // piece)
    return pl.pallas_call(
        mix_kernel,
        grid=(pieces // group,),
        in_specs=[
            pl.BlockSpec((count, width), lambda j: (0, 0)),
            pl.BlockSpec((count, ff), lambda j: (0, 0)),
            pl.BlockSpec((group, width, piece), lambda j: (j, 0, 0)),
            pl.BlockSpec((group, ff, piece), lambda j: (j, 0, 0)),
        ],
        out_specs=pl.BlockSpec((count, group * piece), lambda j: (0, j)),
        out_shape=jax.ShapeDtypeStruct((count, pieces * piece), BF16),
        cost_estimate=cost(2 * count * (width + ff) * pieces * piece, 4 * count * ff),
        name="mix",
    )(att, act, wo, wd)


def mixed_kernel(x_ref, sum_ref, bias_ref, o_ref):
    o_ref[...] = (x_ref[...].astype(F32) + sum_ref[...].astype(F32) + bias_ref[...]).astype(BF16)


def mixed_out(x, total, bias):
    rows, width = x.shape
    step = min(256, rows)
    tile = pl.BlockSpec((step, width), lambda i: (i, 0))
    return pl.pallas_call(
        mixed_kernel,
        grid=(rows // step,),
        in_specs=[tile, tile, pl.BlockSpec((1, width), lambda i: (0, 0))],
        out_specs=tile,
        out_shape=jax.ShapeDtypeStruct(x.shape, BF16),
        cost_estimate=cost(rows * width * 4, rows * width * 6),
        name="mixed_out",
    )(x, total, bias)


def backward_kernel(came, tiles, where_ref, *refs):
    c_refs, refs = refs[:came], refs[came:]
    wo_ref, wd_ref, slope_ref = refs[:3]
    cot_ref, ga_ref, gh_ref = refs[-3:]
    i = pl.program_id(0)
    j, _, busy = pick(where_ref, i, tiles)
    rows = cot_ref.shape[0]
    step = min(ROWS, rows)

    @pl.when(busy & (j == 0))
    def _():
        pick_shard(where_ref, i, tiles, c_refs, cot_ref)
        weight = side_by_side(wo_ref)
        for m in range(0, rows, step):
            ga_ref[m : m + step, :] = dot_nt(cot_ref[m : m + step, :], weight).astype(BF16)

    @pl.when(busy & (j > 0))
    def _():
        weight = side_by_side(wd_ref)
        for m in range(0, rows, step):
            gh_ref[m : m + step, :] = (
                dot_nt(cot_ref[m : m + step, :], weight) * slope_ref[m : m + step, :].astype(F32)
            ).astype(BF16)


def backward_chunk(where, cots, wo, wd, slope, bufs, parts):
    rows, depth = cots[0].shape
    pieces, width, piece = wo.shape
    ff = wd.shape[1]
    tiles = 1 + ff // width

    def at(k):
        def index(i, w):
            j, slot, _ = pick(w, i, tiles)
            return ((0, 0), (0, jnp.maximum(j - 1, 0), 0), (slot, jnp.maximum(j - 1, 0)), (slot, 0))[k]

        return index

    in_specs = [pl.BlockSpec((rows, depth), at(0))] * len(cots) + [
        whole(wo),
        pl.BlockSpec((pieces, width, piece), at(1)),
        pl.BlockSpec((rows, width), at(2)),
    ]
    total = (parts + 1) * rows
    shapes = [(total, depth), (total, width), (total, ff)]
    args = [where, *cots, wo, wd, slope]
    aliases = {}
    if bufs is not None:
        aliases = {len(args) + k: k for k in range(3)}
        args += list(bufs)
        in_specs += [pl.BlockSpec(memory_space=pl.ANY)] * 3
    return pl.pallas_call(
        functools.partial(backward_kernel, len(cots), tiles),
        grid_spec=pltpu.PrefetchScalarGridSpec(
            num_scalar_prefetch=1,
            grid=(len(cots) * tiles,),
            in_specs=in_specs,
            out_specs=[
                pl.BlockSpec((rows, depth), at(3)),
                pl.BlockSpec((rows, width), at(3)),
                pl.BlockSpec((rows, width), at(2)),
            ],
        ),
        out_shape=[jax.ShapeDtypeStruct(s, BF16) for s in shapes],
        input_output_aliases=aliases,
        cost_estimate=cost(2 * rows * depth * (width + ff), 2 * depth * (width + ff)),
        name="backward_chunk",
    )(*args)


def grad_kernel(gq_ref, gk_ref, gv_ref, gh_ref, wq_ref, wu_ref, o_ref):
    step = min(512, gq_ref.shape[0])
    width = gq_ref.shape[1]
    for m in range(0, gq_ref.shape[0], step):
        rs = slice(m, m + step)
        left = jnp.concatenate([r[rs, :] for r in (gq_ref, gk_ref, gv_ref)], axis=1)
        o_ref[rs, :] = (dot_nt(left, wq_ref[...]) + dot_nt(gh_ref[rs, :], wu_ref[...])).astype(BF16)


def grad_normed(gqkv, gh, wq, wu, start, stop):
    count, width = gqkv[0].shape
    ff = gh.shape[1]
    tile = min(256, stop - start)
    first = start // tile
    return pl.pallas_call(
        grad_kernel,
        grid=((stop - start) // tile,),
        in_specs=[once((count, width))] * 3
        + [
            once((count, ff)),
            pl.BlockSpec((tile, wq.shape[1]), lambda j: (first + j, 0)),
            pl.BlockSpec((tile, wu.shape[1]), lambda j: (first + j, 0)),
        ],
        out_specs=pl.BlockSpec((count, tile), lambda j: (0, j)),
        out_shape=jax.ShapeDtypeStruct((count, stop - start), BF16),
        cost_estimate=cost(2 * count * (stop - start) * (3 * width + ff), 4 * count * ff),
        name="grad_normed",
    )(*gqkv, gh, wq, wu)


def put_columns(att_ref, act_ref, cot, o_ref, start, stop, add):
    width = att_ref.shape[1]
    at = start
    while at < stop:
        if at < width:
            end = min(stop, width)
            left = att_ref[:, at:end]
        else:
            end = min(stop, at + 512)
            left = act_ref[:, at - width : end - width]
        rows = slice(at - start, end - start)
        total = dot_tn(left, cot)
        if add is not None:
            total = total + add[0, rows, :].astype(F32)
        o_ref[0, rows, :] = total.astype(BF16)
        at = end


def columns_send_kernel(where_ref, att_ref, act_ref, c_ref, o_ref):
    put_columns(att_ref, act_ref, c_ref[...], o_ref, 0, o_ref.shape[1], None)


def columns_keep_kernel(where_ref, att_ref, act_ref, c_ref, came_ref, a_ref, b_ref):
    half = a_ref.shape[1]
    first = pl.program_id(0) < pl.num_programs(0) // 2

    @pl.when(first)
    def _():
        put_columns(att_ref, act_ref, c_ref[...], a_ref, 0, half, came_ref)

    @pl.when(jnp.logical_not(first))
    def _():
        put_columns(att_ref, act_ref, c_ref[...], b_ref, half, 2 * half, came_ref)


def rows_send_kernel(arrays, where_ref, x_ref, *refs):
    g_refs, o_ref, sum_ref = refs[:arrays], refs[-2], refs[-1]
    x = x_ref[...]
    first = pl.program_id(0) == 0
    start = 0
    for g_ref in g_refs:
        width = g_ref.shape[1]
        step = min(512, width)
        for m in range(0, width, step):
            o_ref[0, :, start + m : start + m + step] = dot_tn(x, g_ref[:, m : m + step]).astype(BF16)

        @pl.when(first)
        def _():
            ones = jnp.ones((8, g_ref.shape[0]), BF16)
            for m in range(0, width, step):
                sum_ref[:, start + m : start + m + step] = dot_nn(ones, g_ref[:, m : m + step])

        start += width


def rows_keep_kernel(arrays, where_ref, x_ref, *refs):
    g_refs, came_ref, a_ref, b_ref = refs[:arrays], *refs[arrays:]
    first = pl.program_id(0) < pl.num_programs(0) // 2
    x = x_ref[...]
    half = a_ref.shape[2]

    def put(o_ref, low):
        start = 0
        for g_ref in g_refs:
            width = g_ref.shape[1]
            at = max(start, low)
            while at < min(start + width, low + half):
                end = min(start + width, low + half, at + 512)
                o_ref[0, :, at - low : end - low] = (
                    dot_tn(x, g_ref[:, at - start : end - start])
                    + came_ref[0, :, at - low : end - low].astype(F32)
                ).astype(BF16)
                at = end
            start += width

    pl.when(first)(lambda: put(a_ref, 0))
    pl.when(jnp.logical_not(first))(lambda: put(b_ref, half))


def once(shape):
    return pl.BlockSpec(shape, lambda *_: (0,) * len(shape), pipeline_mode=pl.Buffered(1))


def column_grads(where, att, act, cot, places, came=None):
    count, width = att.shape
    ff = act.shape[1]
    piece = cot.shape[1] // (2 * places)
    flops = 2 * count * (width + ff) * piece * places
    base = [once((count, width)), once((count, ff)), pl.BlockSpec((count, piece), lambda t, w: (0, w[t]))]
    if came is None:
        return pl.pallas_call(
            columns_send_kernel,
            grid_spec=pltpu.PrefetchScalarGridSpec(
                num_scalar_prefetch=1,
                grid=(places,),
                in_specs=base,
                out_specs=pl.BlockSpec((1, width + ff, piece), lambda t, w: (t, 0, 0)),
            ),
            out_shape=jax.ShapeDtypeStruct((places, width + ff, piece), BF16),
            cost_estimate=cost(flops, 2 * count * (width + ff)),
            name="columns_send",
        )(where, att, act, cot)
    half = (width + ff) // 2
    turns = 2 * places
    return pl.pallas_call(
        columns_keep_kernel,
        grid_spec=pltpu.PrefetchScalarGridSpec(
            num_scalar_prefetch=1,
            grid=(turns,),
            in_specs=base
            + [pl.BlockSpec((1, half, piece), lambda t, w: (w[turns + t], t // places, 0))],
            out_specs=[
                pl.BlockSpec((1, half, piece), lambda t, w: (jnp.minimum(t, places - 1), 0, 0)),
                pl.BlockSpec((1, half, piece), lambda t, w: (jnp.maximum(t - places, 0), 0, 0)),
            ],
        ),
        out_shape=[jax.ShapeDtypeStruct((places, half, piece), BF16)] * 2,
        cost_estimate=cost(flops, 2 * count * (width + ff)),
        name="columns_keep",
    )(where, att, act, cot, came)


def row_grads(where, x, gs, count, places, came=None):
    width = sum(g.shape[1] for g in gs)
    piece = x.shape[1] // (2 * places)
    flops = 2 * count * width * piece * places
    base = [pl.BlockSpec((count, piece), lambda t, w: (0, w[t]))] + [once((count, g.shape[1])) for g in gs]
    if came is None:
        return pl.pallas_call(
            functools.partial(rows_send_kernel, len(gs)),
            grid_spec=pltpu.PrefetchScalarGridSpec(
                num_scalar_prefetch=1,
                grid=(places,),
                in_specs=base,
                out_specs=[
                    pl.BlockSpec((1, piece, width), lambda t, w: (t, 0, 0)),
                    pl.BlockSpec((8, width), lambda t, w: (0, 0)),
                ],
            ),
            out_shape=[
                jax.ShapeDtypeStruct((places, piece, width), BF16),
                jax.ShapeDtypeStruct((8, width), F32),
            ],
            cost_estimate=cost(flops, 2 * count * width),
            name="rows_send",
        )(where, x, *gs)
    half = width // 2
    turns = 2 * places
    return pl.pallas_call(
        functools.partial(rows_keep_kernel, len(gs)),
        grid_spec=pltpu.PrefetchScalarGridSpec(
            num_scalar_prefetch=1,
            grid=(turns,),
            in_specs=base
            + [pl.BlockSpec((1, piece, half), lambda t, w: (w[turns + t], 0, t // places))],
            out_specs=[
                pl.BlockSpec((1, piece, half), lambda t, w: (jnp.minimum(t, places - 1), 0, 0)),
                pl.BlockSpec((1, piece, half), lambda t, w: (jnp.maximum(t - places, 0), 0, 0)),
            ],
        ),
        out_shape=[jax.ShapeDtypeStruct((places, piece, half), BF16)] * 2,
        cost_estimate=cost(flops, 2 * count * width),
        name="rows_keep",
    )(where, x, *gs, came)


def after(value, *marks):
    return lax.optimization_barrier((value, *marks))[0]


def swap(x, bit):
    size = lax.axis_size("dp")
    return lax.ppermute(x, "dp", [(i, i ^ (1 << bit)) for i in range(size)])


def halve(xs, orders, k, sent=None):
    kept = []
    for x, y, bits in zip(xs, sent or xs, orders):
        rest = x.shape[0] // 2
        came = swap(y[rest:], bits[k])
        total = x[:rest].astype(F32) + came.astype(F32)
        kept.append(total if k == len(bits) - 1 else total.astype(BF16))
    return kept


def small_sum_kernel(phases, x_ref, o_ref, sent_ref, came_ref, send_sems, came_sems):
    barrier = pltpu.get_barrier_semaphore()

    def partner(axis, bit):
        return {axis: lax.axis_index(axis) ^ (1 << bit)}

    for axis, bit, _ in phases:
        pl.semaphore_signal(
            barrier, inc=1, device_id=partner(axis, bit), device_id_type=pl.DeviceIdType.MESH
        )
    pl.semaphore_wait(barrier, len(phases))
    sent_ref[0] = x_ref[...]
    for k, (axis, bit, rows) in enumerate(phases):
        span = pl.ds(0, rows)
        copy = pltpu.make_async_remote_copy(
            src_ref=sent_ref.at[k, span],
            dst_ref=came_ref.at[k, span],
            send_sem=send_sems.at[k],
            recv_sem=came_sems.at[k],
            device_id=partner(axis, bit),
            device_id_type=pl.DeviceIdType.MESH,
        )
        copy.start()
        copy.wait()
        total = sent_ref[k, 0:rows] + came_ref[k, 0:rows]
        if k == len(phases) - 1:
            o_ref[...] = sent_ref[k]
            o_ref[0:rows] = total
        else:
            sent_ref[k + 1] = sent_ref[k]
            sent_ref[k + 1, 0:rows] = total


def small_sums(x, common):
    rows = x.shape[0]
    phases = []
    for axis, height in (("dp", rows), ("tensor", common)):
        for bit in range(lax.axis_size(axis).bit_length() - 1):
            phases.append((axis, bit, height))
    return pl.pallas_call(
        functools.partial(small_sum_kernel, phases),
        in_specs=[pl.BlockSpec(memory_space=pltpu.VMEM)],
        out_specs=pl.BlockSpec(memory_space=pltpu.VMEM),
        out_shape=jax.ShapeDtypeStruct(x.shape, F32),
        scratch_shapes=[
            pltpu.VMEM((len(phases), *x.shape), F32),
            pltpu.VMEM((len(phases), *x.shape), F32),
            pltpu.SemaphoreType.DMA((len(phases),)),
            pltpu.SemaphoreType.DMA((len(phases),)),
        ],
        compiler_params=pltpu.CompilerParams(collective_id=0, has_side_effects=True),
        name="small_sums",
    )(x)


def local(
    tokens, segments, ln_gain, ln_shift, qkv_weight, qkv_bias, out_weight, out_bias,
    fc1_weight, fc1_bias, fc2_weight, fc2_bias, cotangent,
):
    n = lax.axis_size("tensor")
    pieces = lax.axis_size("dp")
    me = lax.axis_index("tensor")
    rows, depth = tokens.shape
    count = segments.shape[1]
    width = qkv_weight.shape[2]

    def shift(x, pairs):
        return lax.ppermute(x, "tensor", pairs)

    def turns(step):
        left, right = me - step, me + step
        has_left, has_right = left >= 0, right < n
        one = jnp.where(has_left, left, right)
        last = jnp.where(has_right, right, jnp.where(has_left, left, n))
        busy = has_left.astype(jnp.int32) + has_right.astype(jnp.int32)
        values = [one, jnp.where(has_left, 0, 1), right, 1, busy, last]
        return jnp.stack([jnp.asarray(v, jnp.int32) for v in values])

    def places_of(shards, present):
        shards, present = jnp.stack(shards), jnp.stack(present)
        order = jnp.sort(jnp.where(present, shards, n))
        order = jnp.concatenate([order, jnp.full((n,), n, order.dtype)])[:n]
        return jnp.concatenate(
            [
                jnp.sum(present.astype(jnp.int32))[None],
                order,
                jnp.stack([jnp.clip(shards, 0, n - 1), present.astype(jnp.int32)], axis=1).reshape(-1),
            ]
        ).astype(jnp.int32)

    def present_shards(steps):
        shards = [me] + [me + d * s for s in range(1, steps + 1) for d in (-1, 1)]
        return places_of(shards, [(x >= 0) & (x < n) for x in shards])

    early = present_shards(n - 2)
    late = turns(n - 1)
    middle = [turns(s) for s in range(2, n - 1)]
    cot_shards, cot_there = [me], [me >= 0]
    for s in range(1, n - 1):
        for direction in range(2):
            at_end = me == (n - 1, 0)[direction]
            shard = me + (-s, s)[direction]
            cot_shards += [shard, shard]
            cot_there += [(shard >= 0) & (shard < n) & jnp.logical_not(at_end), at_end]
    if n == 4:
        table = jnp.array([[-1, 0, 3, -1], [-1, 2, 1, -1], [1, -1, -1, 2], [2, -1, -1, 1], [-1, 3, 0, -1]])[:, me]
        cot_shards = [me] + [table[k] for k in range(5)]
        cot_there = [x >= 0 for x in cot_shards]
    cot_early = places_of(cot_shards, cot_there)

    bits = [b for b in range(1, pieces.bit_length() - 1)]
    places = pieces // 2
    mine = lax.axis_index("dp")

    def place_of(r, order):
        return sum(((r >> (len(order) - 1 - k)) & 1) << bit for k, bit in enumerate(order))

    kept = [place_of(r, bits) for r in range(places)] + [place_of(r, bits[::-1]) for r in range(places)]
    send_where = mine ^ jnp.array([2 * q + 1 for q in range(places)], jnp.int32)
    keep_where = jnp.concatenate([mine ^ jnp.array(kept, jnp.int32), jnp.array(kept, jnp.int32) // 2])
    plans = [early, late, *middle, cot_early, send_where, keep_where]

    own_normed = norm(tokens, ln_gain[None], ln_shift[None])

    w_qkv = lax.all_gather(qkv_weight.reshape(-1, 3 * width), "dp", axis=0, tiled=True)
    w_up = lax.all_gather(fc1_weight, "dp", axis=0, tiled=True)
    w_out = lax.all_gather(out_weight, "dp", axis=0)
    w_down = lax.all_gather(fc2_weight, "dp", axis=0)

    segment_row = segments[0]
    starts = seq_starts(segment_row)
    tables = rotary_tables(jnp.arange(count, dtype=jnp.int32) - starts)
    first = starts[::BLOCK] // BLOCK
    segc, segr = segment_row[:, None], segment_row[None, :]

    bias_qkv, bias_up = qkv_bias.reshape(1, -1), fc1_bias[None]
    def line_step(pair, s):
        right, left = pair
        return [
            shift(right, [(i, i + 1) for i in range(s - 1, n - 1)]),
            shift(left, [(i, i - 1) for i in range(1, n - s + 1)]),
        ]

    def line_sum(x):
        return lax.psum_scatter(x, "tensor", scatter_dimension=0, tiled=True)

    def flat(pairs):
        return [x for pair in pairs for x in pair]

    project = (w_qkv, w_up, bias_qkv, bias_up, tables)
    normed_in = [line_step([own_normed] * 2, 1)]
    plans = lax.optimization_barrier(plans)
    early, late, cot_early, send_where, keep_where = plans[0], plans[1], *plans[-3:]
    middle = plans[2:-3]
    normed, qkv = queries_early(
        after(present_shards(1), *plans, first, segc), [own_normed] + normed_in[0], w_qkv, bias_qkv, tables, n
    )
    early_qkv = qkv
    for s in range(2, n):
        normed_in.append(line_step(after(tuple(normed_in[-1]), qkv) if s == 3 else normed_in[-1], s))
    for s in range(2, n - 1):
        normed, qkv = queries_chunk(middle[s - 2], normed_in[s - 1], w_qkv, bias_qkv, tables, (normed, qkv), n)
    act, slope = units_early(
        after(early, qkv), [own_normed] + flat(normed_in[:-1]), w_up, bias_up, width, n
    )
    def inner_step(pair, s):
        right, left = pair
        return [
            shift(right, [(i, i + 1) for i in range(s - 1, n - 2)]),
            shift(left, [(i, i - 1) for i in range(2, n - s + 1)]),
        ]

    def end_step(pair):
        right, left = pair
        return [shift(right, [(n - 2, n - 1)]), shift(left, [(1, 0)])]

    soon = after(cotangent, *normed_in[-2], early_qkv)
    if n == 4:
        cross, out = [(1, 2), (2, 1)], [(2, 3), (1, 0)]
        outside, across = shift(soon, [(0, 1), (3, 2)]), shift(soon, cross)
        outside, across = after((outside, across), *normed_in[-1], act)
        near = shift(after(cotangent, outside), out)
        next_ = shift(across, out)
        over = shift(outside, cross)
        cot_from = [cotangent, outside, across, near, next_, over]
    else:
        inner = [inner_step([soon] * 2, 1)]
        ready = after(tuple(inner[0]), *normed_in[-1], act)
        ends = [end_step([after(cotangent, *ready)] * 2)]
        inner.append(inner_step(ready, 2))
        cot_from = [cotangent]
    normed, qkv, act, slope = forward_chunk(late, normed_in[-1], *project, (normed, qkv, act, slope), n)

    if n == 4:
        att, lse = attend(qkv, segc, segr, first, 0, 1, None)
        last_in = [shift(after(over, att), out)] * 2
    else:
        att_half = attend(qkv, segc, segr, first, 0, 2, None)
        ends.append(end_step(after(tuple(ready), *ends[0], *inner[1], att_half[0])))
        att, lse = attend(qkv, segc, segr, first, 1, 2, att_half)
        for s in range(3, n):
            ready = after(tuple(inner[-1]), att)
            ends.append(end_step(ready))
            if s < n - 1:
                inner.append(inner_step(ready, s))
        for s in range(1, n - 1):
            for direction in range(2):
                cot_from += [inner[s - 1][direction], ends[s - 1][direction]]
        last_in = ends[-1]
    part = mix(att, act, w_out, w_down)
    bufs = backward_early(after(cot_early, part), cot_from, w_out, w_down, slope, n)
    block_sum = line_sum(after(part, bufs[2], *last_in))
    cot, grad_att, grad_hid = backward_chunk(late, last_in, w_out, w_down, slope, bufs, n)
    orders = (bits, bits[::-1])

    def finish(pair, axis, *marks):
        for k in range(1, len(bits)):
            pair = halve([after(half, *marks) for half in pair], orders, k, pair)
        return jnp.concatenate([half[0].astype(F32) for half in pair], axis=axis)

    col_send = column_grads(send_where, att, act, cot, places)
    up_send, up_sum = row_grads(send_where, normed, [after(grad_hid, col_send)], count, places)
    grad_qkv = attend_back(
        qkv, after(grad_att, up_sum), att, lse, segc, segr, first, tables, 0, 1, None
    )
    col_came, up_came = swap(col_send, 0), swap(up_send, 0)
    part = grad_normed(grad_qkv, after(grad_hid, col_came, up_came), w_qkv, w_up, 0, depth)
    grad_sum = line_sum(after(part, block_sum))
    col_pair = column_grads(keep_where, att, act, after(cot, part), places, col_came)
    qkv_send, qkv_sum = row_grads(send_where, normed, after(tuple(grad_qkv), col_pair[0]), count, places)
    up_pair = row_grads(
        keep_where, normed, [after(grad_hid, qkv_sum)], count, places, up_came
    )
    col_pair = halve([after(c, up_pair[0]) for c in col_pair], orders, 0, col_pair)
    qkv_pair = row_grads(
        keep_where, after(normed, *col_pair), grad_qkv, count, places, swap(qkv_send, 0)
    )
    up_pair = halve([after(u, qkv_pair[0]) for u in up_pair], orders, 0, up_pair)
    qkv_kept = qkv_pair[0]
    qkv_pair = halve(qkv_pair, orders, 0)
    mixed = mixed_out(tokens, after(block_sum, qkv_kept), (out_bias + fc2_bias)[None])
    input_grad, sums = norm_back(tokens, after(cotangent, mixed, *qkv_pair), [grad_sum], ln_gain[None])
    common = 3 * depth // 128
    pack = jnp.concatenate([a.reshape(-1, 128) for a in (sums[:3], up_sum[0], qkv_sum[0])])
    pack = jnp.pad(pack, ((0, -pack.shape[0] % 8), (0, 0)))
    pack = small_sums(pack, common)
    col_out, up_out, qkv_out = finish(col_pair, 0, qkv_kept), finish(up_pair, 1, *qkv_pair), finish(qkv_pair, 1)
    total = pack[:common].reshape(3, depth)
    ff_rows = up_sum.shape[1] // 128
    up_bias_grad = pack[common : common + ff_rows].reshape(-1)
    qkv_bias_grad = pack[common + ff_rows : common + ff_rows + 3 * width // 128].reshape(3, width)
    return (
        mixed,
        input_grad,
        qkv_out.reshape(-1, 3, width),
        qkv_bias_grad,
        col_out[:width],
        total[2],
        up_out,
        up_bias_grad,
        col_out[width:],
        total[2],
        total[0],
        total[1],
    )


def solution(mesh):
    in_specs = (
        P(("dp", "tensor"), None),
        P("dp", None),
        P(),
        P(),
        P("dp", None, "tensor"),
        P(None, "tensor"),
        P("tensor", "dp"),
        P(),
        P("dp", "tensor"),
        P("tensor"),
        P("tensor", "dp"),
        P(),
        P(("dp", "tensor"), None),
    )
    out_specs = (
        P(("dp", "tensor"), None),
        P(("dp", "tensor"), None),
        P("dp", None, "tensor"),
        P(None, "tensor"),
        P("tensor", "dp"),
        P(),
        P("dp", "tensor"),
        P("tensor"),
        P("tensor", "dp"),
        P(),
        P(),
        P(),
    )
    return jax.shard_map(local, mesh=mesh, in_specs=in_specs, out_specs=out_specs, check_vma=False)
```

```python
import functools

import jax
import jax.numpy as jnp
from jax import lax
from jax.experimental import pallas as pl
from jax.experimental.pallas import tpu as pltpu
from jax.sharding import PartitionSpec as P

HD = 64
ROT = 32
EPS = 1e-05
ROPE_BASE = 10000.0
NEGATIVE = -1e30
BLOCK = 256
ROWS = 256
SHRINK = 20

F32 = jnp.float32
BF16 = jnp.bfloat16


def dot_nn(a, b):
    return lax.dot_general(a, b, (((1,), (0,)), ((), ())), preferred_element_type=F32)


def dot_nt(a, b):
    return lax.dot_general(a, b, (((1,), (1,)), ((), ())), preferred_element_type=F32)


def dot_tn(a, b):
    return lax.dot_general(a, b, (((0,), (0,)), ((), ())), preferred_element_type=F32)


def cost(flops, moved, trans=0):
    return pl.CostEstimate(flops=int(flops / SHRINK), bytes_accessed=int(moved / SHRINK), transcendentals=0)


def whole(a):
    return pl.BlockSpec(a.shape, lambda *_: (0,) * a.ndim)


def seq_starts(segment_row):
    count = segment_row.shape[0]
    index = jnp.arange(count, dtype=jnp.int32)
    begins = jnp.concatenate([jnp.ones((1,), dtype=bool), segment_row[1:] != segment_row[:-1]])
    return lax.cummax(jnp.where(begins, index, jnp.zeros_like(index)), axis=0)


def rotary_tables(positions):
    half = ROT // 2
    lane = jnp.arange(128, dtype=jnp.int32) % HD
    frequency = ROPE_BASE ** (-((lane % half).astype(F32) * 2.0) / ROT)
    angles = positions.astype(F32)[:, None] * frequency[None, :]
    cosine = jnp.where(lane < ROT, jnp.cos(angles), 1.0)
    sine = jnp.sin(angles)
    sine_up = jnp.where(lane < half, -sine, 0.0)
    sine_down = jnp.where((lane >= half) & (lane < ROT), sine, 0.0)
    return cosine, sine_up, sine_down


def rotate(x, cosine, sine_up, sine_down):
    return (
        x * cosine
        + pltpu.roll(x, 128 - ROT // 2, axis=1) * sine_up
        + pltpu.roll(x, ROT // 2, axis=1) * sine_down
    )


def unrotate(x, cosine, sine_up, sine_down):
    return (
        x * cosine
        - pltpu.roll(x, 128 - ROT // 2, axis=1) * sine_up
        - pltpu.roll(x, ROT // 2, axis=1) * sine_down
    )


def norm_kernel(x_ref, gain_ref, shift_ref, o_ref):
    x = x_ref[...].astype(F32)
    centred = x - jnp.mean(x, axis=1, keepdims=True)
    inv_std = lax.rsqrt(jnp.mean(centred * centred, axis=1, keepdims=True) + EPS)
    o_ref[...] = (centred * inv_std * gain_ref[...] + shift_ref[...]).astype(BF16)


def norm(x, gain, shift):
    rows, width = x.shape
    step = rows // 2
    row = pl.BlockSpec((1, width), lambda i: (0, 0))
    tile = pl.BlockSpec((step, width), lambda i: (i, 0))
    return pl.pallas_call(
        norm_kernel,
        grid=(rows // step,),
        in_specs=[tile, row, row],
        out_specs=tile,
        out_shape=jax.ShapeDtypeStruct(x.shape, BF16),
        cost_estimate=cost(rows * width * 8, rows * width * 4),
        name="norm",
    )(x, gain, shift)


def norm_back_kernel(x_ref, cot_ref, *refs):
    gain_ref, o_ref, sums_ref = refs[-3:]

    @pl.when(pl.program_id(0) == 0)
    def _():
        sums_ref[...] = jnp.zeros_like(sums_ref)

    x = x_ref[...].astype(F32)
    centred = x - jnp.mean(x, axis=1, keepdims=True)
    inv_std = lax.rsqrt(jnp.mean(centred * centred, axis=1, keepdims=True) + EPS)
    normalized = centred * inv_std
    grad = jnp.concatenate([r[...] for r in refs[:-3]], axis=1).astype(F32)
    sums_ref[0:1, :] += jnp.sum(grad * normalized, axis=0, keepdims=True)
    sums_ref[1:2, :] += jnp.sum(grad, axis=0, keepdims=True)
    cot = cot_ref[...].astype(F32)
    sums_ref[2:3, :] += jnp.sum(cot, axis=0, keepdims=True)
    scaled = grad * gain_ref[...]
    first = jnp.mean(scaled, axis=1, keepdims=True)
    second = jnp.mean(scaled * normalized, axis=1, keepdims=True)
    o_ref[...] = (inv_std * (scaled - first - normalized * second) + cot).astype(BF16)


def norm_back(x, cot, grads, gain):
    rows, width = x.shape
    step = min(128, rows)
    tile = pl.BlockSpec((step, width), lambda i: (i, 0))
    return pl.pallas_call(
        norm_back_kernel,
        grid=(rows // step,),
        in_specs=[tile, tile]
        + [pl.BlockSpec((step, g.shape[1]), lambda i: (i, 0)) for g in grads]
        + [pl.BlockSpec((1, width), lambda i: (0, 0))],
        out_specs=[tile, pl.BlockSpec((8, width), lambda i: (0, 0))],
        out_shape=[jax.ShapeDtypeStruct(x.shape, BF16), jax.ShapeDtypeStruct((8, width), F32)],
        cost_estimate=cost(rows * width * 20, rows * width * 12),
        name="norm_back",
    )(x, cot, *grads, gain)


def pick(where_ref, i, tiles):
    turn = lax.div(i, tiles)
    busy = turn < where_ref[4]
    slot = jnp.where(busy, where_ref[2 * turn], where_ref[5])
    return jnp.where(busy, lax.rem(i, tiles), tiles - 1), slot, busy


def pick_shard(where_ref, i, tiles, refs, o_ref):
    turn = lax.div(i, tiles)
    if len(refs) == 1:
        o_ref[...] = refs[0][...]
        return

    @pl.when(where_ref[2 * turn + 1] == 0)
    def _():
        o_ref[...] = refs[0][...]

    @pl.when(where_ref[2 * turn + 1] == 1)
    def _():
        o_ref[...] = refs[1][...]


def project_tile(j, tall, x_ref, wq_ref, wu_ref, bq_ref, bu_ref, tables, qkv_ref, act_ref, slope_ref, over):
    if qkv_ref is not None:
        width = wq_ref.shape[1]

        @pl.when(j < 2)
        def _():
            scale = jnp.where(j == 0, HD**-0.5, 1.0).astype(F32)

            def turned(m, t):
                raw = (dot_nn(x_ref[m, :], wq_ref[...]) + bq_ref[...]) * scale
                turn = [r[t, :] for r in tables]
                for p in range(width // 128):
                    lanes = slice(p * 128, (p + 1) * 128)
                    qkv_ref[m, lanes] = rotate(raw[:, lanes], *turn).astype(BF16)

            over(turned)

        @pl.when(j == 2)
        def _():
            def plain(m, t):
                qkv_ref[m, :] = (dot_nn(x_ref[m, :], wq_ref[...]) + bq_ref[...]).astype(BF16)

            over(plain)

    if act_ref is not None:

        @pl.when(j > 2)
        def _():
            def gelu(m, t):
                act_ref[m, :], slope_ref[m, :] = gelu_and_slope(dot_nn(x_ref[m, :], wu_ref[...]) + bu_ref[...])

            over(gelu)


def gelu_and_slope(v):
    root = 0.7978845608028654
    cubic = 0.044715
    square = v * v
    t = jnp.tanh(v * (root + (root * cubic) * square))
    half = 0.5 + 0.5 * t
    slope = half + (v * (0.5 - 0.5 * (t * t))) * (root + (3.0 * root * cubic) * square)
    return (v * half).astype(BF16), slope.astype(BF16)


def forward_kernel(came, tiles, where_ref, *refs):
    x_refs, refs = refs[:came], refs[came:]
    wq_ref, wu_ref, bq_ref, bu_ref = refs[:4]
    tables = refs[4:7]
    normed_ref, qkv_ref, act_ref, slope_ref = refs[-4:]
    i = pl.program_id(0)
    j, _, busy = pick(where_ref, i, tiles)
    rows = normed_ref.shape[0]
    step = min(ROWS, rows)

    @pl.when(busy & (j == 0))
    def _():
        pick_shard(where_ref, i, tiles, x_refs, normed_ref)

    def over(act):
        for m in range(0, rows, step):
            act(slice(m, m + step), slice(m, m + step))

    @pl.when(busy)
    def _():
        project_tile(j, None, normed_ref, wq_ref, wu_ref, bq_ref, bu_ref, tables, qkv_ref, act_ref, slope_ref, over)


def queries_kernel(came, tiles, where_ref, *refs):
    x_refs, refs = refs[:came], refs[came:]
    wq_ref, bq_ref = refs[:2]
    tables = refs[2:5]
    normed_ref, qkv_ref = refs[-2:]
    i = pl.program_id(0)
    j, _, busy = pick(where_ref, i, tiles)
    rows = normed_ref.shape[0]
    step = min(ROWS, rows)

    @pl.when(busy & (j == 0))
    def _():
        pick_shard(where_ref, i, tiles, x_refs, normed_ref)

    def over(act):
        for m in range(0, rows, step):
            act(slice(m, m + step), slice(m, m + step))

    @pl.when(busy)
    def _():
        project_tile(j, None, normed_ref, wq_ref, None, bq_ref, None, tables, qkv_ref, None, None, over)


def queries_chunk(where, xs, wq, bq, tables, bufs, parts):
    rows, depth = xs[0].shape
    width = wq.shape[1] // 3
    tiles = 3

    def at(k):
        def index(i, w):
            j, slot, _ = pick(w, i, tiles)
            return ((slot, j), (0, j), (0, 0), (slot, 0), (jnp.minimum(slot, parts - 1), 0))[k]

        return index

    args = [where, *xs, wq, bq, *tables]
    return pl.pallas_call(
        functools.partial(queries_kernel, len(xs), tiles),
        grid_spec=pltpu.PrefetchScalarGridSpec(
            num_scalar_prefetch=1,
            grid=(len(xs) * tiles,),
            in_specs=[pl.BlockSpec((rows, depth), at(2))] * len(xs)
            + [pl.BlockSpec((depth, width), at(1)), pl.BlockSpec((1, width), at(1))]
            + [pl.BlockSpec((rows, 128), at(4))] * 3
            + [pl.BlockSpec(memory_space=pl.ANY)] * 2,
            out_specs=[pl.BlockSpec((rows, depth), at(3)), pl.BlockSpec((rows, width), at(0))],
        ),
        out_shape=[jax.ShapeDtypeStruct(b.shape, BF16) for b in bufs],
        input_output_aliases={len(args): 0, len(args) + 1: 1},
        cost_estimate=cost(6 * rows * depth * width, 6 * depth * width),
        name="queries_chunk",
    )(*args, *bufs)


def forward_chunk(where, xs, wq, wu, bq, bu, tables, bufs, parts):
    rows, depth = xs[0].shape
    width = wq.shape[1] // 3
    ff = wu.shape[1]
    tiles = 3 + ff // width

    def at(k):
        def index(i, w):
            j, slot, _ = pick(w, i, tiles)
            return (
                (slot, jnp.minimum(j, 2)),
                (slot, jnp.maximum(j - 3, 0)),
                (slot, 0),
                (0, jnp.minimum(j, 2)),
                (0, jnp.maximum(j - 3, 0)),
                (0, 0),
                (jnp.minimum(slot, parts - 1), 0),
            )[k]

        return index

    in_specs = (
        [pl.BlockSpec((rows, depth), at(5))] * len(xs)
        + [
            pl.BlockSpec((depth, width), at(3)),
            pl.BlockSpec((depth, width), at(4)),
            pl.BlockSpec((1, width), at(3)),
            pl.BlockSpec((1, width), at(4)),
        ]
        + [pl.BlockSpec((rows, 128), at(6))] * 3
    )
    total = (parts + 1) * rows
    shapes = [(total, depth), (total, 3 * width), (total, ff), (total, ff)]
    args = [where, *xs, wq, wu, bq, bu, *tables]
    aliases = {}
    if bufs is not None:
        aliases = {len(args) + k: k for k in range(4)}
        args += list(bufs)
        in_specs += [pl.BlockSpec(memory_space=pl.ANY)] * 4
    return pl.pallas_call(
        functools.partial(forward_kernel, len(xs), tiles),
        grid_spec=pltpu.PrefetchScalarGridSpec(
            num_scalar_prefetch=1,
            grid=(len(xs) * tiles,),
            in_specs=in_specs,
            out_specs=[
                pl.BlockSpec((rows, depth), at(2)),
                pl.BlockSpec((rows, width), at(0)),
                pl.BlockSpec((rows, width), at(1)),
                pl.BlockSpec((rows, width), at(1)),
            ],
        ),
        out_shape=[jax.ShapeDtypeStruct(s, BF16) for s in shapes],
        input_output_aliases=aliases,
        cost_estimate=cost(2 * rows * depth * (3 * width + ff), 2 * depth * (3 * width + ff)),
        name="forward_chunk",
    )(*args)


def collect(where_ref, came, shards, x_refs, held_ref, full_ref, in_sems, out_sems, first, last):
    rows = x_refs[0].shape[0]

    def spot(c):
        return pl.ds(pl.multiple_of(where_ref[1 + shards + 2 * c] * rows, rows), rows)

    def loads(c):
        return pltpu.make_async_copy(x_refs[c], held_ref.at[spot(c)], in_sems.at[c])

    def stores(c):
        return pltpu.make_async_copy(held_ref.at[spot(c)], full_ref.at[spot(c)], out_sems.at[c])

    def each(act):
        for c in range(came):
            pl.when(where_ref[2 + shards + 2 * c] > 0)(functools.partial(act, c))

    @pl.when(first)
    def _():
        each(lambda c: loads(c).start())
        each(lambda c: loads(c).wait())
        if full_ref is not None:
            each(lambda c: stores(c).start())

    def finish():
        pl.when(last)(lambda: each(lambda c: stores(c).wait()))

    return finish


def early_over(where_ref, rows):
    step = min(ROWS, rows)

    def over(act):
        def body(t, carry):
            for m in range(0, rows, step):
                at = pl.ds(pl.multiple_of(where_ref[1 + t] * rows + m, step), step)
                act(at, at)
            return carry

        lax.fori_loop(0, where_ref[0], body, 0)

    return over


def queries_early_kernel(came, shards, where_ref, *refs):
    x_refs, refs = refs[:came], refs[came:]
    wq_ref, bq_ref = refs[:2]
    tables = refs[2:5]
    normed_ref, qkv_ref, held_ref, in_sems, out_sems = refs[5:]
    j = pl.program_id(0)
    finish = collect(
        where_ref, came, shards, x_refs, held_ref, normed_ref, in_sems, out_sems,
        j == 0, j == pl.num_programs(0) - 1,
    )
    over = early_over(where_ref, x_refs[0].shape[0])
    project_tile(j, None, held_ref, wq_ref, None, bq_ref, None, tables, qkv_ref, None, None, over)
    finish()


def units_early_kernel(came, shards, where_ref, *refs):
    x_refs, refs = refs[:came], refs[came:]
    wu_ref, bu_ref, act_ref, slope_ref, held_ref, in_sems = refs
    j = pl.program_id(0)
    collect(where_ref, came, shards, x_refs, held_ref, None, in_sems, None, j == 0, None)
    over = early_over(where_ref, x_refs[0].shape[0])
    project_tile(j + 3, None, held_ref, None, wu_ref, None, bu_ref, None, None, act_ref, slope_ref, over)


def queries_early(where, xs, wq, bq, tables, parts):
    rows, depth = xs[0].shape
    width = wq.shape[1] // 3
    count = parts * rows
    in_place = pl.BlockSpec(memory_space=pl.ANY)
    return pl.pallas_call(
        functools.partial(queries_early_kernel, len(xs), parts),
        grid_spec=pltpu.PrefetchScalarGridSpec(
            num_scalar_prefetch=1,
            grid=(3,),
            in_specs=[in_place] * len(xs)
            + [pl.BlockSpec((depth, width), lambda j, w: (0, j)), pl.BlockSpec((1, width), lambda j, w: (0, j))]
            + [whole(t) for t in tables],
            out_specs=[in_place, pl.BlockSpec((count, width), lambda j, w: (0, j))],
            scratch_shapes=[
                pltpu.VMEM((count, depth), BF16),
                pltpu.SemaphoreType.DMA((len(xs),)),
                pltpu.SemaphoreType.DMA((len(xs),)),
            ],
        ),
        out_shape=[
            jax.ShapeDtypeStruct((count + rows, depth), BF16),
            jax.ShapeDtypeStruct((count + rows, 3 * width), BF16),
        ],
        cost_estimate=cost(6 * count * depth * width, 6 * depth * width),
        name="queries_early",
    )(where, *xs, wq, bq, *tables)


def units_early(where, xs, wu, bu, width, parts):
    rows, depth = xs[0].shape
    ff = wu.shape[1]
    count = parts * rows
    return pl.pallas_call(
        functools.partial(units_early_kernel, len(xs), parts),
        grid_spec=pltpu.PrefetchScalarGridSpec(
            num_scalar_prefetch=1,
            grid=(ff // width,),
            in_specs=[pl.BlockSpec(memory_space=pl.ANY)] * len(xs)
            + [pl.BlockSpec((depth, width), lambda j, w: (0, j)), pl.BlockSpec((1, width), lambda j, w: (0, j))],
            out_specs=[pl.BlockSpec((count, width), lambda j, w: (0, j))] * 2,
            scratch_shapes=[pltpu.VMEM((count, depth), BF16), pltpu.SemaphoreType.DMA((len(xs),))],
        ),
        out_shape=[jax.ShapeDtypeStruct((count + rows, ff), BF16)] * 2,
        cost_estimate=cost(2 * count * depth * ff, 2 * depth * ff),
        name="units_early",
    )(where, *xs, wu, bu)


def backward_early_kernel(came, shards, where_ref, *refs):
    c_refs, refs = refs[:came], refs[came:]
    wo_ref, wd_ref, slope_ref, cot_ref, ga_ref, gh_ref, held_ref, in_sems, out_sems = refs
    j = pl.program_id(0)
    finish = collect(
        where_ref, came, shards, c_refs, held_ref, cot_ref, in_sems, out_sems,
        j == 0, j == pl.num_programs(0) - 1,
    )
    rows = c_refs[0].shape[0]
    step = min(ROWS, rows)

    def over(act):
        def body(t, carry):
            for m in range(0, rows, step):
                act(pl.ds(pl.multiple_of(where_ref[1 + t] * rows + m, step), step))
            return carry

        lax.fori_loop(0, where_ref[0], body, 0)

    @pl.when(j == 0)
    def _():
        weight = side_by_side(wo_ref)

        def act(m):
            ga_ref[m, :] = dot_nt(held_ref[m, :], weight).astype(BF16)

        over(act)

    @pl.when(j > 0)
    def _():
        weight = side_by_side(wd_ref)

        def act(m):
            gh_ref[m, :] = (dot_nt(held_ref[m, :], weight) * slope_ref[m, :].astype(F32)).astype(BF16)

        over(act)

    finish()


def backward_early(where, cots, wo, wd, slope, parts):
    rows, depth = cots[0].shape
    pieces, width, piece = wo.shape
    ff = wd.shape[1]
    count = parts * rows
    total = count + rows
    in_place = pl.BlockSpec(memory_space=pl.ANY)

    def tile(j):
        return jnp.maximum(j - 1, 0)

    return pl.pallas_call(
        functools.partial(backward_early_kernel, len(cots), parts),
        grid_spec=pltpu.PrefetchScalarGridSpec(
            num_scalar_prefetch=1,
            grid=(1 + ff // width,),
            in_specs=[in_place] * len(cots)
            + [
                whole(wo),
                pl.BlockSpec((pieces, width, piece), lambda j, w: (0, tile(j), 0)),
                pl.BlockSpec((count, width), lambda j, w: (0, tile(j))),
            ],
            out_specs=[
                in_place,
                pl.BlockSpec((count, width), lambda j, w: (0, 0)),
                pl.BlockSpec((count, width), lambda j, w: (0, tile(j))),
            ],
            scratch_shapes=[
                pltpu.VMEM((count, depth), BF16),
                pltpu.SemaphoreType.DMA((len(cots),)),
                pltpu.SemaphoreType.DMA((len(cots),)),
            ],
        ),
        out_shape=[jax.ShapeDtypeStruct(s, BF16) for s in ((total, depth), (total, width), (total, ff))],
        cost_estimate=cost(2 * count * depth * (width + ff), 2 * depth * (width + ff)),
        name="backward_early",
    )(where, *cots, wo, wd, slope)


def low_lanes(rows):
    return lax.broadcasted_iota(jnp.int32, (rows, 128), 1) < HD


def attend_kernel(
    skipped, first_ref, q_ref, k_ref, v_ref, segc_ref, segr_ref, *refs
):
    o_ref, lse_ref, max_ref, acc_ref, bias_ref = refs[-5:]
    i = pl.program_id(0) + skipped
    block, width = q_ref.shape
    pairs = width // 128
    low = low_lanes(block)
    owns = (low, jnp.logical_not(low))
    max_ref[...] = jnp.full_like(max_ref, NEGATIVE)
    lse_ref[...] = jnp.zeros_like(lse_ref)
    acc_ref[...] = jnp.zeros_like(acc_ref)
    q0 = pl.multiple_of(i * block, block)
    query_seg = segr_ref[:, pl.ds(q0, block)]
    query_row = q0 + lax.broadcasted_iota(jnp.int32, (1, block), 1)

    def set_bias(k0):
        key_seg = segc_ref[pl.ds(k0, block), :]
        key_row = k0 + lax.broadcasted_iota(jnp.int32, (block, 1), 0)
        bias_ref[...] = jnp.where((key_seg == query_seg) & (key_row <= query_row), 0.0, NEGATIVE)

    def scores(k0, p, h):
        lanes = slice(p * 128, (p + 1) * 128)
        q = q_ref[:, lanes]
        mine = jnp.where(owns[h], q, jnp.zeros_like(q))
        return dot_nt(k_ref[pl.ds(k0, block), lanes], mine) + bias_ref[...]

    def find_max(j, carry):
        k0 = pl.multiple_of(j * block, block)
        set_bias(k0)
        for p in range(pairs):
            for h in range(2):
                s = scores(k0, p, h)
                max_ref[2 * p + h] = jnp.maximum(max_ref[2 * p + h], jnp.max(s, axis=0, keepdims=True))
        return carry

    lax.fori_loop(first_ref[i], i + 1, find_max, 0)

    def add_up(j, carry):
        k0 = pl.multiple_of(j * block, block)
        set_bias(k0)
        for p in range(pairs):
            v = v_ref[pl.ds(k0, block), p * 128 : (p + 1) * 128]
            for h in range(2):
                e = jnp.exp(scores(k0, p, h) - max_ref[2 * p + h])
                lse_ref[p, h : h + 1, :] += jnp.sum(e, axis=0, keepdims=True)
                acc_ref[2 * p + h] += dot_tn(e.astype(BF16), jnp.where(owns[h], v, jnp.ones_like(v)))
        return carry

    lax.fori_loop(first_ref[i], i + 1, add_up, 0)
    for p in range(pairs):
        even, odd = acc_ref[2 * p], acc_ref[2 * p + 1]
        o_ref[:, p * 128 : (p + 1) * 128] = jnp.where(
            low, even / pltpu.roll(even, HD, axis=1), odd / pltpu.roll(odd, HD, axis=1)
        ).astype(BF16)
        for h in range(2):
            lse_ref[p, h : h + 1, :] = max_ref[2 * p + h] + jnp.log(lse_ref[p, h : h + 1, :])


def attend(qkv, segc, segr, first, part, parts, bufs):
    count = segr.shape[1]
    width = qkv.shape[1] // 3
    pairs = width // 128
    steps = count // BLOCK // parts
    skipped = part * steps
    in_place = [] if bufs is None else [pl.BlockSpec(memory_space=pl.ANY)] * 2
    return pl.pallas_call(
        functools.partial(attend_kernel, skipped),
        grid_spec=pltpu.PrefetchScalarGridSpec(
            num_scalar_prefetch=1,
            grid=(steps,),
            in_specs=[
                pl.BlockSpec((BLOCK, width), lambda i, f: (i + skipped, 0)),
                pl.BlockSpec((count, width), lambda i, f: (0, 1)),
                pl.BlockSpec((count, width), lambda i, f: (0, 2)),
                whole(segc),
                whole(segr),
            ]
            + in_place,
            out_specs=[
                pl.BlockSpec((BLOCK, width), lambda i, f: (i + skipped, 0)),
                pl.BlockSpec((pairs, 8, BLOCK), lambda i, f: (0, 0, i + skipped)),
            ],
            scratch_shapes=[
                pltpu.VMEM((2 * pairs, 1, BLOCK), F32),
                pltpu.VMEM((2 * pairs, BLOCK, 128), F32),
                pltpu.VMEM((BLOCK, BLOCK), F32),
            ],
        ),
        out_shape=[
            jax.ShapeDtypeStruct((count, width), BF16),
            jax.ShapeDtypeStruct((pairs, 8, count), F32),
        ],
        input_output_aliases={} if bufs is None else {6: 0, 7: 1},
        cost_estimate=cost(30e9 * width / 512, count * width * 8),
        name="attend",
    )(first, qkv, qkv, qkv, segc, segr, *([] if bufs is None else bufs))


def attend_back_kernel(
    first_ref, q_ref, k_ref, v_ref, go_ref, o_ref, lse_ref, segc_ref, segr_ref,
    cos_ref, up_ref, down_ref, *refs,
):
    gq_ref, gk_ref, gv_ref, dq_ref, dk_ref, dv_ref, bias_ref = refs[-7:]
    i = pl.program_id(0)
    steps = pl.num_programs(0)
    block, width = q_ref.shape
    pairs = width // 128
    low = low_lanes(block)
    owns = (low, jnp.logical_not(low))

    @pl.when(i == 0)
    def _():
        dk_ref[...] = jnp.zeros_like(dk_ref)
        dv_ref[...] = jnp.zeros_like(dv_ref)

    dq_ref[...] = jnp.zeros_like(dq_ref)
    q0 = pl.multiple_of(i * block, block)
    query_seg = segr_ref[:, pl.ds(q0, block)]
    query_row = q0 + lax.broadcasted_iota(jnp.int32, (1, block), 1)
    half = jnp.where(
        lax.broadcasted_iota(jnp.int32, (8, 128), 1) // HD == lax.broadcasted_iota(jnp.int32, (8, 128), 0),
        1.0,
        0.0,
    ).astype(F32)
    inner = []
    for p in range(pairs):
        lanes = slice(p * 128, (p + 1) * 128)
        product = go_ref[:, lanes].astype(F32) * o_ref[:, lanes].astype(F32)
        inner.append(
            lax.dot_general(
                half, product, (((1,), (1,)), ((), ())),
                precision=lax.Precision.HIGHEST, preferred_element_type=F32,
            )
        )

    def body(j, carry):
        k0 = pl.multiple_of(j * block, block)
        key_seg = segc_ref[pl.ds(k0, block), :]
        key_row = k0 + lax.broadcasted_iota(jnp.int32, (block, 1), 0)
        bias_ref[...] = jnp.where((key_seg == query_seg) & (key_row <= query_row), 0.0, NEGATIVE)
        for p in range(pairs):
            lanes = slice(p * 128, (p + 1) * 128)
            k = k_ref[pl.ds(k0, block), lanes]
            v = v_ref[pl.ds(k0, block), lanes]
            q = q_ref[:, lanes]
            go = go_ref[:, lanes]
            sums = None
            for h in range(2):
                q_own, go_own, k_own = [jnp.where(owns[h], a, jnp.zeros_like(a)) for a in (q, go, k)]
                prob = jnp.exp(dot_nt(k, q_own) + bias_ref[...] - lse_ref[p, h : h + 1, :])
                grad_score = (prob * (dot_nt(v, go_own) - inner[p][h : h + 1, :])).astype(BF16)
                new = (
                    dot_nn(prob.astype(BF16), go_own),
                    dot_nn(grad_score, q_own),
                    dot_tn(grad_score, k_own),
                )
                sums = new if sums is None else tuple(a + b for a, b in zip(sums, new))
            dv_ref[pl.ds(k0, block), lanes] += sums[0]
            dk_ref[pl.ds(k0, block), lanes] += sums[1]
            dq_ref[:, lanes] += sums[2]
        return carry

    lax.fori_loop(first_ref[i], i + 1, body, 0)
    turn = [r[pl.ds(q0, block), :] for r in (cos_ref, up_ref, down_ref)]
    for p in range(pairs):
        lanes = slice(p * 128, (p + 1) * 128)
        gq_ref[:, lanes] = unrotate(dq_ref[:, lanes] * HD**-0.5, *turn).astype(BF16)

    @pl.when(i == steps - 1)
    def _():
        def finish(j, carry):
            k0 = pl.multiple_of(j * block, block)
            rows = pl.ds(k0, block)
            turn = [r[rows, :] for r in (cos_ref, up_ref, down_ref)]
            for p in range(pairs):
                lanes = slice(p * 128, (p + 1) * 128)
                gk_ref[rows, lanes] = unrotate(dk_ref[rows, lanes], *turn).astype(BF16)
                gv_ref[rows, lanes] = dv_ref[rows, lanes].astype(BF16)
            return carry

        lax.fori_loop(0, steps, finish, 0)


def attend_back(qkv, grad_out, out, lse, segc, segr, first, tables, part, parts, bufs):
    count = segr.shape[1]
    whole_width = qkv.shape[1] // 3
    width = whole_width // parts
    pairs = width // 128
    row_tile = pl.BlockSpec((BLOCK, width), lambda i, f: (i, part))
    column = pl.BlockSpec((count, width), lambda i, f: (0, part))
    in_place = [] if bufs is None else [pl.BlockSpec(memory_space=pl.ANY)] * 3
    args = [first, qkv, qkv, qkv, grad_out, out, lse, segc, segr, *tables]
    return pl.pallas_call(
        attend_back_kernel,
        grid_spec=pltpu.PrefetchScalarGridSpec(
            num_scalar_prefetch=1,
            grid=(count // BLOCK,),
            in_specs=[
                row_tile,
                pl.BlockSpec((count, width), lambda i, f: (0, parts + part)),
                pl.BlockSpec((count, width), lambda i, f: (0, 2 * parts + part)),
                row_tile,
                row_tile,
                pl.BlockSpec((pairs, 8, BLOCK), lambda i, f: (part, 0, i)),
                whole(segc),
                whole(segr),
                *[whole(t) for t in tables],
            ]
            + in_place,
            out_specs=[row_tile, column, column],
            scratch_shapes=[
                pltpu.VMEM((BLOCK, width), F32),
                pltpu.VMEM((count, width), F32),
                pltpu.VMEM((count, width), F32),
                pltpu.VMEM((BLOCK, BLOCK), F32),
            ],
        ),
        out_shape=[jax.ShapeDtypeStruct((count, whole_width), BF16)] * 3,
        input_output_aliases={} if bufs is None else {len(args) + k: k for k in range(3)},
        cost_estimate=cost(44e9 * width / 512, count * width * 20),
        name="attend_back",
    )(*args, *([] if bufs is None else bufs))


def side_by_side(ref):
    return jnp.concatenate([ref[b] for b in range(ref.shape[0])], axis=1)


def mix_kernel(att_ref, act_ref, wo_ref, wd_ref, o_ref):
    wo, wd = side_by_side(wo_ref), side_by_side(wd_ref)
    step = min(512, att_ref.shape[0])
    for m in range(0, att_ref.shape[0], step):
        rs = slice(m, m + step)
        o_ref[rs, :] = (dot_nn(att_ref[rs, :], wo) + dot_nn(act_ref[rs, :], wd)).astype(BF16)


def mix(att, act, wo, wd):
    pieces, width, piece = wo.shape
    ff = wd.shape[1]
    count = att.shape[0]
    group = max(1, 512 // piece)
    return pl.pallas_call(
        mix_kernel,
        grid=(pieces // group,),
        in_specs=[
            pl.BlockSpec((count, width), lambda j: (0, 0)),
            pl.BlockSpec((count, ff), lambda j: (0, 0)),
            pl.BlockSpec((group, width, piece), lambda j: (j, 0, 0)),
            pl.BlockSpec((group, ff, piece), lambda j: (j, 0, 0)),
        ],
        out_specs=pl.BlockSpec((count, group * piece), lambda j: (0, j)),
        out_shape=jax.ShapeDtypeStruct((count, pieces * piece), BF16),
        cost_estimate=cost(2 * count * (width + ff) * pieces * piece, 4 * count * ff),
        name="mix",
    )(att, act, wo, wd)


def mixed_kernel(x_ref, sum_ref, bias_ref, o_ref):
    o_ref[...] = (x_ref[...].astype(F32) + sum_ref[...].astype(F32) + bias_ref[...]).astype(BF16)


def mixed_out(x, total, bias):
    rows, width = x.shape
    step = min(256, rows)
    tile = pl.BlockSpec((step, width), lambda i: (i, 0))
    return pl.pallas_call(
        mixed_kernel,
        grid=(rows // step,),
        in_specs=[tile, tile, pl.BlockSpec((1, width), lambda i: (0, 0))],
        out_specs=tile,
        out_shape=jax.ShapeDtypeStruct(x.shape, BF16),
        cost_estimate=cost(rows * width * 4, rows * width * 6),
        name="mixed_out",
    )(x, total, bias)


def backward_kernel(came, tiles, where_ref, *refs):
    c_refs, refs = refs[:came], refs[came:]
    wo_ref, wd_ref, slope_ref = refs[:3]
    cot_ref, ga_ref, gh_ref = refs[-3:]
    i = pl.program_id(0)
    j, _, busy = pick(where_ref, i, tiles)
    rows = cot_ref.shape[0]
    step = min(ROWS, rows)

    @pl.when(busy & (j == 0))
    def _():
        pick_shard(where_ref, i, tiles, c_refs, cot_ref)
        weight = side_by_side(wo_ref)
        for m in range(0, rows, step):
            ga_ref[m : m + step, :] = dot_nt(cot_ref[m : m + step, :], weight).astype(BF16)

    @pl.when(busy & (j > 0))
    def _():
        weight = side_by_side(wd_ref)
        for m in range(0, rows, step):
            gh_ref[m : m + step, :] = (
                dot_nt(cot_ref[m : m + step, :], weight) * slope_ref[m : m + step, :].astype(F32)
            ).astype(BF16)


def backward_chunk(where, cots, wo, wd, slope, bufs, parts):
    rows, depth = cots[0].shape
    pieces, width, piece = wo.shape
    ff = wd.shape[1]
    tiles = 1 + ff // width

    def at(k):
        def index(i, w):
            j, slot, _ = pick(w, i, tiles)
            return ((0, 0), (0, jnp.maximum(j - 1, 0), 0), (slot, jnp.maximum(j - 1, 0)), (slot, 0))[k]

        return index

    in_specs = [pl.BlockSpec((rows, depth), at(0))] * len(cots) + [
        whole(wo),
        pl.BlockSpec((pieces, width, piece), at(1)),
        pl.BlockSpec((rows, width), at(2)),
    ]
    total = (parts + 1) * rows
    shapes = [(total, depth), (total, width), (total, ff)]
    args = [where, *cots, wo, wd, slope]
    aliases = {}
    if bufs is not None:
        aliases = {len(args) + k: k for k in range(3)}
        args += list(bufs)
        in_specs += [pl.BlockSpec(memory_space=pl.ANY)] * 3
    return pl.pallas_call(
        functools.partial(backward_kernel, len(cots), tiles),
        grid_spec=pltpu.PrefetchScalarGridSpec(
            num_scalar_prefetch=1,
            grid=(len(cots) * tiles,),
            in_specs=in_specs,
            out_specs=[
                pl.BlockSpec((rows, depth), at(3)),
                pl.BlockSpec((rows, width), at(3)),
                pl.BlockSpec((rows, width), at(2)),
            ],
        ),
        out_shape=[jax.ShapeDtypeStruct(s, BF16) for s in shapes],
        input_output_aliases=aliases,
        cost_estimate=cost(2 * rows * depth * (width + ff), 2 * depth * (width + ff)),
        name="backward_chunk",
    )(*args)


def grad_kernel(gq_ref, gk_ref, gv_ref, gh_ref, wq_ref, wu_ref, o_ref):
    step = min(512, gq_ref.shape[0])
    width = gq_ref.shape[1]
    for m in range(0, gq_ref.shape[0], step):
        rs = slice(m, m + step)
        left = jnp.concatenate([r[rs, :] for r in (gq_ref, gk_ref, gv_ref)], axis=1)
        o_ref[rs, :] = (dot_nt(left, wq_ref[...]) + dot_nt(gh_ref[rs, :], wu_ref[...])).astype(BF16)


def grad_normed(gqkv, gh, wq, wu, start, stop):
    count, width = gqkv[0].shape
    ff = gh.shape[1]
    tile = min(256, stop - start)
    first = start // tile
    return pl.pallas_call(
        grad_kernel,
        grid=((stop - start) // tile,),
        in_specs=[once((count, width))] * 3
        + [
            once((count, ff)),
            pl.BlockSpec((tile, wq.shape[1]), lambda j: (first + j, 0)),
            pl.BlockSpec((tile, wu.shape[1]), lambda j: (first + j, 0)),
        ],
        out_specs=pl.BlockSpec((count, tile), lambda j: (0, j)),
        out_shape=jax.ShapeDtypeStruct((count, stop - start), BF16),
        cost_estimate=cost(2 * count * (stop - start) * (3 * width + ff), 4 * count * ff),
        name="grad_normed",
    )(*gqkv, gh, wq, wu)


def put_columns(att_ref, act_ref, cot, o_ref, start, stop, add):
    width = att_ref.shape[1]
    at = start
    while at < stop:
        if at < width:
            end = min(stop, width)
            left = att_ref[:, at:end]
        else:
            end = min(stop, at + 512)
            left = act_ref[:, at - width : end - width]
        rows = slice(at - start, end - start)
        total = dot_tn(left, cot)
        if add is not None:
            total = total + add[0, rows, :].astype(F32)
        o_ref[0, rows, :] = total.astype(BF16)
        at = end


def columns_send_kernel(where_ref, att_ref, act_ref, c_ref, o_ref):
    put_columns(att_ref, act_ref, c_ref[...], o_ref, 0, o_ref.shape[1], None)


def columns_keep_kernel(where_ref, att_ref, act_ref, c_ref, came_ref, a_ref, b_ref):
    half = a_ref.shape[1]
    first = pl.program_id(0) < pl.num_programs(0) // 2

    @pl.when(first)
    def _():
        put_columns(att_ref, act_ref, c_ref[...], a_ref, 0, half, came_ref)

    @pl.when(jnp.logical_not(first))
    def _():
        put_columns(att_ref, act_ref, c_ref[...], b_ref, half, 2 * half, came_ref)


def rows_send_kernel(arrays, where_ref, x_ref, *refs):
    g_refs, o_ref, sum_ref = refs[:arrays], refs[-2], refs[-1]
    x = x_ref[...]
    first = pl.program_id(0) == 0
    start = 0
    for g_ref in g_refs:
        width = g_ref.shape[1]
        step = min(512, width)
        for m in range(0, width, step):
            o_ref[0, :, start + m : start + m + step] = dot_tn(x, g_ref[:, m : m + step]).astype(BF16)

        @pl.when(first)
        def _():
            ones = jnp.ones((8, g_ref.shape[0]), BF16)
            for m in range(0, width, step):
                sum_ref[:, start + m : start + m + step] = dot_nn(ones, g_ref[:, m : m + step])

        start += width


def rows_keep_kernel(arrays, where_ref, x_ref, *refs):
    g_refs, came_ref, a_ref, b_ref = refs[:arrays], *refs[arrays:]
    first = pl.program_id(0) < pl.num_programs(0) // 2
    x = x_ref[...]
    half = a_ref.shape[2]

    def put(o_ref, low):
        start = 0
        for g_ref in g_refs:
            width = g_ref.shape[1]
            at = max(start, low)
            while at < min(start + width, low + half):
                end = min(start + width, low + half, at + 512)
                o_ref[0, :, at - low : end - low] = (
                    dot_tn(x, g_ref[:, at - start : end - start])
                    + came_ref[0, :, at - low : end - low].astype(F32)
                ).astype(BF16)
                at = end
            start += width

    pl.when(first)(lambda: put(a_ref, 0))
    pl.when(jnp.logical_not(first))(lambda: put(b_ref, half))


def once(shape):
    return pl.BlockSpec(shape, lambda *_: (0,) * len(shape), pipeline_mode=pl.Buffered(1))


def column_grads(where, att, act, cot, places, came=None):
    count, width = att.shape
    ff = act.shape[1]
    piece = cot.shape[1] // (2 * places)
    flops = 2 * count * (width + ff) * piece * places
    base = [once((count, width)), once((count, ff)), pl.BlockSpec((count, piece), lambda t, w: (0, w[t]))]
    if came is None:
        return pl.pallas_call(
            columns_send_kernel,
            grid_spec=pltpu.PrefetchScalarGridSpec(
                num_scalar_prefetch=1,
                grid=(places,),
                in_specs=base,
                out_specs=pl.BlockSpec((1, width + ff, piece), lambda t, w: (t, 0, 0)),
            ),
            out_shape=jax.ShapeDtypeStruct((places, width + ff, piece), BF16),
            cost_estimate=cost(flops, 2 * count * (width + ff)),
            name="columns_send",
        )(where, att, act, cot)
    half = (width + ff) // 2
    turns = 2 * places
    return pl.pallas_call(
        columns_keep_kernel,
        grid_spec=pltpu.PrefetchScalarGridSpec(
            num_scalar_prefetch=1,
            grid=(turns,),
            in_specs=base
            + [pl.BlockSpec((1, half, piece), lambda t, w: (w[turns + t], t // places, 0))],
            out_specs=[
                pl.BlockSpec((1, half, piece), lambda t, w: (jnp.minimum(t, places - 1), 0, 0)),
                pl.BlockSpec((1, half, piece), lambda t, w: (jnp.maximum(t - places, 0), 0, 0)),
            ],
        ),
        out_shape=[jax.ShapeDtypeStruct((places, half, piece), BF16)] * 2,
        cost_estimate=cost(flops, 2 * count * (width + ff)),
        name="columns_keep",
    )(where, att, act, cot, came)


def row_grads(where, x, gs, count, places, came=None):
    width = sum(g.shape[1] for g in gs)
    piece = x.shape[1] // (2 * places)
    flops = 2 * count * width * piece * places
    base = [pl.BlockSpec((count, piece), lambda t, w: (0, w[t]))] + [once((count, g.shape[1])) for g in gs]
    if came is None:
        return pl.pallas_call(
            functools.partial(rows_send_kernel, len(gs)),
            grid_spec=pltpu.PrefetchScalarGridSpec(
                num_scalar_prefetch=1,
                grid=(places,),
                in_specs=base,
                out_specs=[
                    pl.BlockSpec((1, piece, width), lambda t, w: (t, 0, 0)),
                    pl.BlockSpec((8, width), lambda t, w: (0, 0)),
                ],
            ),
            out_shape=[
                jax.ShapeDtypeStruct((places, piece, width), BF16),
                jax.ShapeDtypeStruct((8, width), F32),
            ],
            cost_estimate=cost(flops, 2 * count * width),
            name="rows_send",
        )(where, x, *gs)
    half = width // 2
    turns = 2 * places
    return pl.pallas_call(
        functools.partial(rows_keep_kernel, len(gs)),
        grid_spec=pltpu.PrefetchScalarGridSpec(
            num_scalar_prefetch=1,
            grid=(turns,),
            in_specs=base
            + [pl.BlockSpec((1, piece, half), lambda t, w: (w[turns + t], 0, t // places))],
            out_specs=[
                pl.BlockSpec((1, piece, half), lambda t, w: (jnp.minimum(t, places - 1), 0, 0)),
                pl.BlockSpec((1, piece, half), lambda t, w: (jnp.maximum(t - places, 0), 0, 0)),
            ],
        ),
        out_shape=[jax.ShapeDtypeStruct((places, piece, half), BF16)] * 2,
        cost_estimate=cost(flops, 2 * count * width),
        name="rows_keep",
    )(where, x, *gs, came)


def after(value, *marks):
    return lax.optimization_barrier((value, *marks))[0]


def swap(x, bit):
    size = lax.axis_size("dp")
    return lax.ppermute(x, "dp", [(i, i ^ (1 << bit)) for i in range(size)])


def halve(xs, orders, k, sent=None):
    kept = []
    for x, y, bits in zip(xs, sent or xs, orders):
        rest = x.shape[0] // 2
        came = swap(y[rest:], bits[k])
        total = x[:rest].astype(F32) + came.astype(F32)
        kept.append(total if k == len(bits) - 1 else total.astype(BF16))
    return kept


def small_sum_kernel(phases, x_ref, o_ref, sent_ref, came_ref, send_sems, came_sems):
    barrier = pltpu.get_barrier_semaphore()

    def partner(axis, bit):
        return {axis: lax.axis_index(axis) ^ (1 << bit)}

    for axis, bit, _ in phases:
        pl.semaphore_signal(
            barrier, inc=1, device_id=partner(axis, bit), device_id_type=pl.DeviceIdType.MESH
        )
    pl.semaphore_wait(barrier, len(phases))
    sent_ref[0] = x_ref[...]
    for k, (axis, bit, rows) in enumerate(phases):
        span = pl.ds(0, rows)
        copy = pltpu.make_async_remote_copy(
            src_ref=sent_ref.at[k, span],
            dst_ref=came_ref.at[k, span],
            send_sem=send_sems.at[k],
            recv_sem=came_sems.at[k],
            device_id=partner(axis, bit),
            device_id_type=pl.DeviceIdType.MESH,
        )
        copy.start()
        copy.wait()
        total = sent_ref[k, 0:rows] + came_ref[k, 0:rows]
        if k == len(phases) - 1:
            o_ref[...] = sent_ref[k]
            o_ref[0:rows] = total
        else:
            sent_ref[k + 1] = sent_ref[k]
            sent_ref[k + 1, 0:rows] = total


def small_sums(x, common):
    rows = x.shape[0]
    phases = []
    for axis, height in (("dp", rows), ("tensor", common)):
        for bit in range(lax.axis_size(axis).bit_length() - 1):
            phases.append((axis, bit, height))
    return pl.pallas_call(
        functools.partial(small_sum_kernel, phases),
        in_specs=[pl.BlockSpec(memory_space=pltpu.VMEM)],
        out_specs=pl.BlockSpec(memory_space=pltpu.VMEM),
        out_shape=jax.ShapeDtypeStruct(x.shape, F32),
        scratch_shapes=[
            pltpu.VMEM((len(phases), *x.shape), F32),
            pltpu.VMEM((len(phases), *x.shape), F32),
            pltpu.SemaphoreType.DMA((len(phases),)),
            pltpu.SemaphoreType.DMA((len(phases),)),
        ],
        compiler_params=pltpu.CompilerParams(collective_id=0, has_side_effects=True),
        name="small_sums",
    )(x)


def local(
    tokens, segments, ln_gain, ln_shift, qkv_weight, qkv_bias, out_weight, out_bias,
    fc1_weight, fc1_bias, fc2_weight, fc2_bias, cotangent,
):
    n = lax.axis_size("tensor")
    pieces = lax.axis_size("dp")
    me = lax.axis_index("tensor")
    rows, depth = tokens.shape
    count = segments.shape[1]
    width = qkv_weight.shape[2]

    def shift(x, pairs):
        return lax.ppermute(x, "tensor", pairs)

    def turns(step):
        left, right = me - step, me + step
        has_left, has_right = left >= 0, right < n
        one = jnp.where(has_left, left, right)
        last = jnp.where(has_right, right, jnp.where(has_left, left, n))
        busy = has_left.astype(jnp.int32) + has_right.astype(jnp.int32)
        values = [one, jnp.where(has_left, 0, 1), right, 1, busy, last]
        return jnp.stack([jnp.asarray(v, jnp.int32) for v in values])

    def places_of(shards, present):
        shards, present = jnp.stack(shards), jnp.stack(present)
        order = jnp.sort(jnp.where(present, shards, n))
        order = jnp.concatenate([order, jnp.full((n,), n, order.dtype)])[:n]
        return jnp.concatenate(
            [
                jnp.sum(present.astype(jnp.int32))[None],
                order,
                jnp.stack([jnp.clip(shards, 0, n - 1), present.astype(jnp.int32)], axis=1).reshape(-1),
            ]
        ).astype(jnp.int32)

    def present_shards(steps):
        shards = [me] + [me + d * s for s in range(1, steps + 1) for d in (-1, 1)]
        return places_of(shards, [(x >= 0) & (x < n) for x in shards])

    early = present_shards(n - 2)
    late = turns(n - 1)
    middle = [turns(s) for s in range(2, n - 1)]
    cot_shards, cot_there = [me], [me >= 0]
    for s in range(1, n - 1):
        for direction in range(2):
            at_end = me == (n - 1, 0)[direction]
            shard = me + (-s, s)[direction]
            cot_shards += [shard, shard]
            cot_there += [(shard >= 0) & (shard < n) & jnp.logical_not(at_end), at_end]
    if n == 4:
        table = jnp.array([[-1, 0, 3, -1], [-1, 2, 1, -1], [1, -1, -1, 2], [2, -1, -1, 1], [-1, 3, 0, -1]])[:, me]
        cot_shards = [me] + [table[k] for k in range(5)]
        cot_there = [x >= 0 for x in cot_shards]
    cot_early = places_of(cot_shards, cot_there)

    bits = [b for b in range(1, pieces.bit_length() - 1)]
    places = pieces // 2
    mine = lax.axis_index("dp")

    def place_of(r, order):
        return sum(((r >> (len(order) - 1 - k)) & 1) << bit for k, bit in enumerate(order))

    kept = [place_of(r, bits) for r in range(places)] + [place_of(r, bits[::-1]) for r in range(places)]
    send_where = mine ^ jnp.array([2 * q + 1 for q in range(places)], jnp.int32)
    keep_where = jnp.concatenate([mine ^ jnp.array(kept, jnp.int32), jnp.array(kept, jnp.int32) // 2])
    plans = [early, late, *middle, cot_early, send_where, keep_where]

    own_normed = norm(tokens, ln_gain[None], ln_shift[None])

    w_qkv = lax.all_gather(qkv_weight.reshape(-1, 3 * width), "dp", axis=0, tiled=True)
    w_up = lax.all_gather(fc1_weight, "dp", axis=0, tiled=True)
    w_out = lax.all_gather(out_weight, "dp", axis=0)
    w_down = lax.all_gather(fc2_weight, "dp", axis=0)

    segment_row = segments[0]
    starts = seq_starts(segment_row)
    tables = rotary_tables(jnp.arange(count, dtype=jnp.int32) - starts)
    first = starts[::BLOCK] // BLOCK
    segc, segr = segment_row[:, None], segment_row[None, :]

    bias_qkv, bias_up = qkv_bias.reshape(1, -1), fc1_bias[None]
    def line_step(pair, s):
        right, left = pair
        return [
            shift(right, [(i, i + 1) for i in range(s - 1, n - 1)]),
            shift(left, [(i, i - 1) for i in range(1, n - s + 1)]),
        ]

    def line_sum(x):
        return lax.psum_scatter(x, "tensor", scatter_dimension=0, tiled=True)

    def flat(pairs):
        return [x for pair in pairs for x in pair]

    project = (w_qkv, w_up, bias_qkv, bias_up, tables)
    normed_in = [line_step([own_normed] * 2, 1)]
    plans = lax.optimization_barrier(plans)
    early, late, cot_early, send_where, keep_where = plans[0], plans[1], *plans[-3:]
    middle = plans[2:-3]
    normed, qkv = queries_early(
        after(present_shards(1), *plans, first, segc), [own_normed] + normed_in[0], w_qkv, bias_qkv, tables, n
    )
    early_qkv = qkv
    for s in range(2, n):
        normed_in.append(line_step(after(tuple(normed_in[-1]), qkv) if s == 3 else normed_in[-1], s))
    for s in range(2, n - 1):
        normed, qkv = queries_chunk(middle[s - 2], normed_in[s - 1], w_qkv, bias_qkv, tables, (normed, qkv), n)
    act, slope = units_early(
        after(early, qkv), [own_normed] + flat(normed_in[:-1]), w_up, bias_up, width, n
    )
    def inner_step(pair, s):
        right, left = pair
        return [
            shift(right, [(i, i + 1) for i in range(s - 1, n - 2)]),
            shift(left, [(i, i - 1) for i in range(2, n - s + 1)]),
        ]

    def end_step(pair):
        right, left = pair
        return [shift(right, [(n - 2, n - 1)]), shift(left, [(1, 0)])]

    soon = after(cotangent, *normed_in[-2], early_qkv)
    if n == 4:
        cross, out = [(1, 2), (2, 1)], [(2, 3), (1, 0)]
        outside, across = shift(soon, [(0, 1), (3, 2)]), shift(soon, cross)
        outside, across = after((outside, across), *normed_in[-1], act)
        near = shift(after(cotangent, outside), out)
        next_ = shift(across, out)
        over = shift(outside, cross)
        cot_from = [cotangent, outside, across, near, next_, over]
    else:
        inner = [inner_step([soon] * 2, 1)]
        ready = after(tuple(inner[0]), *normed_in[-1], act)
        ends = [end_step([after(cotangent, *ready)] * 2)]
        inner.append(inner_step(ready, 2))
        cot_from = [cotangent]
    normed, qkv, act, slope = forward_chunk(late, normed_in[-1], *project, (normed, qkv, act, slope), n)

    if n == 4:
        att, lse = attend(qkv, segc, segr, first, 0, 1, None)
        last_in = [shift(after(over, att), out)] * 2
    else:
        att_half = attend(qkv, segc, segr, first, 0, 2, None)
        ends.append(end_step(after(tuple(ready), *ends[0], *inner[1], att_half[0])))
        att, lse = attend(qkv, segc, segr, first, 1, 2, att_half)
        for s in range(3, n):
            ready = after(tuple(inner[-1]), att)
            ends.append(end_step(ready))
            if s < n - 1:
                inner.append(inner_step(ready, s))
        for s in range(1, n - 1):
            for direction in range(2):
                cot_from += [inner[s - 1][direction], ends[s - 1][direction]]
        last_in = ends[-1]
    part = mix(att, act, w_out, w_down)
    bufs = backward_early(after(cot_early, part), cot_from, w_out, w_down, slope, n)
    block_sum = line_sum(after(part, bufs[2], *last_in))
    cot, grad_att, grad_hid = backward_chunk(late, last_in, w_out, w_down, slope, bufs, n)
    orders = (bits, bits[::-1])

    def finish(pair, axis, *marks):
        for k in range(1, len(bits)):
            pair = halve([after(half, *marks) for half in pair], orders, k, pair)
        return jnp.concatenate([half[0].astype(F32) for half in pair], axis=axis)

    col_send = column_grads(send_where, att, act, cot, places)
    up_send, up_sum = row_grads(send_where, normed, [after(grad_hid, col_send)], count, places)
    grad_qkv = attend_back(
        qkv, after(grad_att, up_sum), att, lse, segc, segr, first, tables, 0, 1, None
    )
    col_came, up_came = swap(col_send, 0), swap(up_send, 0)
    part = grad_normed(grad_qkv, after(grad_hid, col_came, up_came), w_qkv, w_up, 0, depth)
    grad_sum = line_sum(after(part, block_sum))
    col_pair = column_grads(keep_where, att, act, after(cot, part), places, col_came)
    qkv_send, qkv_sum = row_grads(send_where, normed, after(tuple(grad_qkv), col_pair[0]), count, places)
    up_pair = row_grads(
        keep_where, normed, [after(grad_hid, qkv_sum)], count, places, up_came
    )
    col_pair = halve([after(c, up_pair[0]) for c in col_pair], orders, 0, col_pair)
    qkv_pair = row_grads(
        keep_where, after(normed, *col_pair), grad_qkv, count, places, swap(qkv_send, 0)
    )
    up_pair = halve([after(u, qkv_pair[0]) for u in up_pair], orders, 0, up_pair)
    qkv_kept = qkv_pair[0]
    mixed = mixed_out(tokens, after(block_sum, qkv_kept), (out_bias + fc2_bias)[None])
    qkv_pair = halve([after(half, mixed) for half in qkv_pair], orders, 0, qkv_pair)
    input_grad, sums = norm_back(tokens, after(cotangent, mixed, *qkv_pair), [grad_sum], ln_gain[None])
    common = 3 * depth // 128
    pack = jnp.concatenate([a.reshape(-1, 128) for a in (sums[:3], up_sum[0], qkv_sum[0])])
    pack = jnp.pad(pack, ((0, -pack.shape[0] % 8), (0, 0)))
    pack = small_sums(pack, common)
    col_out, up_out, qkv_out = finish(col_pair, 0, qkv_kept), finish(up_pair, 1, *qkv_pair), finish(qkv_pair, 1)
    total = pack[:common].reshape(3, depth)
    ff_rows = up_sum.shape[1] // 128
    up_bias_grad = pack[common : common + ff_rows].reshape(-1)
    qkv_bias_grad = pack[common + ff_rows : common + ff_rows + 3 * width // 128].reshape(3, width)
    return (
        mixed,
        input_grad,
        qkv_out.reshape(-1, 3, width),
        qkv_bias_grad,
        col_out[:width],
        total[2],
        up_out,
        up_bias_grad,
        col_out[width:],
        total[2],
        total[0],
        total[1],
    )


def solution(mesh):
    in_specs = (
        P(("dp", "tensor"), None),
        P("dp", None),
        P(),
        P(),
        P("dp", None, "tensor"),
        P(None, "tensor"),
        P("tensor", "dp"),
        P(),
        P("dp", "tensor"),
        P("tensor"),
        P("tensor", "dp"),
        P(),
        P(("dp", "tensor"), None),
    )
    out_specs = (
        P(("dp", "tensor"), None),
        P(("dp", "tensor"), None),
        P("dp", None, "tensor"),
        P(None, "tensor"),
        P("tensor", "dp"),
        P(),
        P("dp", "tensor"),
        P("tensor"),
        P("tensor", "dp"),
        P(),
        P(),
        P(),
    )
    return jax.shard_map(local, mesh=mesh, in_specs=in_specs, out_specs=out_specs, check_vma=False)
```

```python
import functools

import jax
import jax.numpy as jnp
from jax import lax
from jax.experimental import pallas as pl
from jax.experimental.pallas import tpu as pltpu
from jax.sharding import PartitionSpec as P

HD = 64
ROT = 32
EPS = 1e-05
ROPE_BASE = 10000.0
NEGATIVE = -1e30
BLOCK = 256
ROWS = 256
SHRINK = 20

F32 = jnp.float32
BF16 = jnp.bfloat16


def dot_nn(a, b):
    return lax.dot_general(a, b, (((1,), (0,)), ((), ())), preferred_element_type=F32)


def dot_nt(a, b):
    return lax.dot_general(a, b, (((1,), (1,)), ((), ())), preferred_element_type=F32)


def dot_tn(a, b):
    return lax.dot_general(a, b, (((0,), (0,)), ((), ())), preferred_element_type=F32)


def cost(flops, moved, trans=0):
    return pl.CostEstimate(flops=int(flops / SHRINK), bytes_accessed=int(moved / SHRINK), transcendentals=0)


def whole(a):
    return pl.BlockSpec(a.shape, lambda *_: (0,) * a.ndim)


def seq_starts(segment_row):
    count = segment_row.shape[0]
    index = jnp.arange(count, dtype=jnp.int32)
    begins = jnp.concatenate([jnp.ones((1,), dtype=bool), segment_row[1:] != segment_row[:-1]])
    return lax.cummax(jnp.where(begins, index, jnp.zeros_like(index)), axis=0)


def rotary_tables(positions):
    half = ROT // 2
    lane = jnp.arange(128, dtype=jnp.int32) % HD
    frequency = ROPE_BASE ** (-((lane % half).astype(F32) * 2.0) / ROT)
    angles = positions.astype(F32)[:, None] * frequency[None, :]
    cosine = jnp.where(lane < ROT, jnp.cos(angles), 1.0)
    sine = jnp.sin(angles)
    sine_up = jnp.where(lane < half, -sine, 0.0)
    sine_down = jnp.where((lane >= half) & (lane < ROT), sine, 0.0)
    return cosine, sine_up, sine_down


def rotate(x, cosine, sine_up, sine_down):
    return (
        x * cosine
        + pltpu.roll(x, 128 - ROT // 2, axis=1) * sine_up
        + pltpu.roll(x, ROT // 2, axis=1) * sine_down
    )


def unrotate(x, cosine, sine_up, sine_down):
    return (
        x * cosine
        - pltpu.roll(x, 128 - ROT // 2, axis=1) * sine_up
        - pltpu.roll(x, ROT // 2, axis=1) * sine_down
    )


def norm_kernel(x_ref, gain_ref, shift_ref, o_ref):
    x = x_ref[...].astype(F32)
    centred = x - jnp.mean(x, axis=1, keepdims=True)
    inv_std = lax.rsqrt(jnp.mean(centred * centred, axis=1, keepdims=True) + EPS)
    o_ref[...] = (centred * inv_std * gain_ref[...] + shift_ref[...]).astype(BF16)


def norm(x, gain, shift):
    rows, width = x.shape
    step = rows // 2
    row = pl.BlockSpec((1, width), lambda i: (0, 0))
    tile = pl.BlockSpec((step, width), lambda i: (i, 0))
    return pl.pallas_call(
        norm_kernel,
        grid=(rows // step,),
        in_specs=[tile, row, row],
        out_specs=tile,
        out_shape=jax.ShapeDtypeStruct(x.shape, BF16),
        cost_estimate=cost(rows * width * 8, rows * width * 4),
        name="norm",
    )(x, gain, shift)


def norm_back_kernel(x_ref, cot_ref, *refs):
    gain_ref, o_ref, sums_ref = refs[-3:]

    @pl.when(pl.program_id(0) == 0)
    def _():
        sums_ref[...] = jnp.zeros_like(sums_ref)

    x = x_ref[...].astype(F32)
    centred = x - jnp.mean(x, axis=1, keepdims=True)
    inv_std = lax.rsqrt(jnp.mean(centred * centred, axis=1, keepdims=True) + EPS)
    normalized = centred * inv_std
    grad = jnp.concatenate([r[...] for r in refs[:-3]], axis=1).astype(F32)
    sums_ref[0:1, :] += jnp.sum(grad * normalized, axis=0, keepdims=True)
    sums_ref[1:2, :] += jnp.sum(grad, axis=0, keepdims=True)
    cot = cot_ref[...].astype(F32)
    sums_ref[2:3, :] += jnp.sum(cot, axis=0, keepdims=True)
    scaled = grad * gain_ref[...]
    first = jnp.mean(scaled, axis=1, keepdims=True)
    second = jnp.mean(scaled * normalized, axis=1, keepdims=True)
    o_ref[...] = (inv_std * (scaled - first - normalized * second) + cot).astype(BF16)


def norm_back(x, cot, grads, gain):
    rows, width = x.shape
    step = min(256, rows)
    tile = pl.BlockSpec((step, width), lambda i: (i, 0))
    return pl.pallas_call(
        norm_back_kernel,
        grid=(rows // step,),
        in_specs=[tile, tile]
        + [pl.BlockSpec((step, g.shape[1]), lambda i: (i, 0)) for g in grads]
        + [pl.BlockSpec((1, width), lambda i: (0, 0))],
        out_specs=[tile, pl.BlockSpec((8, width), lambda i: (0, 0))],
        out_shape=[jax.ShapeDtypeStruct(x.shape, BF16), jax.ShapeDtypeStruct((8, width), F32)],
        cost_estimate=cost(rows * width * 20, rows * width * 12),
        name="norm_back",
    )(x, cot, *grads, gain)


def pick(where_ref, i, tiles):
    turn = lax.div(i, tiles)
    busy = turn < where_ref[4]
    slot = jnp.where(busy, where_ref[2 * turn], where_ref[5])
    return jnp.where(busy, lax.rem(i, tiles), tiles - 1), slot, busy


def pick_shard(where_ref, i, tiles, refs, o_ref):
    turn = lax.div(i, tiles)
    if len(refs) == 1:
        o_ref[...] = refs[0][...]
        return

    @pl.when(where_ref[2 * turn + 1] == 0)
    def _():
        o_ref[...] = refs[0][...]

    @pl.when(where_ref[2 * turn + 1] == 1)
    def _():
        o_ref[...] = refs[1][...]


def project_tile(j, tall, x_ref, wq_ref, wu_ref, bq_ref, bu_ref, tables, qkv_ref, act_ref, slope_ref, over):
    if qkv_ref is not None:
        width = wq_ref.shape[1]

        @pl.when(j < 2)
        def _():
            scale = jnp.where(j == 0, HD**-0.5, 1.0).astype(F32)

            def turned(m, t):
                raw = (dot_nn(x_ref[m, :], wq_ref[...]) + bq_ref[...]) * scale
                turn = [r[t, :] for r in tables]
                for p in range(width // 128):
                    lanes = slice(p * 128, (p + 1) * 128)
                    qkv_ref[m, lanes] = rotate(raw[:, lanes], *turn).astype(BF16)

            over(turned)

        @pl.when(j == 2)
        def _():
            def plain(m, t):
                qkv_ref[m, :] = (dot_nn(x_ref[m, :], wq_ref[...]) + bq_ref[...]).astype(BF16)

            over(plain)

    if act_ref is not None:

        @pl.when(j > 2)
        def _():
            def gelu(m, t):
                act_ref[m, :], slope_ref[m, :] = gelu_and_slope(dot_nn(x_ref[m, :], wu_ref[...]) + bu_ref[...])

            over(gelu)


def gelu_and_slope(v):
    root = 0.7978845608028654
    cubic = 0.044715
    square = v * v
    t = jnp.tanh(v * (root + (root * cubic) * square))
    half = 0.5 + 0.5 * t
    slope = half + (v * (0.5 - 0.5 * (t * t))) * (root + (3.0 * root * cubic) * square)
    return (v * half).astype(BF16), slope.astype(BF16)


def forward_kernel(came, tiles, where_ref, *refs):
    x_refs, refs = refs[:came], refs[came:]
    wq_ref, wu_ref, bq_ref, bu_ref = refs[:4]
    tables = refs[4:7]
    normed_ref, qkv_ref, act_ref, slope_ref = refs[-4:]
    i = pl.program_id(0)
    j, _, busy = pick(where_ref, i, tiles)
    rows = normed_ref.shape[0]
    step = min(ROWS, rows)

    @pl.when(busy & (j == 0))
    def _():
        pick_shard(where_ref, i, tiles, x_refs, normed_ref)

    def over(act):
        for m in range(0, rows, step):
            act(slice(m, m + step), slice(m, m + step))

    @pl.when(busy)
    def _():
        project_tile(j, None, normed_ref, wq_ref, wu_ref, bq_ref, bu_ref, tables, qkv_ref, act_ref, slope_ref, over)


def queries_kernel(came, tiles, where_ref, *refs):
    x_refs, refs = refs[:came], refs[came:]
    wq_ref, bq_ref = refs[:2]
    tables = refs[2:5]
    normed_ref, qkv_ref = refs[-2:]
    i = pl.program_id(0)
    j, _, busy = pick(where_ref, i, tiles)
    rows = normed_ref.shape[0]
    step = min(ROWS, rows)

    @pl.when(busy & (j == 0))
    def _():
        pick_shard(where_ref, i, tiles, x_refs, normed_ref)

    def over(act):
        for m in range(0, rows, step):
            act(slice(m, m + step), slice(m, m + step))

    @pl.when(busy)
    def _():
        project_tile(j, None, normed_ref, wq_ref, None, bq_ref, None, tables, qkv_ref, None, None, over)


def queries_chunk(where, xs, wq, bq, tables, bufs, parts):
    rows, depth = xs[0].shape
    width = wq.shape[1] // 3
    tiles = 3

    def at(k):
        def index(i, w):
            j, slot, _ = pick(w, i, tiles)
            return ((slot, j), (0, j), (0, 0), (slot, 0), (jnp.minimum(slot, parts - 1), 0))[k]

        return index

    args = [where, *xs, wq, bq, *tables]
    return pl.pallas_call(
        functools.partial(queries_kernel, len(xs), tiles),
        grid_spec=pltpu.PrefetchScalarGridSpec(
            num_scalar_prefetch=1,
            grid=(len(xs) * tiles,),
            in_specs=[pl.BlockSpec((rows, depth), at(2))] * len(xs)
            + [pl.BlockSpec((depth, width), at(1)), pl.BlockSpec((1, width), at(1))]
            + [pl.BlockSpec((rows, 128), at(4))] * 3
            + [pl.BlockSpec(memory_space=pl.ANY)] * 2,
            out_specs=[pl.BlockSpec((rows, depth), at(3)), pl.BlockSpec((rows, width), at(0))],
        ),
        out_shape=[jax.ShapeDtypeStruct(b.shape, BF16) for b in bufs],
        input_output_aliases={len(args): 0, len(args) + 1: 1},
        cost_estimate=cost(6 * rows * depth * width, 6 * depth * width),
        name="queries_chunk",
    )(*args, *bufs)


def forward_chunk(where, xs, wq, wu, bq, bu, tables, bufs, parts):
    rows, depth = xs[0].shape
    width = wq.shape[1] // 3
    ff = wu.shape[1]
    tiles = 3 + ff // width

    def at(k):
        def index(i, w):
            j, slot, _ = pick(w, i, tiles)
            return (
                (slot, jnp.minimum(j, 2)),
                (slot, jnp.maximum(j - 3, 0)),
                (slot, 0),
                (0, jnp.minimum(j, 2)),
                (0, jnp.maximum(j - 3, 0)),
                (0, 0),
                (jnp.minimum(slot, parts - 1), 0),
            )[k]

        return index

    in_specs = (
        [pl.BlockSpec((rows, depth), at(5))] * len(xs)
        + [
            pl.BlockSpec((depth, width), at(3)),
            pl.BlockSpec((depth, width), at(4)),
            pl.BlockSpec((1, width), at(3)),
            pl.BlockSpec((1, width), at(4)),
        ]
        + [pl.BlockSpec((rows, 128), at(6))] * 3
    )
    total = (parts + 1) * rows
    shapes = [(total, depth), (total, 3 * width), (total, ff), (total, ff)]
    args = [where, *xs, wq, wu, bq, bu, *tables]
    aliases = {}
    if bufs is not None:
        aliases = {len(args) + k: k for k in range(4)}
        args += list(bufs)
        in_specs += [pl.BlockSpec(memory_space=pl.ANY)] * 4
    return pl.pallas_call(
        functools.partial(forward_kernel, len(xs), tiles),
        grid_spec=pltpu.PrefetchScalarGridSpec(
            num_scalar_prefetch=1,
            grid=(len(xs) * tiles,),
            in_specs=in_specs,
            out_specs=[
                pl.BlockSpec((rows, depth), at(2)),
                pl.BlockSpec((rows, width), at(0)),
                pl.BlockSpec((rows, width), at(1)),
                pl.BlockSpec((rows, width), at(1)),
            ],
        ),
        out_shape=[jax.ShapeDtypeStruct(s, BF16) for s in shapes],
        input_output_aliases=aliases,
        cost_estimate=cost(2 * rows * depth * (3 * width + ff), 2 * depth * (3 * width + ff)),
        name="forward_chunk",
    )(*args)


def collect(where_ref, came, shards, x_refs, held_ref, full_ref, in_sems, out_sems, first, last):
    rows = x_refs[0].shape[0]

    def spot(c):
        return pl.ds(pl.multiple_of(where_ref[1 + shards + 2 * c] * rows, rows), rows)

    def loads(c):
        return pltpu.make_async_copy(x_refs[c], held_ref.at[spot(c)], in_sems.at[c])

    def stores(c):
        return pltpu.make_async_copy(held_ref.at[spot(c)], full_ref.at[spot(c)], out_sems.at[c])

    def each(act):
        for c in range(came):
            pl.when(where_ref[2 + shards + 2 * c] > 0)(functools.partial(act, c))

    @pl.when(first)
    def _():
        each(lambda c: loads(c).start())
        each(lambda c: loads(c).wait())
        if full_ref is not None:
            each(lambda c: stores(c).start())

    def finish():
        pl.when(last)(lambda: each(lambda c: stores(c).wait()))

    return finish


def early_over(where_ref, rows):
    step = min(ROWS, rows)

    def over(act):
        def body(t, carry):
            for m in range(0, rows, step):
                at = pl.ds(pl.multiple_of(where_ref[1 + t] * rows + m, step), step)
                act(at, at)
            return carry

        lax.fori_loop(0, where_ref[0], body, 0)

    return over


def queries_early_kernel(came, shards, where_ref, *refs):
    x_refs, refs = refs[:came], refs[came:]
    wq_ref, bq_ref = refs[:2]
    tables = refs[2:5]
    normed_ref, qkv_ref, held_ref, in_sems, out_sems = refs[5:]
    j = pl.program_id(0)
    finish = collect(
        where_ref, came, shards, x_refs, held_ref, normed_ref, in_sems, out_sems,
        j == 0, j == pl.num_programs(0) - 1,
    )
    over = early_over(where_ref, x_refs[0].shape[0])
    project_tile(j, None, held_ref, wq_ref, None, bq_ref, None, tables, qkv_ref, None, None, over)
    finish()


def units_early_kernel(came, shards, where_ref, *refs):
    x_refs, refs = refs[:came], refs[came:]
    wu_ref, bu_ref, act_ref, slope_ref, held_ref, in_sems = refs
    j = pl.program_id(0)
    collect(where_ref, came, shards, x_refs, held_ref, None, in_sems, None, j == 0, None)
    over = early_over(where_ref, x_refs[0].shape[0])
    project_tile(j + 3, None, held_ref, None, wu_ref, None, bu_ref, None, None, act_ref, slope_ref, over)


def queries_early(where, xs, wq, bq, tables, parts):
    rows, depth = xs[0].shape
    width = wq.shape[1] // 3
    count = parts * rows
    in_place = pl.BlockSpec(memory_space=pl.ANY)
    return pl.pallas_call(
        functools.partial(queries_early_kernel, len(xs), parts),
        grid_spec=pltpu.PrefetchScalarGridSpec(
            num_scalar_prefetch=1,
            grid=(3,),
            in_specs=[in_place] * len(xs)
            + [pl.BlockSpec((depth, width), lambda j, w: (0, j)), pl.BlockSpec((1, width), lambda j, w: (0, j))]
            + [whole(t) for t in tables],
            out_specs=[in_place, pl.BlockSpec((count, width), lambda j, w: (0, j))],
            scratch_shapes=[
                pltpu.VMEM((count, depth), BF16),
                pltpu.SemaphoreType.DMA((len(xs),)),
                pltpu.SemaphoreType.DMA((len(xs),)),
            ],
        ),
        out_shape=[
            jax.ShapeDtypeStruct((count + rows, depth), BF16),
            jax.ShapeDtypeStruct((count + rows, 3 * width), BF16),
        ],
        cost_estimate=cost(6 * count * depth * width, 6 * depth * width),
        name="queries_early",
    )(where, *xs, wq, bq, *tables)


def units_early(where, xs, wu, bu, width, parts):
    rows, depth = xs[0].shape
    ff = wu.shape[1]
    count = parts * rows
    return pl.pallas_call(
        functools.partial(units_early_kernel, len(xs), parts),
        grid_spec=pltpu.PrefetchScalarGridSpec(
            num_scalar_prefetch=1,
            grid=(ff // width,),
            in_specs=[pl.BlockSpec(memory_space=pl.ANY)] * len(xs)
            + [pl.BlockSpec((depth, width), lambda j, w: (0, j)), pl.BlockSpec((1, width), lambda j, w: (0, j))],
            out_specs=[pl.BlockSpec((count, width), lambda j, w: (0, j))] * 2,
            scratch_shapes=[pltpu.VMEM((count, depth), BF16), pltpu.SemaphoreType.DMA((len(xs),))],
        ),
        out_shape=[jax.ShapeDtypeStruct((count + rows, ff), BF16)] * 2,
        cost_estimate=cost(2 * count * depth * ff, 2 * depth * ff),
        name="units_early",
    )(where, *xs, wu, bu)


def backward_early_kernel(came, shards, where_ref, *refs):
    c_refs, refs = refs[:came], refs[came:]
    wo_ref, wd_ref, slope_ref, cot_ref, ga_ref, gh_ref, held_ref, in_sems, out_sems = refs
    j = pl.program_id(0)
    finish = collect(
        where_ref, came, shards, c_refs, held_ref, cot_ref, in_sems, out_sems,
        j == 0, j == pl.num_programs(0) - 1,
    )
    rows = c_refs[0].shape[0]
    step = min(ROWS, rows)

    def over(act):
        def body(t, carry):
            for m in range(0, rows, step):
                act(pl.ds(pl.multiple_of(where_ref[1 + t] * rows + m, step), step))
            return carry

        lax.fori_loop(0, where_ref[0], body, 0)

    @pl.when(j == 0)
    def _():
        weight = side_by_side(wo_ref)

        def act(m):
            ga_ref[m, :] = dot_nt(held_ref[m, :], weight).astype(BF16)

        over(act)

    @pl.when(j > 0)
    def _():
        weight = side_by_side(wd_ref)

        def act(m):
            gh_ref[m, :] = (dot_nt(held_ref[m, :], weight) * slope_ref[m, :].astype(F32)).astype(BF16)

        over(act)

    finish()


def backward_early(where, cots, wo, wd, slope, parts):
    rows, depth = cots[0].shape
    pieces, width, piece = wo.shape
    ff = wd.shape[1]
    count = parts * rows
    total = count + rows
    in_place = pl.BlockSpec(memory_space=pl.ANY)

    def tile(j):
        return jnp.maximum(j - 1, 0)

    return pl.pallas_call(
        functools.partial(backward_early_kernel, len(cots), parts),
        grid_spec=pltpu.PrefetchScalarGridSpec(
            num_scalar_prefetch=1,
            grid=(1 + ff // width,),
            in_specs=[in_place] * len(cots)
            + [
                whole(wo),
                pl.BlockSpec((pieces, width, piece), lambda j, w: (0, tile(j), 0)),
                pl.BlockSpec((count, width), lambda j, w: (0, tile(j))),
            ],
            out_specs=[
                in_place,
                pl.BlockSpec((count, width), lambda j, w: (0, 0)),
                pl.BlockSpec((count, width), lambda j, w: (0, tile(j))),
            ],
            scratch_shapes=[
                pltpu.VMEM((count, depth), BF16),
                pltpu.SemaphoreType.DMA((len(cots),)),
                pltpu.SemaphoreType.DMA((len(cots),)),
            ],
        ),
        out_shape=[jax.ShapeDtypeStruct(s, BF16) for s in ((total, depth), (total, width), (total, ff))],
        cost_estimate=cost(2 * count * depth * (width + ff), 2 * depth * (width + ff)),
        name="backward_early",
    )(where, *cots, wo, wd, slope)


def low_lanes(rows):
    return lax.broadcasted_iota(jnp.int32, (rows, 128), 1) < HD


def attend_kernel(
    skipped, first_ref, q_ref, k_ref, v_ref, segc_ref, segr_ref, *refs
):
    o_ref, lse_ref, max_ref, acc_ref, bias_ref = refs[-5:]
    i = pl.program_id(0) + skipped
    block, width = q_ref.shape
    pairs = width // 128
    low = low_lanes(block)
    owns = (low, jnp.logical_not(low))
    max_ref[...] = jnp.full_like(max_ref, NEGATIVE)
    lse_ref[...] = jnp.zeros_like(lse_ref)
    acc_ref[...] = jnp.zeros_like(acc_ref)
    q0 = pl.multiple_of(i * block, block)
    query_seg = segr_ref[:, pl.ds(q0, block)]
    query_row = q0 + lax.broadcasted_iota(jnp.int32, (1, block), 1)

    def set_bias(k0):
        key_seg = segc_ref[pl.ds(k0, block), :]
        key_row = k0 + lax.broadcasted_iota(jnp.int32, (block, 1), 0)
        bias_ref[...] = jnp.where((key_seg == query_seg) & (key_row <= query_row), 0.0, NEGATIVE)

    def scores(k0, p, h):
        lanes = slice(p * 128, (p + 1) * 128)
        q = q_ref[:, lanes]
        mine = jnp.where(owns[h], q, jnp.zeros_like(q))
        return dot_nt(k_ref[pl.ds(k0, block), lanes], mine) + bias_ref[...]

    def find_max(j, carry):
        k0 = pl.multiple_of(j * block, block)
        set_bias(k0)
        for p in range(pairs):
            for h in range(2):
                s = scores(k0, p, h)
                max_ref[2 * p + h] = jnp.maximum(max_ref[2 * p + h], jnp.max(s, axis=0, keepdims=True))
        return carry

    lax.fori_loop(first_ref[i], i + 1, find_max, 0)

    def add_up(j, carry):
        k0 = pl.multiple_of(j * block, block)
        set_bias(k0)
        for p in range(pairs):
            v = v_ref[pl.ds(k0, block), p * 128 : (p + 1) * 128]
            for h in range(2):
                e = jnp.exp(scores(k0, p, h) - max_ref[2 * p + h])
                lse_ref[p, h : h + 1, :] += jnp.sum(e, axis=0, keepdims=True)
                acc_ref[2 * p + h] += dot_tn(e.astype(BF16), jnp.where(owns[h], v, jnp.ones_like(v)))
        return carry

    lax.fori_loop(first_ref[i], i + 1, add_up, 0)
    for p in range(pairs):
        even, odd = acc_ref[2 * p], acc_ref[2 * p + 1]
        o_ref[:, p * 128 : (p + 1) * 128] = jnp.where(
            low, even / pltpu.roll(even, HD, axis=1), odd / pltpu.roll(odd, HD, axis=1)
        ).astype(BF16)
        for h in range(2):
            lse_ref[p, h : h + 1, :] = max_ref[2 * p + h] + jnp.log(lse_ref[p, h : h + 1, :])


def attend(qkv, segc, segr, first, part, parts, bufs):
    count = segr.shape[1]
    width = qkv.shape[1] // 3
    pairs = width // 128
    steps = count // BLOCK // parts
    skipped = part * steps
    in_place = [] if bufs is None else [pl.BlockSpec(memory_space=pl.ANY)] * 2
    return pl.pallas_call(
        functools.partial(attend_kernel, skipped),
        grid_spec=pltpu.PrefetchScalarGridSpec(
            num_scalar_prefetch=1,
            grid=(steps,),
            in_specs=[
                pl.BlockSpec((BLOCK, width), lambda i, f: (i + skipped, 0)),
                pl.BlockSpec((count, width), lambda i, f: (0, 1)),
                pl.BlockSpec((count, width), lambda i, f: (0, 2)),
                whole(segc),
                whole(segr),
            ]
            + in_place,
            out_specs=[
                pl.BlockSpec((BLOCK, width), lambda i, f: (i + skipped, 0)),
                pl.BlockSpec((pairs, 8, BLOCK), lambda i, f: (0, 0, i + skipped)),
            ],
            scratch_shapes=[
                pltpu.VMEM((2 * pairs, 1, BLOCK), F32),
                pltpu.VMEM((2 * pairs, BLOCK, 128), F32),
                pltpu.VMEM((BLOCK, BLOCK), F32),
            ],
        ),
        out_shape=[
            jax.ShapeDtypeStruct((count, width), BF16),
            jax.ShapeDtypeStruct((pairs, 8, count), F32),
        ],
        input_output_aliases={} if bufs is None else {6: 0, 7: 1},
        cost_estimate=cost(30e9 * width / 512, count * width * 8),
        name="attend",
    )(first, qkv, qkv, qkv, segc, segr, *([] if bufs is None else bufs))


def attend_back_kernel(
    first_ref, q_ref, k_ref, v_ref, go_ref, o_ref, lse_ref, segc_ref, segr_ref,
    cos_ref, up_ref, down_ref, *refs,
):
    gq_ref, gk_ref, gv_ref, dq_ref, dk_ref, dv_ref, bias_ref = refs[-7:]
    i = pl.program_id(0)
    steps = pl.num_programs(0)
    block, width = q_ref.shape
    pairs = width // 128
    low = low_lanes(block)
    owns = (low, jnp.logical_not(low))

    @pl.when(i == 0)
    def _():
        dk_ref[...] = jnp.zeros_like(dk_ref)
        dv_ref[...] = jnp.zeros_like(dv_ref)

    dq_ref[...] = jnp.zeros_like(dq_ref)
    q0 = pl.multiple_of(i * block, block)
    query_seg = segr_ref[:, pl.ds(q0, block)]
    query_row = q0 + lax.broadcasted_iota(jnp.int32, (1, block), 1)
    half = jnp.where(
        lax.broadcasted_iota(jnp.int32, (8, 128), 1) // HD == lax.broadcasted_iota(jnp.int32, (8, 128), 0),
        1.0,
        0.0,
    ).astype(F32)
    inner = []
    for p in range(pairs):
        lanes = slice(p * 128, (p + 1) * 128)
        product = go_ref[:, lanes].astype(F32) * o_ref[:, lanes].astype(F32)
        inner.append(
            lax.dot_general(
                half, product, (((1,), (1,)), ((), ())),
                precision=lax.Precision.HIGHEST, preferred_element_type=F32,
            )
        )

    def body(j, carry):
        k0 = pl.multiple_of(j * block, block)
        key_seg = segc_ref[pl.ds(k0, block), :]
        key_row = k0 + lax.broadcasted_iota(jnp.int32, (block, 1), 0)
        bias_ref[...] = jnp.where((key_seg == query_seg) & (key_row <= query_row), 0.0, NEGATIVE)
        for p in range(pairs):
            lanes = slice(p * 128, (p + 1) * 128)
            k = k_ref[pl.ds(k0, block), lanes]
            v = v_ref[pl.ds(k0, block), lanes]
            q = q_ref[:, lanes]
            go = go_ref[:, lanes]
            sums = None
            for h in range(2):
                q_own, go_own, k_own = [jnp.where(owns[h], a, jnp.zeros_like(a)) for a in (q, go, k)]
                prob = jnp.exp(dot_nt(k, q_own) + bias_ref[...] - lse_ref[p, h : h + 1, :])
                grad_score = (prob * (dot_nt(v, go_own) - inner[p][h : h + 1, :])).astype(BF16)
                new = (
                    dot_nn(prob.astype(BF16), go_own),
                    dot_nn(grad_score, q_own),
                    dot_tn(grad_score, k_own),
                )
                sums = new if sums is None else tuple(a + b for a, b in zip(sums, new))
            dv_ref[pl.ds(k0, block), lanes] += sums[0]
            dk_ref[pl.ds(k0, block), lanes] += sums[1]
            dq_ref[:, lanes] += sums[2]
        return carry

    lax.fori_loop(first_ref[i], i + 1, body, 0)
    turn = [r[pl.ds(q0, block), :] for r in (cos_ref, up_ref, down_ref)]
    for p in range(pairs):
        lanes = slice(p * 128, (p + 1) * 128)
        gq_ref[:, lanes] = unrotate(dq_ref[:, lanes] * HD**-0.5, *turn).astype(BF16)

    @pl.when(i == steps - 1)
    def _():
        def finish(j, carry):
            k0 = pl.multiple_of(j * block, block)
            rows = pl.ds(k0, block)
            turn = [r[rows, :] for r in (cos_ref, up_ref, down_ref)]
            for p in range(pairs):
                lanes = slice(p * 128, (p + 1) * 128)
                gk_ref[rows, lanes] = unrotate(dk_ref[rows, lanes], *turn).astype(BF16)
                gv_ref[rows, lanes] = dv_ref[rows, lanes].astype(BF16)
            return carry

        lax.fori_loop(0, steps, finish, 0)


def attend_back(qkv, grad_out, out, lse, segc, segr, first, tables, part, parts, bufs):
    count = segr.shape[1]
    whole_width = qkv.shape[1] // 3
    width = whole_width // parts
    pairs = width // 128
    row_tile = pl.BlockSpec((BLOCK, width), lambda i, f: (i, part))
    column = pl.BlockSpec((count, width), lambda i, f: (0, part))
    in_place = [] if bufs is None else [pl.BlockSpec(memory_space=pl.ANY)] * 3
    args = [first, qkv, qkv, qkv, grad_out, out, lse, segc, segr, *tables]
    return pl.pallas_call(
        attend_back_kernel,
        grid_spec=pltpu.PrefetchScalarGridSpec(
            num_scalar_prefetch=1,
            grid=(count // BLOCK,),
            in_specs=[
                row_tile,
                pl.BlockSpec((count, width), lambda i, f: (0, parts + part)),
                pl.BlockSpec((count, width), lambda i, f: (0, 2 * parts + part)),
                row_tile,
                row_tile,
                pl.BlockSpec((pairs, 8, BLOCK), lambda i, f: (part, 0, i)),
                whole(segc),
                whole(segr),
                *[whole(t) for t in tables],
            ]
            + in_place,
            out_specs=[row_tile, column, column],
            scratch_shapes=[
                pltpu.VMEM((BLOCK, width), F32),
                pltpu.VMEM((count, width), F32),
                pltpu.VMEM((count, width), F32),
                pltpu.VMEM((BLOCK, BLOCK), F32),
            ],
        ),
        out_shape=[jax.ShapeDtypeStruct((count, whole_width), BF16)] * 3,
        input_output_aliases={} if bufs is None else {len(args) + k: k for k in range(3)},
        cost_estimate=cost(44e9 * width / 512, count * width * 20),
        name="attend_back",
    )(*args, *([] if bufs is None else bufs))


def side_by_side(ref):
    return jnp.concatenate([ref[b] for b in range(ref.shape[0])], axis=1)


def mix_kernel(att_ref, act_ref, wo_ref, wd_ref, o_ref):
    wo, wd = side_by_side(wo_ref), side_by_side(wd_ref)
    step = min(512, att_ref.shape[0])
    for m in range(0, att_ref.shape[0], step):
        rs = slice(m, m + step)
        o_ref[rs, :] = (dot_nn(att_ref[rs, :], wo) + dot_nn(act_ref[rs, :], wd)).astype(BF16)


def mix(att, act, wo, wd):
    pieces, width, piece = wo.shape
    ff = wd.shape[1]
    count = att.shape[0]
    group = max(1, 512 // piece)
    return pl.pallas_call(
        mix_kernel,
        grid=(pieces // group,),
        in_specs=[
            pl.BlockSpec((count, width), lambda j: (0, 0)),
            pl.BlockSpec((count, ff), lambda j: (0, 0)),
            pl.BlockSpec((group, width, piece), lambda j: (j, 0, 0)),
            pl.BlockSpec((group, ff, piece), lambda j: (j, 0, 0)),
        ],
        out_specs=pl.BlockSpec((count, group * piece), lambda j: (0, j)),
        out_shape=jax.ShapeDtypeStruct((count, pieces * piece), BF16),
        cost_estimate=cost(2 * count * (width + ff) * pieces * piece, 4 * count * ff),
        name="mix",
    )(att, act, wo, wd)


def mixed_kernel(x_ref, sum_ref, bias_ref, o_ref):
    o_ref[...] = (x_ref[...].astype(F32) + sum_ref[...].astype(F32) + bias_ref[...]).astype(BF16)


def mixed_out(x, total, bias):
    rows, width = x.shape
    step = min(256, rows)
    tile = pl.BlockSpec((step, width), lambda i: (i, 0))
    return pl.pallas_call(
        mixed_kernel,
        grid=(rows // step,),
        in_specs=[tile, tile, pl.BlockSpec((1, width), lambda i: (0, 0))],
        out_specs=tile,
        out_shape=jax.ShapeDtypeStruct(x.shape, BF16),
        cost_estimate=cost(rows * width * 4, rows * width * 6),
        name="mixed_out",
    )(x, total, bias)


def backward_kernel(came, tiles, where_ref, *refs):
    c_refs, refs = refs[:came], refs[came:]
    wo_ref, wd_ref, slope_ref = refs[:3]
    cot_ref, ga_ref, gh_ref = refs[-3:]
    i = pl.program_id(0)
    j, _, busy = pick(where_ref, i, tiles)
    rows = cot_ref.shape[0]
    step = min(ROWS, rows)

    @pl.when(busy & (j == 0))
    def _():
        pick_shard(where_ref, i, tiles, c_refs, cot_ref)
        weight = side_by_side(wo_ref)
        for m in range(0, rows, step):
            ga_ref[m : m + step, :] = dot_nt(cot_ref[m : m + step, :], weight).astype(BF16)

    @pl.when(busy & (j > 0))
    def _():
        weight = side_by_side(wd_ref)
        for m in range(0, rows, step):
            gh_ref[m : m + step, :] = (
                dot_nt(cot_ref[m : m + step, :], weight) * slope_ref[m : m + step, :].astype(F32)
            ).astype(BF16)


def backward_chunk(where, cots, wo, wd, slope, bufs, parts):
    rows, depth = cots[0].shape
    pieces, width, piece = wo.shape
    ff = wd.shape[1]
    tiles = 1 + ff // width

    def at(k):
        def index(i, w):
            j, slot, _ = pick(w, i, tiles)
            return ((0, 0), (0, jnp.maximum(j - 1, 0), 0), (slot, jnp.maximum(j - 1, 0)), (slot, 0))[k]

        return index

    in_specs = [pl.BlockSpec((rows, depth), at(0))] * len(cots) + [
        whole(wo),
        pl.BlockSpec((pieces, width, piece), at(1)),
        pl.BlockSpec((rows, width), at(2)),
    ]
    total = (parts + 1) * rows
    shapes = [(total, depth), (total, width), (total, ff)]
    args = [where, *cots, wo, wd, slope]
    aliases = {}
    if bufs is not None:
        aliases = {len(args) + k: k for k in range(3)}
        args += list(bufs)
        in_specs += [pl.BlockSpec(memory_space=pl.ANY)] * 3
    return pl.pallas_call(
        functools.partial(backward_kernel, len(cots), tiles),
        grid_spec=pltpu.PrefetchScalarGridSpec(
            num_scalar_prefetch=1,
            grid=(len(cots) * tiles,),
            in_specs=in_specs,
            out_specs=[
                pl.BlockSpec((rows, depth), at(3)),
                pl.BlockSpec((rows, width), at(3)),
                pl.BlockSpec((rows, width), at(2)),
            ],
        ),
        out_shape=[jax.ShapeDtypeStruct(s, BF16) for s in shapes],
        input_output_aliases=aliases,
        cost_estimate=cost(2 * rows * depth * (width + ff), 2 * depth * (width + ff)),
        name="backward_chunk",
    )(*args)


def grad_kernel(gq_ref, gk_ref, gv_ref, gh_ref, wq_ref, wu_ref, o_ref):
    step = min(512, gq_ref.shape[0])
    width = gq_ref.shape[1]
    for m in range(0, gq_ref.shape[0], step):
        rs = slice(m, m + step)
        left = jnp.concatenate([r[rs, :] for r in (gq_ref, gk_ref, gv_ref)], axis=1)
        o_ref[rs, :] = (dot_nt(left, wq_ref[...]) + dot_nt(gh_ref[rs, :], wu_ref[...])).astype(BF16)


def grad_normed(gqkv, gh, wq, wu, start, stop):
    count, width = gqkv[0].shape
    ff = gh.shape[1]
    tile = min(256, stop - start)
    first = start // tile
    return pl.pallas_call(
        grad_kernel,
        grid=((stop - start) // tile,),
        in_specs=[once((count, width))] * 3
        + [
            once((count, ff)),
            pl.BlockSpec((tile, wq.shape[1]), lambda j: (first + j, 0)),
            pl.BlockSpec((tile, wu.shape[1]), lambda j: (first + j, 0)),
        ],
        out_specs=pl.BlockSpec((count, tile), lambda j: (0, j)),
        out_shape=jax.ShapeDtypeStruct((count, stop - start), BF16),
        cost_estimate=cost(2 * count * (stop - start) * (3 * width + ff), 4 * count * ff),
        name="grad_normed",
    )(*gqkv, gh, wq, wu)


def put_columns(att_ref, act_ref, cot, o_ref, start, stop, add):
    width = att_ref.shape[1]
    at = start
    while at < stop:
        if at < width:
            end = min(stop, width)
            left = att_ref[:, at:end]
        else:
            end = min(stop, at + 512)
            left = act_ref[:, at - width : end - width]
        rows = slice(at - start, end - start)
        total = dot_tn(left, cot)
        if add is not None:
            total = total + add[0, rows, :].astype(F32)
        o_ref[0, rows, :] = total.astype(BF16)
        at = end


def columns_send_kernel(where_ref, att_ref, act_ref, c_ref, o_ref):
    put_columns(att_ref, act_ref, c_ref[...], o_ref, 0, o_ref.shape[1], None)


def columns_keep_kernel(where_ref, att_ref, act_ref, c_ref, came_ref, a_ref, b_ref):
    half = a_ref.shape[1]
    first = pl.program_id(0) < pl.num_programs(0) // 2

    @pl.when(first)
    def _():
        put_columns(att_ref, act_ref, c_ref[...], a_ref, 0, half, came_ref)

    @pl.when(jnp.logical_not(first))
    def _():
        put_columns(att_ref, act_ref, c_ref[...], b_ref, half, 2 * half, came_ref)


def rows_send_kernel(arrays, where_ref, x_ref, *refs):
    g_refs, o_ref, sum_ref = refs[:arrays], refs[-2], refs[-1]
    x = x_ref[...]
    first = pl.program_id(0) == 0
    start = 0
    for g_ref in g_refs:
        width = g_ref.shape[1]
        step = min(512, width)
        for m in range(0, width, step):
            o_ref[0, :, start + m : start + m + step] = dot_tn(x, g_ref[:, m : m + step]).astype(BF16)

        @pl.when(first)
        def _():
            ones = jnp.ones((8, g_ref.shape[0]), BF16)
            for m in range(0, width, step):
                sum_ref[:, start + m : start + m + step] = dot_nn(ones, g_ref[:, m : m + step])

        start += width


def rows_keep_kernel(arrays, where_ref, x_ref, *refs):
    g_refs, came_ref, a_ref, b_ref = refs[:arrays], *refs[arrays:]
    first = pl.program_id(0) < pl.num_programs(0) // 2
    x = x_ref[...]
    half = a_ref.shape[2]

    def put(o_ref, low):
        start = 0
        for g_ref in g_refs:
            width = g_ref.shape[1]
            at = max(start, low)
            while at < min(start + width, low + half):
                end = min(start + width, low + half, at + 512)
                o_ref[0, :, at - low : end - low] = (
                    dot_tn(x, g_ref[:, at - start : end - start])
                    + came_ref[0, :, at - low : end - low].astype(F32)
                ).astype(BF16)
                at = end
            start += width

    pl.when(first)(lambda: put(a_ref, 0))
    pl.when(jnp.logical_not(first))(lambda: put(b_ref, half))


def once(shape):
    return pl.BlockSpec(shape, lambda *_: (0,) * len(shape), pipeline_mode=pl.Buffered(1))


def column_grads(where, att, act, cot, places, came=None):
    count, width = att.shape
    ff = act.shape[1]
    piece = cot.shape[1] // (2 * places)
    flops = 2 * count * (width + ff) * piece * places
    base = [once((count, width)), once((count, ff)), pl.BlockSpec((count, piece), lambda t, w: (0, w[t]))]
    if came is None:
        return pl.pallas_call(
            columns_send_kernel,
            grid_spec=pltpu.PrefetchScalarGridSpec(
                num_scalar_prefetch=1,
                grid=(places,),
                in_specs=base,
                out_specs=pl.BlockSpec((1, width + ff, piece), lambda t, w: (t, 0, 0)),
            ),
            out_shape=jax.ShapeDtypeStruct((places, width + ff, piece), BF16),
            cost_estimate=cost(flops, 2 * count * (width + ff)),
            name="columns_send",
        )(where, att, act, cot)
    half = (width + ff) // 2
    turns = 2 * places
    return pl.pallas_call(
        columns_keep_kernel,
        grid_spec=pltpu.PrefetchScalarGridSpec(
            num_scalar_prefetch=1,
            grid=(turns,),
            in_specs=base
            + [pl.BlockSpec((1, half, piece), lambda t, w: (w[turns + t], t // places, 0))],
            out_specs=[
                pl.BlockSpec((1, half, piece), lambda t, w: (jnp.minimum(t, places - 1), 0, 0)),
                pl.BlockSpec((1, half, piece), lambda t, w: (jnp.maximum(t - places, 0), 0, 0)),
            ],
        ),
        out_shape=[jax.ShapeDtypeStruct((places, half, piece), BF16)] * 2,
        cost_estimate=cost(flops, 2 * count * (width + ff)),
        name="columns_keep",
    )(where, att, act, cot, came)


def row_grads(where, x, gs, count, places, came=None):
    width = sum(g.shape[1] for g in gs)
    piece = x.shape[1] // (2 * places)
    flops = 2 * count * width * piece * places
    base = [pl.BlockSpec((count, piece), lambda t, w: (0, w[t]))] + [once((count, g.shape[1])) for g in gs]
    if came is None:
        return pl.pallas_call(
            functools.partial(rows_send_kernel, len(gs)),
            grid_spec=pltpu.PrefetchScalarGridSpec(
                num_scalar_prefetch=1,
                grid=(places,),
                in_specs=base,
                out_specs=[
                    pl.BlockSpec((1, piece, width), lambda t, w: (t, 0, 0)),
                    pl.BlockSpec((8, width), lambda t, w: (0, 0)),
                ],
            ),
            out_shape=[
                jax.ShapeDtypeStruct((places, piece, width), BF16),
                jax.ShapeDtypeStruct((8, width), F32),
            ],
            cost_estimate=cost(flops, 2 * count * width),
            name="rows_send",
        )(where, x, *gs)
    half = width // 2
    turns = 2 * places
    return pl.pallas_call(
        functools.partial(rows_keep_kernel, len(gs)),
        grid_spec=pltpu.PrefetchScalarGridSpec(
            num_scalar_prefetch=1,
            grid=(turns,),
            in_specs=base
            + [pl.BlockSpec((1, piece, half), lambda t, w: (w[turns + t], 0, t // places))],
            out_specs=[
                pl.BlockSpec((1, piece, half), lambda t, w: (jnp.minimum(t, places - 1), 0, 0)),
                pl.BlockSpec((1, piece, half), lambda t, w: (jnp.maximum(t - places, 0), 0, 0)),
            ],
        ),
        out_shape=[jax.ShapeDtypeStruct((places, piece, half), BF16)] * 2,
        cost_estimate=cost(flops, 2 * count * width),
        name="rows_keep",
    )(where, x, *gs, came)


def after(value, *marks):
    return lax.optimization_barrier((value, *marks))[0]


def swap(x, bit):
    size = lax.axis_size("dp")
    return lax.ppermute(x, "dp", [(i, i ^ (1 << bit)) for i in range(size)])


def halve(xs, orders, k, sent=None):
    kept = []
    for x, y, bits in zip(xs, sent or xs, orders):
        rest = x.shape[0] // 2
        came = swap(y[rest:], bits[k])
        total = x[:rest].astype(F32) + came.astype(F32)
        kept.append(total if k == len(bits) - 1 else total.astype(BF16))
    return kept


def small_sum_kernel(phases, x_ref, o_ref, sent_ref, came_ref, send_sems, came_sems):
    barrier = pltpu.get_barrier_semaphore()

    def partner(axis, bit):
        return {axis: lax.axis_index(axis) ^ (1 << bit)}

    for axis, bit, _ in phases:
        pl.semaphore_signal(
            barrier, inc=1, device_id=partner(axis, bit), device_id_type=pl.DeviceIdType.MESH
        )
    pl.semaphore_wait(barrier, len(phases))
    sent_ref[0] = x_ref[...]
    for k, (axis, bit, rows) in enumerate(phases):
        span = pl.ds(0, rows)
        copy = pltpu.make_async_remote_copy(
            src_ref=sent_ref.at[k, span],
            dst_ref=came_ref.at[k, span],
            send_sem=send_sems.at[k],
            recv_sem=came_sems.at[k],
            device_id=partner(axis, bit),
            device_id_type=pl.DeviceIdType.MESH,
        )
        copy.start()
        copy.wait()
        total = sent_ref[k, 0:rows] + came_ref[k, 0:rows]
        if k == len(phases) - 1:
            o_ref[...] = sent_ref[k]
            o_ref[0:rows] = total
        else:
            sent_ref[k + 1] = sent_ref[k]
            sent_ref[k + 1, 0:rows] = total


def small_sums(x, common):
    rows = x.shape[0]
    phases = []
    for axis, height in (("dp", rows), ("tensor", common)):
        for bit in range(lax.axis_size(axis).bit_length() - 1):
            phases.append((axis, bit, height))
    return pl.pallas_call(
        functools.partial(small_sum_kernel, phases),
        in_specs=[pl.BlockSpec(memory_space=pltpu.VMEM)],
        out_specs=pl.BlockSpec(memory_space=pltpu.VMEM),
        out_shape=jax.ShapeDtypeStruct(x.shape, F32),
        scratch_shapes=[
            pltpu.VMEM((len(phases), *x.shape), F32),
            pltpu.VMEM((len(phases), *x.shape), F32),
            pltpu.SemaphoreType.DMA((len(phases),)),
            pltpu.SemaphoreType.DMA((len(phases),)),
        ],
        compiler_params=pltpu.CompilerParams(collective_id=0, has_side_effects=True),
        name="small_sums",
    )(x)


def local(
    tokens, segments, ln_gain, ln_shift, qkv_weight, qkv_bias, out_weight, out_bias,
    fc1_weight, fc1_bias, fc2_weight, fc2_bias, cotangent,
):
    n = lax.axis_size("tensor")
    pieces = lax.axis_size("dp")
    me = lax.axis_index("tensor")
    rows, depth = tokens.shape
    count = segments.shape[1]
    width = qkv_weight.shape[2]

    def shift(x, pairs):
        return lax.ppermute(x, "tensor", pairs)

    def turns(step):
        left, right = me - step, me + step
        has_left, has_right = left >= 0, right < n
        one = jnp.where(has_left, left, right)
        last = jnp.where(has_right, right, jnp.where(has_left, left, n))
        busy = has_left.astype(jnp.int32) + has_right.astype(jnp.int32)
        values = [one, jnp.where(has_left, 0, 1), right, 1, busy, last]
        return jnp.stack([jnp.asarray(v, jnp.int32) for v in values])

    def places_of(shards, present):
        shards, present = jnp.stack(shards), jnp.stack(present)
        order = jnp.sort(jnp.where(present, shards, n))
        order = jnp.concatenate([order, jnp.full((n,), n, order.dtype)])[:n]
        return jnp.concatenate(
            [
                jnp.sum(present.astype(jnp.int32))[None],
                order,
                jnp.stack([jnp.clip(shards, 0, n - 1), present.astype(jnp.int32)], axis=1).reshape(-1),
            ]
        ).astype(jnp.int32)

    def present_shards(steps):
        shards = [me] + [me + d * s for s in range(1, steps + 1) for d in (-1, 1)]
        return places_of(shards, [(x >= 0) & (x < n) for x in shards])

    early = present_shards(n - 2)
    late = turns(n - 1)
    middle = [turns(s) for s in range(2, n - 1)]
    cot_shards, cot_there = [me], [me >= 0]
    for s in range(1, n - 1):
        for direction in range(2):
            at_end = me == (n - 1, 0)[direction]
            shard = me + (-s, s)[direction]
            cot_shards += [shard, shard]
            cot_there += [(shard >= 0) & (shard < n) & jnp.logical_not(at_end), at_end]
    if n == 4:
        table = jnp.array([[-1, 0, 3, -1], [-1, 2, 1, -1], [1, -1, -1, 2], [2, -1, -1, 1], [-1, 3, 0, -1]])[:, me]
        cot_shards = [me] + [table[k] for k in range(5)]
        cot_there = [x >= 0 for x in cot_shards]
    cot_early = places_of(cot_shards, cot_there)

    bits = [b for b in range(1, pieces.bit_length() - 1)]
    places = pieces // 2
    mine = lax.axis_index("dp")

    def place_of(r, order):
        return sum(((r >> (len(order) - 1 - k)) & 1) << bit for k, bit in enumerate(order))

    kept = [place_of(r, bits) for r in range(places)] + [place_of(r, bits[::-1]) for r in range(places)]
    send_where = mine ^ jnp.array([2 * q + 1 for q in range(places)], jnp.int32)
    keep_where = jnp.concatenate([mine ^ jnp.array(kept, jnp.int32), jnp.array(kept, jnp.int32) // 2])
    plans = [early, late, *middle, cot_early, send_where, keep_where]

    own_normed = norm(tokens, ln_gain[None], ln_shift[None])

    w_qkv = lax.all_gather(qkv_weight.reshape(-1, 3 * width), "dp", axis=0, tiled=True)
    w_up = lax.all_gather(fc1_weight, "dp", axis=0, tiled=True)
    w_out = lax.all_gather(out_weight, "dp", axis=0)
    w_down = lax.all_gather(fc2_weight, "dp", axis=0)

    segment_row = segments[0]
    starts = seq_starts(segment_row)
    tables = rotary_tables(jnp.arange(count, dtype=jnp.int32) - starts)
    first = starts[::BLOCK] // BLOCK
    segc, segr = segment_row[:, None], segment_row[None, :]

    bias_qkv, bias_up = qkv_bias.reshape(1, -1), fc1_bias[None]
    def line_step(pair, s):
        right, left = pair
        return [
            shift(right, [(i, i + 1) for i in range(s - 1, n - 1)]),
            shift(left, [(i, i - 1) for i in range(1, n - s + 1)]),
        ]

    def line_sum(x):
        return lax.psum_scatter(x, "tensor", scatter_dimension=0, tiled=True)

    def flat(pairs):
        return [x for pair in pairs for x in pair]

    project = (w_qkv, w_up, bias_qkv, bias_up, tables)
    normed_in = [line_step([own_normed] * 2, 1)]
    plans = lax.optimization_barrier(plans)
    early, late, cot_early, send_where, keep_where = plans[0], plans[1], *plans[-3:]
    middle = plans[2:-3]
    normed, qkv = queries_early(
        after(present_shards(1), *plans, first, segc), [own_normed] + normed_in[0], w_qkv, bias_qkv, tables, n
    )
    early_qkv = qkv
    for s in range(2, n):
        normed_in.append(line_step(after(tuple(normed_in[-1]), qkv) if s == 3 else normed_in[-1], s))
    for s in range(2, n - 1):
        normed, qkv = queries_chunk(middle[s - 2], normed_in[s - 1], w_qkv, bias_qkv, tables, (normed, qkv), n)
    act, slope = units_early(
        after(early, qkv), [own_normed] + flat(normed_in[:-1]), w_up, bias_up, width, n
    )
    def inner_step(pair, s):
        right, left = pair
        return [
            shift(right, [(i, i + 1) for i in range(s - 1, n - 2)]),
            shift(left, [(i, i - 1) for i in range(2, n - s + 1)]),
        ]

    def end_step(pair):
        right, left = pair
        return [shift(right, [(n - 2, n - 1)]), shift(left, [(1, 0)])]

    soon = after(cotangent, *normed_in[-2], early_qkv)
    if n == 4:
        cross, out = [(1, 2), (2, 1)], [(2, 3), (1, 0)]
        outside, across = shift(soon, [(0, 1), (3, 2)]), shift(soon, cross)
        outside, across = after((outside, across), *normed_in[-1], act)
        near = shift(after(cotangent, outside), out)
        next_ = shift(across, out)
        over = shift(outside, cross)
        cot_from = [cotangent, outside, across, near, next_, over]
    else:
        inner = [inner_step([soon] * 2, 1)]
        ready = after(tuple(inner[0]), *normed_in[-1], act)
        ends = [end_step([after(cotangent, *ready)] * 2)]
        inner.append(inner_step(ready, 2))
        cot_from = [cotangent]
    normed, qkv, act, slope = forward_chunk(late, normed_in[-1], *project, (normed, qkv, act, slope), n)

    if n == 4:
        att, lse = attend(qkv, segc, segr, first, 0, 1, None)
        last_in = [shift(after(over, att), out)] * 2
    else:
        att_half = attend(qkv, segc, segr, first, 0, 2, None)
        ends.append(end_step(after(tuple(ready), *ends[0], *inner[1], att_half[0])))
        att, lse = attend(qkv, segc, segr, first, 1, 2, att_half)
        for s in range(3, n):
            ready = after(tuple(inner[-1]), att)
            ends.append(end_step(ready))
            if s < n - 1:
                inner.append(inner_step(ready, s))
        for s in range(1, n - 1):
            for direction in range(2):
                cot_from += [inner[s - 1][direction], ends[s - 1][direction]]
        last_in = ends[-1]
    part = mix(att, act, w_out, w_down)
    bufs = backward_early(after(cot_early, part), cot_from, w_out, w_down, slope, n)
    block_sum = line_sum(after(part, bufs[2], *last_in))
    cot, grad_att, grad_hid = backward_chunk(late, last_in, w_out, w_down, slope, bufs, n)
    orders = (bits, bits[::-1])

    def finish(pair, axis, *marks):
        for k in range(1, len(bits)):
            pair = halve([after(half, *marks) for half in pair], orders, k, pair)
        return jnp.concatenate([half[0].astype(F32) for half in pair], axis=axis)

    col_send = column_grads(send_where, att, act, cot, places)
    up_send, up_sum = row_grads(send_where, normed, [after(grad_hid, col_send)], count, places)
    grad_qkv = attend_back(
        qkv, after(grad_att, up_sum), att, lse, segc, segr, first, tables, 0, 1, None
    )
    col_came, up_came = swap(col_send, 0), swap(up_send, 0)
    part = grad_normed(grad_qkv, after(grad_hid, col_came, up_came), w_qkv, w_up, 0, depth)
    grad_sum = line_sum(after(part, block_sum))
    col_pair = column_grads(keep_where, att, act, after(cot, part), places, col_came)
    qkv_send, qkv_sum = row_grads(send_where, normed, after(tuple(grad_qkv), col_pair[0]), count, places)
    up_pair = row_grads(
        keep_where, normed, [after(grad_hid, qkv_sum)], count, places, up_came
    )
    col_pair = halve([after(c, up_pair[0]) for c in col_pair], orders, 0, col_pair)
    qkv_pair = row_grads(
        keep_where, after(normed, *col_pair), grad_qkv, count, places, swap(qkv_send, 0)
    )
    up_pair = halve([after(u, qkv_pair[0]) for u in up_pair], orders, 0, up_pair)
    qkv_kept = qkv_pair[0]
    mixed = mixed_out(tokens, after(block_sum, qkv_kept), (out_bias + fc2_bias)[None])
    qkv_pair = halve([after(half, mixed) for half in qkv_pair], orders, 0, qkv_pair)
    input_grad, sums = norm_back(tokens, after(cotangent, mixed, *qkv_pair), [grad_sum], ln_gain[None])
    common = 3 * depth // 128
    pack = jnp.concatenate([a.reshape(-1, 128) for a in (sums[:3], up_sum[0], qkv_sum[0])])
    pack = jnp.pad(pack, ((0, -pack.shape[0] % 8), (0, 0)))
    pack = small_sums(pack, common)
    col_out, up_out, qkv_out = finish(col_pair, 0, qkv_kept), finish(up_pair, 1, *qkv_pair), finish(qkv_pair, 1)
    total = pack[:common].reshape(3, depth)
    ff_rows = up_sum.shape[1] // 128
    up_bias_grad = pack[common : common + ff_rows].reshape(-1)
    qkv_bias_grad = pack[common + ff_rows : common + ff_rows + 3 * width // 128].reshape(3, width)
    return (
        mixed,
        input_grad,
        qkv_out.reshape(-1, 3, width),
        qkv_bias_grad,
        col_out[:width],
        total[2],
        up_out,
        up_bias_grad,
        col_out[width:],
        total[2],
        total[0],
        total[1],
    )


def solution(mesh):
    in_specs = (
        P(("dp", "tensor"), None),
        P("dp", None),
        P(),
        P(),
        P("dp", None, "tensor"),
        P(None, "tensor"),
        P("tensor", "dp"),
        P(),
        P("dp", "tensor"),
        P("tensor"),
        P("tensor", "dp"),
        P(),
        P(("dp", "tensor"), None),
    )
    out_specs = (
        P(("dp", "tensor"), None),
        P(("dp", "tensor"), None),
        P("dp", None, "tensor"),
        P(None, "tensor"),
        P("tensor", "dp"),
        P(),
        P("dp", "tensor"),
        P("tensor"),
        P("tensor", "dp"),
        P(),
        P(),
        P(),
    )
    return jax.shard_map(local, mesh=mesh, in_specs=in_specs, out_specs=out_specs, check_vma=False)
```
